128 devices in a mesh: ctx: 32 (over y, z, x_lo), head: 4 (over x_hi, core).
Axes of the slice: x: 4 (x_hi: 2, x_lo: 2; x = x_hi * 2 + x_lo), y: 4, z: 4, core: 2. Of those that a mesh axis runs over, the one named last changes fastest.
Arguments:
- hidden: bfloat16 [8192, 2560], P('ctx'), may hold values from -6 to 6
- norm_gain: float32 [2560], replicated, may hold values from 0.1 to 1.9
- x_weight: bfloat16 [2560, 5120], P(None, 'head'), may hold values from -0.125 to 0.125
- z_weight: bfloat16 [2560, 5120], P(None, 'head'), may hold values from -0.125 to 0.125
- bc_weight: bfloat16 [2560, 256], replicated, may hold values from -0.125 to 0.125
- dt_weight: bfloat16 [2560, 80], P(None, 'head'), may hold values from -0.125 to 0.125
- x_kernel: float32 [4, 5120], P(None, 'head'), may hold values from -3 to 3
- bc_kernel: float32 [4, 256], replicated, may hold values from -3 to 3
- dt_bias: float32 [80], P('head'), may hold values from -1 to 1
- log_rate: float32 [80], P('head'), may hold values from -13 to -3
- out_gain: float32 [5120], P('head'), may hold values from 0.1 to 1.9
- out_weight: bfloat16 [5120, 2560], P('head'), may hold values from -0.078125 to 0.078125
Outputs:
- layer_out: bfloat16 [8192, 2560], P('ctx', 'head')
The draws below stay inside these ranges and needn't reach their ends.
All inputs are finite; a program needn't handle non-finite values.
Results may differ from the reference program's by a relative error of at most 0.014.
Values may be sent and summed in bfloat16 or wider, within the bound.
No kernel may reach another device: no remote copies, remote signals or barrier semaphores. Data moves between devices by JAX's collectives and lax.ppermute only.
A program may use at most 128 MiB of HBM per device.

```python
import jax
import jax.numpy as jnp
from jax import lax

D = 2560
HEADS = 80
HEAD_DIM = 64
STATE = 128
CONV = 4
L_DEV = 256
INNER = 5120
TOKENS = 8192


def draw_log_rate(key, part):
    order_key = jax.random.fold_in(key, 11)
    slow_key = jax.random.fold_in(key, 12)
    fast_key = jax.random.fold_in(key, 13)
    slow_count = HEADS // 2
    rank_order = jax.random.permutation(order_key, HEADS)
    slow_heads = rank_order < slow_count
    slow_rate = jnp.log(0.2 / TOKENS) + jnp.log(5.0) * jax.random.uniform(slow_key, (HEADS,), jnp.float32)
    fast_rate = jnp.log(1.0 / 50.0) + jnp.log(50.0 / 30.0) * jax.random.uniform(fast_key, (HEADS,), jnp.float32)
    return jnp.where(slow_heads, slow_rate, fast_rate).astype(jnp.float32)


def steps_of(rng, extent, cuts, smallest, top_value):
    level, own = 1.0, jax.random.fold_in(rng, 6)
    for dim, shards_of in cuts:
        heights = jnp.exp(jax.random.uniform(jax.random.fold_in(own, dim), (shards_of,), jnp.float32, smallest / len(cuts), top_value / len(cuts)))
        level = level * jnp.repeat(heights, extent[dim] // shards_of).reshape([-1 if axis == dim else 1 for axis in range(len(extent))])
    return level


def gaussian(stream_key, extent, spread, reach, cuts=(), held_as=jnp.bfloat16):
    gain = steps_of(stream_key, extent, cuts, -0.22, 0.18) if cuts else 1.0
    values = jax.random.normal(stream_key, extent, jnp.float32) * spread * gain
    return jnp.minimum(jnp.maximum(values, -reach), reach).astype(held_as)


def setup_inputs(seed: int = 0) -> dict:
    streams_of = jax.random.split(jax.random.key(seed), 13)
    hidden = gaussian(streams_of[0], (TOKENS, D), 1.0, 6.0, ((0, 32),))
    norm_gain = jnp.clip(1.0 + 0.18 * jax.random.normal(streams_of[1], (D,), jnp.float32), 0.1, 1.9)
    x_weight = gaussian(streams_of[2], (D, INNER), D ** -0.5, 0.125, ((1, 4),))
    z_weight = gaussian(streams_of[3], (D, INNER), D ** -0.5, 0.125, ((1, 4),))
    bc_weight = gaussian(streams_of[4], (D, 2 * STATE), D ** -0.5, 0.125)
    dt_weight = gaussian(streams_of[5], (D, HEADS), D ** -0.5, 0.125, ((1, 4),))
    x_kernel = gaussian(streams_of[6], (CONV, INNER), 0.5, 3.0, ((1, 4),), jnp.float32)
    bc_kernel = gaussian(streams_of[7], (CONV, 2 * STATE), 0.5, 3.0, (), jnp.float32)
    dt_bias = jnp.clip(jax.random.uniform(streams_of[8], (HEADS,), jnp.float32, -1.0, 1.0) * steps_of(streams_of[8], (HEADS,), ((0, 4),), -0.4, 0.0), -1.0, 1.0)
    log_rate = draw_log_rate(jax.random.fold_in(streams_of[12], 71), 0)
    out_gain = jnp.clip(1.0 + 0.18 * jax.random.normal(streams_of[10], (INNER,), jnp.float32), 0.1, 1.9)
    out_weight = gaussian(streams_of[11], (INNER, D), INNER ** -0.5, 0.078125, ((0, 4),))
    return {"hidden": hidden, "norm_gain": norm_gain, "x_weight": x_weight, "z_weight": z_weight, "bc_weight": bc_weight, "dt_weight": dt_weight, "x_kernel": x_kernel, "bc_kernel": bc_kernel, "dt_bias": dt_bias, "log_rate": log_rate, "out_gain": out_gain, "out_weight": out_weight}


epsilon = 1e-05
highest = lax.Precision.HIGHEST

def rms_scale(values, scaling):
    mean_sq = lax.optimization_barrier(jnp.mean(values * values, axis=-1, keepdims=True))
    return values * lax.rsqrt(mean_sq + epsilon) * scaling

def conv_silu(series, kernel):
    tap_count = kernel.shape[0]
    row_count = series.shape[0]
    padded = jnp.concatenate([jnp.zeros((tap_count - 1, series.shape[1]), series.dtype), series], axis=0)
    running = jnp.zeros(series.shape, jnp.float32)
    for offset in range(tap_count):
        running = running + kernel[offset] * padded[offset:offset + row_count].astype(jnp.float32)
    return jax.nn.silu(running).astype(jnp.bfloat16)

def block_scan(carried, pieces):
    x_blk, b_blk, c_blk, step_blk, decay_blk = pieces
    row_count = x_blk.shape[0]
    cumulative = jnp.cumsum(decay_blk, axis=0)
    cumul_heads = cumulative.T
    step_heads = step_blk.T
    gram_rows = jnp.dot(c_blk, b_blk.T, preferred_element_type=jnp.float32)
    causal = jnp.arange(row_count)[:, None] >= jnp.arange(row_count)[None, :]
    segment = cumul_heads[:, :, None] - cumul_heads[:, None, :]
    weights = jnp.exp(jnp.where(causal[None], segment, -jnp.inf)) * gram_rows[None] * step_heads[:, None, :]
    x_float = x_blk.astype(jnp.float32)
    b_float = b_blk.astype(jnp.float32)
    c_float = c_blk.astype(jnp.float32)
    within = jnp.einsum('hts,shp->thp', weights, x_float, precision=highest)
    from_carry = jnp.einsum('tn,hpn->thp', c_float, carried, precision=highest) * jnp.exp(cumulative)[:, :, None]
    final_log = cumul_heads[:, -1]
    weight_end = jnp.exp(final_log[:, None] - cumul_heads) * step_heads
    local_state = jnp.einsum('hs,shp,sn->hpn', weight_end, x_float, b_float, precision=highest)
    new_carry = jnp.exp(final_log)[:, None, None] * carried + local_state
    y_full = within + from_carry
    return (new_carry, y_full)

def mixer(stream, params):
    norm_gain, x_weight, z_weight, bc_weight, dt_weight, x_kernel, bc_kernel, dt_bias, log_rate, out_gain = params
    row_count = stream.shape[0]
    normed = rms_scale(stream.astype(jnp.float32), norm_gain).astype(jnp.bfloat16)
    x_in = jnp.dot(normed, x_weight, preferred_element_type=jnp.float32).astype(jnp.bfloat16)
    z_in = jnp.dot(normed, z_weight, preferred_element_type=jnp.float32).astype(jnp.bfloat16)
    bc_in = jnp.dot(normed, bc_weight, preferred_element_type=jnp.float32).astype(jnp.bfloat16)
    dt_raw = jnp.dot(normed, dt_weight, preferred_element_type=jnp.float32)
    x_conv = conv_silu(x_in, x_kernel)
    bc_conv = conv_silu(bc_in, bc_kernel)
    step_size = jax.nn.softplus(dt_raw + dt_bias)
    log_decay = -step_size * jnp.exp(log_rate)
    blocks = row_count // L_DEV
    pieces = (x_conv.reshape(blocks, L_DEV, HEADS, HEAD_DIM), bc_conv[:, :STATE].reshape(blocks, L_DEV, STATE), bc_conv[:, STATE:].reshape(blocks, L_DEV, STATE), step_size.reshape(blocks, L_DEV, HEADS), log_decay.reshape(blocks, L_DEV, HEADS))
    initial = jnp.zeros((HEADS, HEAD_DIM, STATE), jnp.float32)
    carried, y_blocks = lax.scan(block_scan, initial, pieces)
    y_full = y_blocks.reshape(row_count, HEADS, HEAD_DIM)
    gating = jax.nn.silu(z_in.astype(jnp.float32)).reshape(row_count, HEADS, HEAD_DIM)
    gated_out = rms_scale(y_full * gating, out_gain.reshape(HEADS, HEAD_DIM))
    return gated_out.astype(jnp.bfloat16).reshape(row_count, HEADS * HEAD_DIM)

def reference(hidden, norm_gain, x_weight, z_weight, bc_weight, dt_weight, x_kernel, bc_kernel, dt_bias, log_rate, out_gain, out_weight):
    params = (norm_gain, x_weight, z_weight, bc_weight, dt_weight, x_kernel, bc_kernel, dt_bias, log_rate, out_gain)
    h_rows = hidden
    h_rc = h_rows[::-1, ::-1]
    forward_out = jnp.dot(mixer(h_rows, params), out_weight, preferred_element_type=jnp.float32)
    backward_out = jnp.dot(mixer(h_rc, params), out_weight, preferred_element_type=jnp.float32)[::-1, ::-1]
    return (h_rows.astype(jnp.float32) + (forward_out + backward_out)).astype(jnp.bfloat16)
```

```python
import functools

import jax
import jax.numpy as jnp
from jax import lax
from jax.experimental import pallas as pl
from jax.experimental.pallas import tpu as pltpu
from jax.sharding import PartitionSpec as P

HEAD_DIM = 64
STATE = 128
HALO = 16
TILE = 256
LANES = 128
epsilon = 1e-05
highest = lax.Precision.HIGHEST
f32 = jnp.float32
bf16 = jnp.bfloat16


def mm(a, b, precision=None):
    return jnp.dot(a, b, preferred_element_type=f32, precision=precision)


def iota(shape, dim):
    return lax.broadcasted_iota(jnp.int32, shape, dim)


def silu(v):
    return v * jax.nn.sigmoid(v)


def flip_matrix(n):
    return (iota((n, n), 0) + iota((n, n), 1) == n - 1).astype(bf16)


def hi_lo(v):
    hi = v.astype(bf16)
    return jnp.concatenate([hi, (v - hi.astype(f32)).astype(bf16)], axis=1)


def spread(first, width):
    rows = iota((2 * LANES, width), 0) % LANES
    return (rows == first + iota((2 * LANES, width), 1) // HEAD_DIM).astype(bf16)


def conv_pair(ext, taps, rows):
    half = rows + HALO
    ahead, behind = ext[:half], ext[half:]
    fwd = jnp.zeros((rows, ext.shape[1]), f32)
    bwd = jnp.zeros((rows, ext.shape[1]), f32)
    for k in range(4):
        fwd = fwd + taps[k : k + 1] * ahead[HALO - 3 + k : HALO - 3 + k + rows]
        bwd = bwd + taps[k : k + 1] * behind[3 - k : 3 - k + rows]
    return silu(fwd).astype(bf16), silu(bwd).astype(bf16)


def entry_kernel(
    h_ref, prev_ref, next_ref, gain_ref, xw_ref, bcw_ref, dtw_ref, xk_ref, bck_ref, dtb_ref, lr_ref,
    x_ref, xconv_ref, bc_ref, delta_ref, cum_ref, cumt_ref, pay_ref,
    ext_ref, st_ref, bt_ref, wend_ref, dec_ref,
):
    rows, width = h_ref.shape
    n = pl.program_id(0)
    steps = pl.num_programs(0)

    @pl.when(n == 0)
    def _():
        ext_ref[0:HALO] = prev_ref[...]
        ext_ref[HALO : HALO + rows] = h_ref[...]
        flip = flip_matrix(TILE)
        blocks = width // TILE
        for b in range(blocks):
            source = slice((blocks - 1 - b) * TILE, (blocks - b) * TILE)
            cols = slice(b * TILE, (b + 1) * TILE)
            ext_ref[HALO + rows : HALO + 2 * rows, cols] = mm(h_ref[:, source], flip).astype(bf16)
            ext_ref[HALO + 2 * rows :, cols] = mm(next_ref[:, source], flip).astype(bf16)

        def normalise(i, _):
            at = pl.ds(pl.multiple_of(i * 32, 32), 32)
            v = ext_ref[at].astype(f32)
            mean_sq = jnp.mean(v * v, axis=-1, keepdims=True)
            ext_ref[at] = (v * lax.rsqrt(mean_sq + epsilon) * gain_ref[...]).astype(bf16)
            return 0

        lax.fori_loop(0, (2 * rows + 2 * HALO) // 32, normalise, 0)
        main = ext_ref[HALO : HALO + 2 * rows]
        x_ref[...] = main
        bc_in = mm(ext_ref[...], bcw_ref[...]).astype(bf16).astype(f32)
        bc_pair = conv_pair(bc_in, bck_ref[...], rows)
        dt = mm(main, dtw_ref[...]) + dtb_ref[...]
        delta = jnp.maximum(dt, 0.0) + jnp.log1p(jnp.exp(-jnp.abs(dt)))
        delta_ref[...] = delta
        log_decay = -delta * jnp.exp(lr_ref[...])
        lower = (iota((rows, rows), 0) >= iota((rows, rows), 1)).astype(f32)
        upper = (iota((rows, rows), 0) <= iota((rows, rows), 1)).astype(f32)
        for d in range(2):
            at = slice(d * rows, (d + 1) * rows)
            bc_ref[at] = bc_pair[d]
            bt_ref[d] = jnp.transpose(bc_pair[d][:, :STATE].astype(f32)).astype(bf16)
            cum = mm(upper if d else lower, log_decay[at], highest)
            cum_ref[at] = cum
            cumt_ref[d] = jnp.transpose(cum)[: cumt_ref.shape[1]]
            last = cum[0:1] if d else cum[rows - 1 : rows]
            wend_ref[at] = hi_lo(jnp.exp(last - cum) * delta[at])
            dec_ref[d : d + 1] = jnp.exp(last)

    x_in = mm(ext_ref[...], xw_ref[...]).astype(bf16).astype(f32)
    pair = conv_pair(x_in, xk_ref[...], rows)
    spread_n = spread(n * (TILE // HEAD_DIM), TILE)
    for d in range(2):
        at = slice(d * rows, (d + 1) * rows)
        xconv_ref[at] = pair[d]
        weighted = (pair[d].astype(f32) * mm(wend_ref[at], spread_n)).astype(bf16)
        column = pl.multiple_of(d * steps * TILE + n * TILE, TILE)
        st_ref[:, pl.ds(column, TILE)] = mm(bt_ref[d], weighted).astype(bf16)

    @pl.when(n == steps - 1)
    def _():
        slots, lanes = pay_ref.shape[0], pay_ref.shape[2] - LANES
        for slot in range(slots):
            i, q = slot // 4, slot % 4
            pay_ref[slot, :, :lanes] = st_ref[16 * i : 16 * i + 16, q * lanes : (q + 1) * lanes]
            dec = jnp.broadcast_to(dec_ref[q // 2 : q // 2 + 1], (16, LANES))
            hi = dec.astype(bf16)
            lo = (dec - hi.astype(f32)).astype(bf16)
            row = iota((16, LANES), 0)
            both = jnp.where(row == 0, hi.astype(f32), jnp.where(row == 1, lo.astype(f32), 0.0))
            pay_ref[slot, :, lanes:] = both.astype(bf16)


def entry(hidden, prev_rows, next_rows, gain, xw, bcw, dtw, xk, bck, dtb, lr, slots):
    rows, width = hidden.shape
    inner = xw.shape[1]
    steps = inner // TILE
    lanes = 2 * inner // 4
    whole = lambda *shape: pl.BlockSpec(shape, lambda n: (0,) * len(shape))
    return pl.pallas_call(
        entry_kernel,
        grid=(steps,),
        in_specs=[
            whole(rows, width), whole(HALO, width), whole(HALO, width), whole(1, width),
            pl.BlockSpec((width, TILE), lambda n: (0, n)),
            whole(width, 2 * STATE), whole(width, LANES),
            pl.BlockSpec((4, TILE), lambda n: (0, n)),
            whole(4, 2 * STATE), whole(1, LANES), whole(1, LANES),
        ],
        out_specs=[
            whole(2 * rows, width),
            pl.BlockSpec((2 * rows, TILE), lambda n: (0, n)),
            whole(2 * rows, 2 * STATE), whole(2 * rows, LANES), whole(2 * rows, LANES),
            whole(2, 24, rows), whole(slots, 16, lanes + LANES),
        ],
        out_shape=[
            jax.ShapeDtypeStruct((2 * rows, width), bf16),
            jax.ShapeDtypeStruct((2 * rows, inner), bf16),
            jax.ShapeDtypeStruct((2 * rows, 2 * STATE), bf16),
            jax.ShapeDtypeStruct((2 * rows, LANES), f32),
            jax.ShapeDtypeStruct((2 * rows, LANES), f32),
            jax.ShapeDtypeStruct((2, 24, rows), f32),
            jax.ShapeDtypeStruct((slots, 16, lanes + LANES), bf16),
        ],
        scratch_shapes=[
            pltpu.VMEM((2 * rows + 2 * HALO, width), bf16),
            pltpu.VMEM((STATE, 2 * inner), bf16),
            pltpu.VMEM((2, STATE, rows), bf16),
            pltpu.VMEM((2 * rows, 2 * LANES), bf16),
            pltpu.VMEM((8, LANES), f32),
        ],
        compiler_params=pltpu.CompilerParams(
            dimension_semantics=("arbitrary",), vmem_limit_bytes=48 << 20
        ),
        cost_estimate=pl.CostEstimate(
            flops=2 * 544 * width * (inner + 384), bytes_accessed=16 << 20, transcendentals=0
        ),
        name="entry",
    )(hidden, prev_rows, next_rows, gain, xw, bcw, dtw, xk, bck, dtb, lr)


def within_kernel(x_ref, bc_ref, cum_ref, cumt_ref, delta_ref, y_ref, gram_ref):
    d, n = pl.program_id(0), pl.program_id(1)
    rows = x_ref.shape[0]
    heads = TILE // HEAD_DIM

    @pl.when(n == 0)
    def _():
        gram = lax.dot_general(
            bc_ref[:, STATE:], bc_ref[:, :STATE], (((1,), (1,)), ((), ())), preferred_element_type=f32
        )
        t, s = iota((rows, rows), 0), iota((rows, rows), 1)
        seen = jnp.where(d == 0, t - s, s - t) >= 0
        gram_ref[...] = jnp.where(seen, gram, 0.0)

    weighted = x_ref[...].astype(f32) * mm(hi_lo(delta_ref[...]), spread(n * heads, TILE))
    cum = pltpu.roll(cum_ref[...], (LANES - n * heads) % LANES, 1)
    owner = iota((rows, TILE), 1) // HEAD_DIM
    total = jnp.zeros((rows, TILE), f32)
    for k in range(heads):
        behind = cumt_ref[0, pl.ds(n * heads + k, 1), :]
        decay = jnp.exp(jnp.minimum(cum[:, k : k + 1] - behind, 0.0)) * gram_ref[...]
        total = total + mm(decay.astype(bf16), jnp.where(owner == k, weighted, 0.0).astype(bf16))
    y_ref[...] = total


def within(xconv, bc, cum, cumt, delta):
    rows = xconv.shape[0] // 2
    inner = xconv.shape[1]
    return pl.pallas_call(
        within_kernel,
        grid=(2, inner // TILE),
        in_specs=[
            pl.BlockSpec((rows, TILE), lambda d, n: (d, n)),
            pl.BlockSpec((rows, 2 * STATE), lambda d, n: (d, 0)),
            pl.BlockSpec((rows, LANES), lambda d, n: (d, 0)),
            pl.BlockSpec((1, 24, rows), lambda d, n: (d, 0, 0)),
            pl.BlockSpec((rows, LANES), lambda d, n: (d, 0)),
        ],
        out_specs=pl.BlockSpec((rows, TILE), lambda d, n: (d, n)),
        out_shape=jax.ShapeDtypeStruct((2 * rows, inner), f32),
        scratch_shapes=[pltpu.VMEM((rows, rows), f32)],
        compiler_params=pltpu.CompilerParams(dimension_semantics=("arbitrary", "arbitrary")),
        cost_estimate=pl.CostEstimate(flops=3 << 30, bytes_accessed=5 << 20, transcendentals=3 << 20),
        name="within",
    )(xconv, bc, cum, cumt, delta)


def scan_kernel(q_ref, pay_ref, out_ref, dec_ref):
    slots, _, lanes = out_ref.shape
    q = q_ref[0]
    half, turned = q % 2, q // 2
    tail = pay_ref[:, :, lanes:]
    place = (iota((LANES, lanes), 0) == half * (lanes // HEAD_DIM) + iota((LANES, lanes), 1) // HEAD_DIM)
    place = place.astype(bf16)
    dec_ref[...] = mm(tail[:, 0, :], place) + mm(tail[:, 1, :], place)

    def one(i, carry):
        at = jnp.where(turned == 1, slots - 1 - i, i)
        out_ref[at] = carry.astype(bf16)
        return carry * dec_ref[pl.ds(at, 1), :] + pay_ref[at, :, :lanes].astype(f32)

    lax.fori_loop(0, slots, one, jnp.zeros((16, lanes), f32))


def scan(q, pay):
    slots, _, lanes = pay.shape
    lanes -= LANES
    return pl.pallas_call(
        scan_kernel,
        in_specs=[pl.BlockSpec(memory_space=pltpu.SMEM), pl.BlockSpec(memory_space=pltpu.VMEM)],
        out_specs=pl.BlockSpec(memory_space=pltpu.VMEM),
        out_shape=jax.ShapeDtypeStruct((slots, 16, lanes), bf16),
        scratch_shapes=[pltpu.VMEM((slots, lanes), f32)],
        name="scan",
    )(q, pay)


def gate_kernel(y_ref, z_ref, bc_ref, cum_ref, st_ref, gain_ref, out_ref):
    q = pl.program_id(0)
    rows, lanes = y_ref.shape
    state = st_ref[...].reshape(STATE, lanes)
    carried = mm(bc_ref[:, STATE:], state)
    spread_q = spread((q % 2) * (lanes // HEAD_DIM), lanes)
    y = y_ref[...] + carried * mm(hi_lo(jnp.exp(cum_ref[...])), spread_q)
    g = y * silu(z_ref[...].astype(f32))
    same = (iota((2 * LANES, LANES), 0) % LANES) // HEAD_DIM == iota((2 * LANES, LANES), 1) // HEAD_DIM
    same = same.astype(bf16)
    for b in range(lanes // LANES):
        at = slice(b * LANES, (b + 1) * LANES)
        part = g[:, at]
        mean_sq = mm(hi_lo(part * part), same) * (1.0 / HEAD_DIM)
        out_ref[:, at] = (part * lax.rsqrt(mean_sq + epsilon) * gain_ref[:, at]).astype(bf16)


def gate(y, z, bc, cum, state, gain):
    rows = y.shape[0] // 2
    inner = y.shape[1]
    lanes = inner // 2
    return pl.pallas_call(
        gate_kernel,
        grid=(4,),
        in_specs=[
            pl.BlockSpec((rows, lanes), lambda q: (q // 2, q % 2)),
            pl.BlockSpec((rows, lanes), lambda q: (q // 2, q % 2)),
            pl.BlockSpec((rows, 2 * STATE), lambda q: (q // 2, 0)),
            pl.BlockSpec((rows, LANES), lambda q: (q // 2, 0)),
            pl.BlockSpec((8, 1, 16, lanes), lambda q: (0, q, 0, 0)),
            pl.BlockSpec((1, lanes), lambda q: (0, q % 2)),
        ],
        out_specs=pl.BlockSpec((rows, lanes), lambda q: (0, q)),
        out_shape=jax.ShapeDtypeStruct((rows, 2 * inner), bf16),
        compiler_params=pltpu.CompilerParams(dimension_semantics=("arbitrary",)),
        name="gate",
    )(y, z, bc, cum, state.reshape(8, 4, 16, lanes), gain)


def project_kernel(has_add, q_ref, gf_ref, gb_ref, wf_ref, wb_ref, *rest):
    adds, (out_ref, accf_ref, accb_ref) = rest[:has_add], rest[has_add:]
    k = pl.program_id(0)

    @pl.when(k == 0)
    def _():
        accf_ref[...] = mm(gf_ref[...], wf_ref[...])
        accb_ref[...] = mm(gb_ref[...], wb_ref[...])

    @pl.when(k > 0)
    def _():
        accf_ref[...] += mm(gf_ref[...], wf_ref[...])
        accb_ref[...] += mm(gb_ref[...], wb_ref[...])

    @pl.when(k == pl.num_programs(0) - 1)
    def _():
        one = flip_matrix(LANES)
        flip = jnp.concatenate([one, one], axis=0)
        blocks = out_ref.shape[1] // LANES
        for b in range(blocks):
            at = slice(b * LANES, (b + 1) * LANES)
            source = slice((blocks - 1 - b) * LANES, (blocks - b) * LANES)
            total = accf_ref[:, at] + mm(hi_lo(accb_ref[:, source]), flip)
            for add in adds:
                total = total + add[:, at].astype(f32)
            out_ref[:, at] = total.astype(out_ref.dtype)


def project(q, gated, weight, dtype, *adds):
    rows = gated.shape[0]
    inner, width = weight.shape
    lanes = width // 4
    steps = inner // TILE
    return pl.pallas_call(
        functools.partial(project_kernel, len(adds)),
        grid_spec=pltpu.PrefetchScalarGridSpec(
            num_scalar_prefetch=1,
            grid=(steps,),
            in_specs=[
                pl.BlockSpec((rows, TILE), lambda k, q: (0, k)),
                pl.BlockSpec((rows, TILE), lambda k, q: (0, steps + k)),
                pl.BlockSpec((TILE, lanes), lambda k, q: (k, q[0])),
                pl.BlockSpec((TILE, lanes), lambda k, q: (k, 3 - q[0])),
            ]
            + [pl.BlockSpec((rows, lanes), lambda k, q: (0, 0)) for _ in adds],
            out_specs=pl.BlockSpec((rows, lanes), lambda k, q: (0, 0)),
            scratch_shapes=[pltpu.VMEM((rows, lanes), f32), pltpu.VMEM((rows, lanes), f32)],
        ),
        out_shape=jax.ShapeDtypeStruct((rows, lanes), dtype),
        compiler_params=pltpu.CompilerParams(dimension_semantics=("arbitrary",)),
        cost_estimate=pl.CostEstimate(
            flops=4 * rows * inner * lanes, bytes_accessed=5 << 20, transcendentals=0
        ),
        name="project",
    )(q, gated, gated, weight, weight, *adds)


def per_device(
    hidden, norm_gain, x_weight, z_weight, bc_weight, dt_weight, x_kernel, bc_kernel,
    dt_bias, log_rate, out_gain, out_weight,
):
    blocks = lax.axis_size("ctx")
    place = lax.axis_index("ctx")
    head = lax.axis_index("head")
    prev_rows = lax.ppermute(hidden[-HALO:], "ctx", [(i, i + 1) for i in range(blocks - 1)])
    next_rows = lax.ppermute(hidden[:HALO], "ctx", [(i + 1, i) for i in range(blocks - 1)])
    pad = LANES - dt_weight.shape[1]
    normed, xconv, bc, delta, cum, cumt, pay = entry(
        hidden, prev_rows, next_rows, norm_gain[None], x_weight, bc_weight,
        jnp.pad(dt_weight, ((0, 0), (0, pad))), x_kernel, bc_kernel,
        jnp.pad(dt_bias, (0, pad))[None], jnp.pad(log_rate, (0, pad))[None], blocks,
    )
    pay = lax.all_to_all(pay, "ctx", 0, 0, tiled=True)
    z_in = jnp.dot(normed, z_weight, preferred_element_type=f32).astype(bf16)
    y = within(xconv, bc, cum, cumt, delta)
    state = scan((place % 4)[None], pay)
    state = lax.all_to_all(state, "ctx", 0, 0, tiled=True)
    gated = gate(y, z_in, bc, cum, state, out_gain[None])
    core, far = head % 2, head // 2
    quarter = lambda f, c: (2 * f + c)[None]
    core_swap = [(0, 1), (1, 0), (2, 3), (3, 2)]
    far_swap = [(0, 2), (2, 0), (1, 3), (3, 1)]
    first = project(quarter(1 - far, 1 - core), gated, out_weight, bf16)
    first = lax.ppermute(first, "head", core_swap)
    second = project(quarter(1 - far, core), gated, out_weight, bf16, first)
    second = lax.ppermute(second, "head", far_swap)
    third = project(quarter(far, 1 - core), gated, out_weight, bf16)
    third = lax.ppermute(third, "head", core_swap)
    lanes = hidden.shape[1] // 4
    residual = lax.dynamic_slice_in_dim(hidden, head * lanes, lanes, 1)
    own = project(quarter(far, core), gated, out_weight, f32, third, residual)
    return (own + second.astype(f32)).astype(bf16)


def solution(mesh):
    return jax.shard_map(
        per_device,
        mesh=mesh,
        in_specs=(
            P("ctx", None), P(), P(None, "head"), P(None, "head"), P(), P(None, "head"),
            P(None, "head"), P(), P("head"), P("head"), P("head"), P("head", None),
        ),
        out_specs=P("ctx", "head"),
        check_vma=False,
    )
```

```python
import functools

import jax
import jax.numpy as jnp
from jax import lax
from jax.experimental import pallas as pl
from jax.experimental.pallas import tpu as pltpu
from jax.sharding import PartitionSpec as P

HEAD_DIM = 64
STATE = 128
HALO = 16
TILE = 256
LANES = 128
epsilon = 1e-05
highest = lax.Precision.HIGHEST
f32 = jnp.float32
bf16 = jnp.bfloat16


def mm(a, b, precision=None):
    return jnp.dot(a, b, preferred_element_type=f32, precision=precision)


def iota(shape, dim):
    return lax.broadcasted_iota(jnp.int32, shape, dim)


def silu(v):
    return v * jax.nn.sigmoid(v)


def flip_matrix(n):
    return (iota((n, n), 0) + iota((n, n), 1) == n - 1).astype(bf16)


def hi_lo(v):
    hi = v.astype(bf16)
    return jnp.concatenate([hi, (v - hi.astype(f32)).astype(bf16)], axis=1)


def spread(first, width):
    rows = iota((2 * LANES, width), 0) % LANES
    return (rows == first + iota((2 * LANES, width), 1) // HEAD_DIM).astype(bf16)


def conv_pair(ext_ref, taps, rows):
    first, second = HALO - 3, HALO + rows
    fwd = bwd = None
    for k in range(4):
        tap = taps[k : k + 1]
        ahead = tap * ext_ref[first + k : first + k + rows]
        behind = tap * ext_ref[second + 3 - k : second + 3 - k + rows]
        fwd = ahead if fwd is None else fwd + ahead
        bwd = behind if bwd is None else bwd + behind
    return silu(fwd).astype(bf16), silu(bwd).astype(bf16)


def cumulate(matrix, v, lanes):
    v = jnp.where(iota(v.shape, 1) < lanes, v, 0.0)
    hi = v.astype(bf16).astype(f32)
    mid = (v - hi).astype(bf16).astype(f32)
    low = v - hi - mid
    packed = hi + pltpu.roll(mid, 32, 1) + pltpu.roll(low, 64, 1)
    out = mm(matrix, packed.astype(bf16))
    return out + pltpu.roll(out, LANES - 32, 1) + pltpu.roll(out, LANES - 64, 1)


def entry_kernel(
    h_ref, prev_ref, next_ref, gain_ref, xw_ref, bcw_ref, dtw_ref, xk_ref, bck_ref, dtb_ref, lr_ref,
    x_ref, xconv_ref, bc_ref, delta_ref, cum_ref, cumt_ref, pay_ref,
    ext_ref, xin_ref, st_ref, bt_ref, wend_ref, dec_ref, rs_ref, dtp_ref,
):
    rows, width = h_ref.shape
    heads = dtb_ref.shape[1]
    n = pl.program_id(0)
    steps = pl.num_programs(0) - 1
    groups = width // LANES

    def scale_of(v):
        return lax.rsqrt(jnp.mean(v * v, axis=-1, keepdims=True) + epsilon)

    def scaled(v, scale, first):
        parts = [
            (v[:, g * LANES : (g + 1) * LANES] * scale) * gain_ref[first + g : first + g + 1]
            for g in range(v.shape[1] // LANES)
        ]
        return jnp.concatenate(parts, axis=1).astype(bf16)

    def prelude():
        def forward(i, _):
            at = pl.ds(pl.multiple_of(i * 32, 32), 32)
            v = h_ref[at].astype(f32)
            scale = scale_of(v)
            rs_ref[at] = jnp.broadcast_to(scale, (32, LANES))
            ext_ref[pl.ds(pl.multiple_of(HALO + i * 32, HALO), 32)] = scaled(v, scale, 0)
            return 0

        lax.fori_loop(0, rows // 32, forward, 0)
        prev = prev_ref[...].astype(f32)
        ext_ref[0:HALO] = scaled(prev, scale_of(prev), 0)
        flip = flip_matrix(TILE)
        blocks = width // TILE
        after = next_ref[...]
        after_scale = scale_of(after.astype(f32))
        stacked = jnp.concatenate([after[:, b * TILE : (b + 1) * TILE] for b in range(blocks)], axis=0)
        stacked = mm(stacked, flip)
        scale = rs_ref[...]
        for b in range(blocks):
            mirror = blocks - 1 - b
            cols = slice(b * TILE, (b + 1) * TILE)
            turned = mm(h_ref[:, mirror * TILE : (mirror + 1) * TILE], flip)
            ext_ref[HALO + rows : HALO + 2 * rows, cols] = scaled(turned, scale, b * 2)
            ext_ref[HALO + 2 * rows :, cols] = scaled(
                stacked[mirror * HALO : (mirror + 1) * HALO], after_scale, b * 2
            )
        main = ext_ref[HALO : HALO + 2 * rows]
        x_ref[...] = main
        xin_ref[...] = mm(ext_ref[...], bcw_ref[...]).astype(bf16).astype(f32)
        dtp_ref[...] = jnp.zeros_like(dtp_ref)
        dtp_ref[0:heads] = dtw_ref[...]
        bias = jnp.concatenate([dtb_ref[...], jnp.zeros((1, LANES - heads), f32)], axis=1)
        rate = jnp.concatenate([lr_ref[...], jnp.zeros((1, LANES - heads), f32)], axis=1)
        dt = lax.dot_general(main, dtp_ref[...], (((1,), (1,)), ((), ())), preferred_element_type=f32)
        dt = dt + bias
        bc_pair = conv_pair(xin_ref, bck_ref[...], rows)
        delta = jnp.maximum(dt, 0.0) + jnp.log1p(jnp.exp(-jnp.abs(dt)))
        delta_ref[...] = delta
        log_decay = -delta * jnp.exp(rate)
        lower = (iota((rows, rows), 0) >= iota((rows, rows), 1)).astype(bf16)
        upper = (iota((rows, rows), 0) <= iota((rows, rows), 1)).astype(bf16)
        for d in range(2):
            at = slice(d * rows, (d + 1) * rows)
            bc_ref[at] = bc_pair[d]
            bt_ref[d] = jnp.transpose(bc_pair[d][:, :STATE].astype(f32)).astype(bf16)
            cum = cumulate(upper if d else lower, log_decay[at], heads)
            cum_ref[at] = cum
            cumt_ref[d] = jnp.transpose(cum)[: cumt_ref.shape[1]]
            last = cum[0:1] if d else cum[rows - 1 : rows]
            wend_ref[at] = hi_lo(jnp.exp(jnp.minimum(last - cum, 0.0)) * delta[at])
            dec_ref[d : d + 1] = jnp.exp(last)

    def product():
        return mm(ext_ref[...], xw_ref[...]).astype(bf16).astype(f32)

    def finish():
        tile = n - 1
        pair = conv_pair(xin_ref, xk_ref[...], rows)
        spread_n = spread(tile * (TILE // HEAD_DIM), TILE)
        for d in range(2):
            at = slice(d * rows, (d + 1) * rows)
            xconv_ref[at] = pair[d]
            weighted = (pair[d].astype(f32) * mm(wend_ref[at], spread_n)).astype(bf16)
            column = pl.multiple_of(d * steps * TILE + tile * TILE, TILE)
            st_ref[:, pl.ds(column, TILE)] = mm(bt_ref[d], weighted).astype(bf16)

    @pl.when(n == 0)
    def _():
        prelude()
        xin_ref[...] = product()

    @pl.when((n > 0) & (n < steps))
    def _():
        finish()
        xin_ref[...] = product()

    @pl.when(n == steps)
    def _():
        finish()
        slots = pay_ref.shape[0]
        row = iota((8, LANES), 0)
        tails = []
        for d in range(2):
            dec = jnp.broadcast_to(dec_ref[d : d + 1], (8, LANES))
            dec = jnp.where(iota((8, LANES), 1) < heads, dec, 0.0)
            hi = dec.astype(bf16).astype(f32)
            tails.append(jnp.where(row == 0, hi, jnp.where(row == 1, dec - hi, 0.0)).astype(bf16))
        for slot in range(slots):
            i, q = slot // 4, slot % 4
            for j in range(5):
                column = (5 * q + j) * LANES
                pay_ref[slot, 16 * j : 16 * j + 16] = st_ref[16 * i : 16 * i + 16, column : column + LANES]
            pay_ref[slot, 80:88] = tails[q // 2]


def entry(hidden, prev_rows, next_rows, gain, xw, bcw, dtw, xk, bck, dtb, lr, slots):
    rows, width = hidden.shape
    inner = xw.shape[1]
    heads = dtb.shape[1]
    steps = inner // TILE
    ahead = lambda n: jnp.minimum(n, steps - 1)
    behind = lambda n: jnp.maximum(n - 1, 0)
    whole = lambda *shape: pl.BlockSpec(shape, lambda n: (0,) * len(shape))
    once = lambda *shape: pl.BlockSpec(
        shape, lambda n: (0,) * len(shape), pipeline_mode=pl.Buffered(1)
    )
    return pl.pallas_call(
        entry_kernel,
        grid=(steps + 1,),
        in_specs=[
            once(rows, width), once(HALO, width), once(HALO, width), once(width // LANES, LANES),
            pl.BlockSpec((width, TILE), lambda n: (0, ahead(n))),
            once(width, 2 * STATE), once(heads, width),
            pl.BlockSpec((4, TILE), lambda n: (0, behind(n))),
            once(4, 2 * STATE), once(1, heads), once(1, heads),
        ],
        out_specs=[
            whole(2 * rows, width),
            pl.BlockSpec((2 * rows, TILE), lambda n: (0, behind(n))),
            whole(2 * rows, 2 * STATE), whole(2 * rows, LANES), whole(2 * rows, LANES),
            whole(2, 24, rows), whole(slots, 88, LANES),
        ],
        out_shape=[
            jax.ShapeDtypeStruct((2 * rows, width), bf16),
            jax.ShapeDtypeStruct((2 * rows, inner), bf16),
            jax.ShapeDtypeStruct((2 * rows, 2 * STATE), bf16),
            jax.ShapeDtypeStruct((2 * rows, LANES), f32),
            jax.ShapeDtypeStruct((2 * rows, LANES), f32),
            jax.ShapeDtypeStruct((2, 24, rows), f32),
            jax.ShapeDtypeStruct((slots, 88, LANES), bf16),
        ],
        scratch_shapes=[
            pltpu.VMEM((2 * rows + 2 * HALO, width), bf16),
            pltpu.VMEM((2 * rows + 2 * HALO, TILE), f32),
            pltpu.VMEM((STATE, 2 * inner), bf16),
            pltpu.VMEM((2, STATE, rows), bf16),
            pltpu.VMEM((2 * rows, 2 * LANES), bf16),
            pltpu.VMEM((8, LANES), f32),
            pltpu.VMEM((rows, LANES), f32),
            pltpu.VMEM((LANES, width), bf16),
        ],
        compiler_params=pltpu.CompilerParams(
            dimension_semantics=("arbitrary",), vmem_limit_bytes=30 << 20
        ),
        cost_estimate=pl.CostEstimate(
            flops=2 * 544 * width * (inner + 384), bytes_accessed=16 << 20, transcendentals=0
        ),
        name="entry",
    )(hidden, prev_rows, next_rows, gain, xw, bcw, dtw, xk, bck, dtb, lr)


def within_kernel(x_ref, bc_ref, cum_ref, cumt_ref, delta_ref, y_ref, gram_ref):
    d, n = pl.program_id(0), pl.program_id(1)
    rows = x_ref.shape[0]
    heads = TILE // HEAD_DIM

    @pl.when(n == 0)
    def _():
        gram = lax.dot_general(
            bc_ref[:, STATE:], bc_ref[:, :STATE], (((1,), (1,)), ((), ())), preferred_element_type=f32
        )
        t, s = iota((rows, rows), 0), iota((rows, rows), 1)
        seen = jnp.where(d == 0, t - s, s - t) >= 0
        gram_ref[...] = jnp.where(seen, gram, 0.0)

    weighted = x_ref[...].astype(f32) * mm(hi_lo(delta_ref[...]), spread(n * heads, TILE))
    cum = pltpu.roll(cum_ref[...], (LANES - n * heads) % LANES, 1)
    owner = iota((rows, TILE), 1) // HEAD_DIM
    total = jnp.zeros((rows, TILE), f32)
    for k in range(heads):
        behind = cumt_ref[0, pl.ds(n * heads + k, 1), :]
        decay = jnp.exp(jnp.minimum(cum[:, k : k + 1] - behind, 0.0)) * gram_ref[...]
        total = total + mm(decay.astype(bf16), jnp.where(owner == k, weighted, 0.0).astype(bf16))
    y_ref[...] = total


def within(xconv, bc, cum, cumt, delta):
    rows = xconv.shape[0] // 2
    inner = xconv.shape[1]
    return pl.pallas_call(
        within_kernel,
        grid=(2, inner // TILE),
        in_specs=[
            pl.BlockSpec((rows, TILE), lambda d, n: (d, n)),
            pl.BlockSpec((rows, 2 * STATE), lambda d, n: (d, 0)),
            pl.BlockSpec((rows, LANES), lambda d, n: (d, 0)),
            pl.BlockSpec((1, 24, rows), lambda d, n: (d, 0, 0)),
            pl.BlockSpec((rows, LANES), lambda d, n: (d, 0)),
        ],
        out_specs=pl.BlockSpec((rows, TILE), lambda d, n: (d, n)),
        out_shape=jax.ShapeDtypeStruct((2 * rows, inner), f32),
        scratch_shapes=[pltpu.VMEM((rows, rows), f32)],
        compiler_params=pltpu.CompilerParams(
            dimension_semantics=("arbitrary", "arbitrary"), vmem_limit_bytes=12 << 20
        ),
        cost_estimate=pl.CostEstimate(flops=3 << 30, bytes_accessed=5 << 20, transcendentals=3 << 20),
        name="within",
    )(xconv, bc, cum, cumt, delta)


def scan_kernel(q_ref, pay_ref, out_ref, carry_ref):
    q = q_ref[0]
    half, turned = q % 2, q // 2
    depth = pay_ref.shape[0]

    @pl.when(pl.program_id(0) == 0)
    def _():
        carry_ref[...] = jnp.zeros_like(carry_ref)

    first = half * (5 * LANES // HEAD_DIM)
    place = iota((LANES, 5 * LANES), 0) == first + iota((LANES, 5 * LANES), 1) // HEAD_DIM
    place = place.astype(bf16)
    carry = [carry_ref[16 * j : 16 * j + 16] for j in range(5)]
    for i in range(depth):
        at = jnp.where(turned == 1, depth - 1 - i, i)
        decays = mm(pay_ref[at, 80:88], place)
        decay = decays[0:1] + decays[1:2]
        for j in range(5):
            rows = slice(16 * j, 16 * j + 16)
            out_ref[at, rows] = carry[j].astype(bf16)
            carry[j] = carry[j] * decay[:, j * LANES : (j + 1) * LANES] + pay_ref[at, rows].astype(f32)
    for j in range(5):
        carry_ref[16 * j : 16 * j + 16] = carry[j]


def scan(q, pay):
    slots = pay.shape[0]
    depth = 8
    steps = slots // depth
    chunk = lambda i, q: (jnp.where(q[0] // 2 == 1, steps - 1 - i, i), 0, 0)
    return pl.pallas_call(
        scan_kernel,
        grid_spec=pltpu.PrefetchScalarGridSpec(
            num_scalar_prefetch=1,
            grid=(steps,),
            in_specs=[pl.BlockSpec((depth, 88, LANES), chunk)],
            out_specs=pl.BlockSpec((depth, 80, LANES), chunk),
            scratch_shapes=[pltpu.VMEM((80, LANES), f32)],
        ),
        out_shape=jax.ShapeDtypeStruct((slots, 80, LANES), bf16),
        compiler_params=pltpu.CompilerParams(
            dimension_semantics=("arbitrary",), vmem_limit_bytes=6 << 20
        ),
        name="scan",
    )(q, pay)


def gate_kernel(y_ref, z_ref, bc_ref, cum_ref, st_ref, gain_ref, out_ref):
    q = pl.program_id(0)
    rows, lanes = y_ref.shape
    groups = lanes // LANES
    state = jnp.concatenate([st_ref[:, 0, j].reshape(STATE, LANES) for j in range(groups)], axis=1)
    carried = mm(bc_ref[:, STATE:], state)
    reach = mm(hi_lo(jnp.exp(cum_ref[...])), spread((q % 2) * (lanes // HEAD_DIM), lanes))
    same = (iota((2 * LANES, LANES), 0) % LANES) // HEAD_DIM == iota((2 * LANES, LANES), 1) // HEAD_DIM
    same = same.astype(bf16)
    for b in range(groups):
        at = slice(b * LANES, (b + 1) * LANES)
        y = y_ref[:, at] + carried[:, at] * reach[:, at]
        part = y * silu(z_ref[:, at].astype(f32))
        mean_sq = mm(hi_lo(part * part), same) * (1.0 / HEAD_DIM)
        gain = gain_ref[pl.ds((q % 2) * groups + b, 1), :]
        out_ref[:, at] = (part * lax.rsqrt(mean_sq + epsilon) * gain).astype(bf16)


def gate(y, z, bc, cum, state, gain):
    rows = y.shape[0] // 2
    inner = y.shape[1]
    lanes = inner // 2
    groups = lanes // LANES
    return pl.pallas_call(
        gate_kernel,
        grid=(4,),
        in_specs=[
            pl.BlockSpec((rows, lanes), lambda q: (q // 2, q % 2)),
            pl.BlockSpec((rows, lanes), lambda q: (q // 2, q % 2)),
            pl.BlockSpec((rows, 2 * STATE), lambda q: (q // 2, 0)),
            pl.BlockSpec((rows, LANES), lambda q: (q // 2, 0)),
            pl.BlockSpec((8, 1, groups, 16, LANES), lambda q: (0, q, 0, 0, 0)),
            pl.BlockSpec((2 * groups, LANES), lambda q: (0, 0)),
        ],
        out_specs=pl.BlockSpec((rows, lanes), lambda q: (0, q)),
        out_shape=jax.ShapeDtypeStruct((rows, 2 * inner), bf16),
        compiler_params=pltpu.CompilerParams(
            dimension_semantics=("arbitrary",), vmem_limit_bytes=14 << 20
        ),
        name="gate",
    )(y, z, bc, cum, state.reshape(8, 4, groups, 16, LANES), gain)


def project_kernel(has_add, q_ref, g_ref, w_ref, *rest):
    adds, (out_ref,) = rest[:has_add], rest[has_add:]
    inner = w_ref.shape[0]
    lanes = out_ref.shape[1]
    q = q_ref[0]
    near = pl.ds(pl.multiple_of(q * lanes, LANES), lanes)
    far = pl.ds(pl.multiple_of((3 - q) * lanes, LANES), lanes)
    ahead = mm(g_ref[:, :inner], w_ref[:, near])
    behind = mm(g_ref[:, inner:], w_ref[:, far])
    one = flip_matrix(LANES)
    flip = jnp.concatenate([one, one], axis=0)
    blocks = lanes // LANES
    for b in range(blocks):
        at = slice(b * LANES, (b + 1) * LANES)
        source = slice((blocks - 1 - b) * LANES, (blocks - b) * LANES)
        total = ahead[:, at] + mm(hi_lo(behind[:, source]), flip)
        for add in adds:
            total = total + add[:, at].astype(f32)
        out_ref[:, at] = total.astype(out_ref.dtype)


def project(q, gated, weight, dtype, *adds):
    rows = gated.shape[0]
    inner, width = weight.shape
    lanes = width // 4
    vmem = pl.BlockSpec(memory_space=pltpu.VMEM)
    return pl.pallas_call(
        functools.partial(project_kernel, len(adds)),
        in_specs=[pl.BlockSpec(memory_space=pltpu.SMEM), vmem, vmem] + [vmem for _ in adds],
        out_specs=vmem,
        out_shape=jax.ShapeDtypeStruct((rows, lanes), dtype),
        compiler_params=pltpu.CompilerParams(vmem_limit_bytes=16 << 20),
        cost_estimate=pl.CostEstimate(
            flops=4 * rows * inner * lanes, bytes_accessed=5 << 20, transcendentals=0
        ),
        name="project",
    )(q, gated, weight, *adds)


def per_device(
    hidden, norm_gain, x_weight, z_weight, bc_weight, dt_weight, x_kernel, bc_kernel,
    dt_bias, log_rate, out_gain, out_weight,
):
    blocks = lax.axis_size("ctx")
    place = lax.axis_index("ctx")
    head = lax.axis_index("head")
    prev_rows = lax.ppermute(hidden[-HALO:], "ctx", [(i, i + 1) for i in range(blocks - 1)])
    next_rows = lax.ppermute(hidden[:HALO], "ctx", [(i + 1, i) for i in range(blocks - 1)])
    normed, xconv, bc, delta, cum, cumt, pay = entry(
        hidden, prev_rows, next_rows, norm_gain.reshape(-1, LANES), x_weight, bc_weight,
        dt_weight.T, x_kernel, bc_kernel, dt_bias[None], log_rate[None], blocks,
    )
    pay = lax.all_to_all(pay, "ctx", 0, 0, tiled=True)
    z_in = jnp.dot(normed, z_weight, preferred_element_type=f32).astype(bf16)
    y = within(xconv, bc, cum, cumt, delta)
    state = scan((place % 4)[None], pay)
    state = lax.all_to_all(state, "ctx", 0, 0, tiled=True)
    gated = gate(y, z_in, bc, cum, state, out_gain.reshape(-1, LANES))
    core, far = head % 2, head // 2
    quarter = lambda f, c: (2 * f + c)[None]
    core_swap = [(0, 1), (1, 0), (2, 3), (3, 2)]
    far_swap = [(0, 2), (2, 0), (1, 3), (3, 1)]
    first = project(quarter(1 - far, 1 - core), gated, out_weight, bf16)
    first = lax.ppermute(first, "head", core_swap)
    second = project(quarter(1 - far, core), gated, out_weight, bf16, first)
    second = lax.ppermute(second, "head", far_swap)
    third = project(quarter(far, 1 - core), gated, out_weight, bf16)
    third = lax.ppermute(third, "head", core_swap)
    lanes = hidden.shape[1] // 4
    residual = lax.dynamic_slice_in_dim(hidden, head * lanes, lanes, 1)
    own = project(quarter(far, core), gated, out_weight, f32, third, residual)
    return (own + second.astype(f32)).astype(bf16)


def solution(mesh):
    return jax.shard_map(
        per_device,
        mesh=mesh,
        in_specs=(
            P("ctx", None), P(), P(None, "head"), P(None, "head"), P(), P(None, "head"),
            P(None, "head"), P(), P("head"), P("head"), P("head"), P("head", None),
        ),
        out_specs=P("ctx", "head"),
        check_vma=False,
    )
```

```python
import functools

import jax
import jax.numpy as jnp
from jax import lax
from jax.experimental import pallas as pl
from jax.experimental.pallas import tpu as pltpu
from jax.sharding import PartitionSpec as P

HEAD_DIM = 64
STATE = 128
HALO = 16
TILE = 256
LANES = 128
epsilon = 1e-05
highest = lax.Precision.HIGHEST
f32 = jnp.float32
bf16 = jnp.bfloat16


def mm(a, b, precision=None):
    return jnp.dot(a, b, preferred_element_type=f32, precision=precision)


def iota(shape, dim):
    return lax.broadcasted_iota(jnp.int32, shape, dim)


def silu(v):
    return v * jax.nn.sigmoid(v)


def flip_matrix(n):
    return (iota((n, n), 0) + iota((n, n), 1) == n - 1).astype(bf16)


def hi_lo(v):
    hi = v.astype(bf16)
    return jnp.concatenate([hi, (v - hi.astype(f32)).astype(bf16)], axis=1)


def spread(first, width):
    rows = iota((2 * LANES, width), 0) % LANES
    return (rows == first + iota((2 * LANES, width), 1) // HEAD_DIM).astype(bf16)


def conv_pair(ext_ref, taps, rows):
    first, second = HALO - 3, HALO + rows
    fwd = bwd = None
    for k in range(4):
        tap = taps[k : k + 1]
        ahead = tap * ext_ref[first + k : first + k + rows]
        behind = tap * ext_ref[second + 3 - k : second + 3 - k + rows]
        fwd = ahead if fwd is None else fwd + ahead
        bwd = behind if bwd is None else bwd + behind
    return silu(fwd).astype(bf16), silu(bwd).astype(bf16)


def cumulate(matrix, v, lanes):
    v = jnp.where(iota(v.shape, 1) < lanes, v, 0.0)
    hi = v.astype(bf16).astype(f32)
    mid = (v - hi).astype(bf16).astype(f32)
    low = v - hi - mid
    packed = hi + pltpu.roll(mid, 32, 1) + pltpu.roll(low, 64, 1)
    out = mm(matrix, packed.astype(bf16))
    return out + pltpu.roll(out, LANES - 32, 1) + pltpu.roll(out, LANES - 64, 1)


def off_chip(x):
    return pltpu.with_memory_space_constraint(x, pltpu.HBM)


def fixed(*shape):
    return pl.BlockSpec(shape, lambda *_: (0,) * len(shape), pipeline_mode=pl.Buffered(1))


def scale_of(v):
    return lax.rsqrt(jnp.mean(v * v, axis=-1, keepdims=True) + epsilon)


def scaled(v, scale, gain_ref, first):
    parts = [
        (v[:, g * LANES : (g + 1) * LANES] * scale) * gain_ref[first + g : first + g + 1]
        for g in range(v.shape[1] // LANES)
    ]
    return jnp.concatenate(parts, axis=1).astype(bf16)


def norm_kernel(
    h_ref, gain_ref, dtw_ref, dtb_ref, lr_ref,
    x_ref, delta_ref, cum_ref, cumt_ref, wend_ref, dec_ref,
    rs_ref, dtp_ref,
):
    rows, width = h_ref.shape
    heads = dtb_ref.shape[1]

    def forward(i, _):
        at = pl.ds(pl.multiple_of(i * 32, 32), 32)
        v = h_ref[at].astype(f32)
        scale = scale_of(v)
        rs_ref[at] = jnp.broadcast_to(scale, (32, LANES))
        x_ref[at] = scaled(v, scale, gain_ref, 0)
        return 0

    lax.fori_loop(0, rows // 32, forward, 0)
    flip = flip_matrix(TILE)
    blocks = width // TILE
    scale = rs_ref[...]
    for b in range(blocks):
        mirror = blocks - 1 - b
        turned = mm(h_ref[:, mirror * TILE : (mirror + 1) * TILE], flip)
        x_ref[rows:, b * TILE : (b + 1) * TILE] = scaled(turned, scale, gain_ref, b * 2)
    dtp_ref[...] = jnp.zeros_like(dtp_ref)
    dtp_ref[0:heads] = dtw_ref[...]
    bias = jnp.concatenate([dtb_ref[...], jnp.zeros((1, LANES - heads), f32)], axis=1)
    rate = jnp.concatenate([lr_ref[...], jnp.zeros((1, LANES - heads), f32)], axis=1)
    dt = lax.dot_general(
        x_ref[...], dtp_ref[...], (((1,), (1,)), ((), ())), preferred_element_type=f32
    )
    dt = dt + bias
    delta = jnp.maximum(dt, 0.0) + jnp.log1p(jnp.exp(-jnp.abs(dt)))
    delta_ref[...] = delta
    log_decay = -delta * jnp.exp(rate)
    lower = (iota((rows, rows), 0) >= iota((rows, rows), 1)).astype(bf16)
    upper = (iota((rows, rows), 0) <= iota((rows, rows), 1)).astype(bf16)
    for d in range(2):
        at = slice(d * rows, (d + 1) * rows)
        cum = cumulate(upper if d else lower, log_decay[at], heads)
        cum_ref[at] = cum
        cumt_ref[d] = jnp.transpose(cum)[: cumt_ref.shape[1]]
        last = cum[0:1] if d else cum[rows - 1 : rows]
        wend_ref[at] = hi_lo(jnp.exp(jnp.minimum(last - cum, 0.0)) * delta[at])
        dec = jnp.where(iota((1, LANES), 1) < heads, jnp.exp(last), 0.0)
        dec_ref[d : d + 1] = dec


def norm(hidden, gain, dtw, dtb, lr):
    rows, width = hidden.shape
    heads = dtb.shape[1]
    return pl.pallas_call(
        norm_kernel,
        grid=(1,),
        in_specs=[
            fixed(rows, width), fixed(width // LANES, LANES), fixed(heads, width),
            fixed(1, heads), fixed(1, heads),
        ],
        out_specs=[
            fixed(2 * rows, width), fixed(2 * rows, LANES), fixed(2 * rows, LANES),
            fixed(2, 24, rows), fixed(2 * rows, 2 * LANES), fixed(8, LANES),
        ],
        out_shape=[
            jax.ShapeDtypeStruct((2 * rows, width), bf16),
            jax.ShapeDtypeStruct((2 * rows, LANES), f32),
            jax.ShapeDtypeStruct((2 * rows, LANES), f32),
            jax.ShapeDtypeStruct((2, 24, rows), f32),
            jax.ShapeDtypeStruct((2 * rows, 2 * LANES), bf16),
            jax.ShapeDtypeStruct((8, LANES), f32),
        ],
        scratch_shapes=[pltpu.VMEM((rows, LANES), f32), pltpu.VMEM((LANES, width), bf16)],
        compiler_params=pltpu.CompilerParams(vmem_limit_bytes=16 << 20),
        cost_estimate=pl.CostEstimate(flops=4 << 30, bytes_accessed=5 << 20, transcendentals=0),
        name="norm",
    )(off_chip(hidden), off_chip(gain), off_chip(dtw), off_chip(dtb), off_chip(lr))


def entry_kernel(
    x_ref, prev_ref, next_ref, gain_ref, xw_ref, bcw_ref, xk_ref, bck_ref, wend_ref, dec_ref,
    xconv_ref, bc_ref, pay_ref,
    ext_ref, xin_ref, bcin_ref, st_ref, bt_ref,
):
    width = x_ref.shape[1]
    rows = x_ref.shape[0] // 2
    n = pl.program_id(0)
    steps = pl.num_programs(0) - 1

    def prelude():
        ext_ref[HALO : HALO + 2 * rows] = x_ref[...]
        prev = prev_ref[...].astype(f32)
        ext_ref[0:HALO] = scaled(prev, scale_of(prev), gain_ref, 0)
        flip = flip_matrix(TILE)
        blocks = width // TILE
        after = next_ref[...]
        after_scale = scale_of(after.astype(f32))
        stacked = jnp.concatenate([after[:, b * TILE : (b + 1) * TILE] for b in range(blocks)], axis=0)
        stacked = mm(stacked, flip)
        for b in range(blocks):
            mirror = blocks - 1 - b
            ext_ref[HALO + 2 * rows :, b * TILE : (b + 1) * TILE] = scaled(
                stacked[mirror * HALO : (mirror + 1) * HALO], after_scale, gain_ref, b * 2
            )
        bcin_ref[...] = mm(ext_ref[...], bcw_ref[...]).astype(bf16).astype(f32)
        bc_pair = conv_pair(bcin_ref, bck_ref[...], rows)
        for d in range(2):
            at = slice(d * rows, (d + 1) * rows)
            bc_ref[at] = bc_pair[d]
            bt_ref[d] = jnp.transpose(bc_pair[d][:, :STATE].astype(f32)).astype(bf16)

    def product():
        return mm(ext_ref[...], xw_ref[...]).astype(bf16).astype(f32)

    def finish():
        tile = n - 1
        pair = conv_pair(xin_ref, xk_ref[...], rows)
        spread_n = spread(tile * (TILE // HEAD_DIM), TILE)
        for d in range(2):
            at = slice(d * rows, (d + 1) * rows)
            xconv_ref[at] = pair[d]
            weighted = (pair[d].astype(f32) * mm(wend_ref[at], spread_n)).astype(bf16)
            column = pl.multiple_of(d * steps * TILE + tile * TILE, TILE)
            st_ref[:, pl.ds(column, TILE)] = mm(bt_ref[d], weighted).astype(bf16)

    @pl.when(n == 0)
    def _():
        prelude()
        xin_ref[...] = product()

    @pl.when((n > 0) & (n < steps))
    def _():
        finish()
        xin_ref[...] = product()

    @pl.when(n == steps)
    def _():
        finish()
        slots = pay_ref.shape[0]
        row = iota((8, LANES), 0)
        tails = []
        for d in range(2):
            dec = jnp.broadcast_to(dec_ref[d : d + 1], (8, LANES))
            hi = dec.astype(bf16).astype(f32)
            tails.append(jnp.where(row == 0, hi, jnp.where(row == 1, dec - hi, 0.0)).astype(bf16))
        for slot in range(slots):
            i, q = slot // 4, slot % 4
            for j in range(5):
                column = (5 * q + j) * LANES
                pay_ref[slot, 16 * j : 16 * j + 16] = st_ref[16 * i : 16 * i + 16, column : column + LANES]
            pay_ref[slot, 80:88] = tails[q // 2]


def entry(x, prev_rows, next_rows, gain, xw, bcw, xk, bck, wend, dec, slots):
    width = x.shape[1]
    rows = x.shape[0] // 2
    inner = xw.shape[1]
    steps = inner // TILE
    ahead = lambda n: jnp.minimum(n, steps - 1)
    behind = lambda n: jnp.maximum(n - 1, 0)
    whole = lambda *shape: pl.BlockSpec(shape, lambda n: (0,) * len(shape))
    once = lambda *shape: pl.BlockSpec(
        shape, lambda n: (0,) * len(shape), pipeline_mode=pl.Buffered(1)
    )
    vmem = pl.BlockSpec(memory_space=pltpu.VMEM)
    return pl.pallas_call(
        entry_kernel,
        grid=(steps + 1,),
        in_specs=[
            vmem, vmem, vmem, once(width // LANES, LANES),
            pl.BlockSpec((width, TILE), lambda n: (0, ahead(n))),
            once(width, 2 * STATE),
            pl.BlockSpec((4, TILE), lambda n: (0, behind(n))),
            once(4, 2 * STATE), vmem, vmem,
        ],
        out_specs=[
            pl.BlockSpec((2 * rows, TILE), lambda n: (0, behind(n))),
            whole(2 * rows, 2 * STATE), whole(slots, 88, LANES),
        ],
        out_shape=[
            pltpu.HBM((2 * rows, inner), bf16),
            pltpu.HBM((2 * rows, 2 * STATE), bf16),
            pltpu.HBM((slots, 88, LANES), bf16),
        ],
        scratch_shapes=[
            pltpu.VMEM((2 * rows + 2 * HALO, width), bf16),
            pltpu.VMEM((2 * rows + 2 * HALO, TILE), f32),
            pltpu.VMEM((2 * rows + 2 * HALO, TILE), f32),
            pltpu.VMEM((STATE, 2 * inner), bf16),
            pltpu.VMEM((2, STATE, rows), bf16),
        ],
        compiler_params=pltpu.CompilerParams(
            dimension_semantics=("arbitrary",), vmem_limit_bytes=26 << 20
        ),
        cost_estimate=pl.CostEstimate(
            flops=2 * 544 * width * (inner + 256), bytes_accessed=12 << 20, transcendentals=0
        ),
        name="entry",
    )(x, prev_rows, next_rows, off_chip(gain), off_chip(xw), off_chip(bcw), off_chip(xk), off_chip(bck), wend, dec)


def open_gate_kernel(x_ref, zw_ref, z_ref):
    z = mm(x_ref[...], zw_ref[...]).astype(bf16).astype(f32)
    z_ref[...] = silu(z).astype(bf16)


def open_gate(x, zw):
    height, width = x.shape
    inner = zw.shape[1]
    return pl.pallas_call(
        open_gate_kernel,
        grid=(inner // TILE,),
        in_specs=[fixed(height, width), pl.BlockSpec((width, TILE), lambda n: (0, n))],
        out_specs=pl.BlockSpec((height, TILE), lambda n: (0, n)),
        out_shape=jax.ShapeDtypeStruct((height, inner), bf16),
        compiler_params=pltpu.CompilerParams(
            dimension_semantics=("arbitrary",), vmem_limit_bytes=16 << 20
        ),
        cost_estimate=pl.CostEstimate(
            flops=2 * height * width * inner, bytes_accessed=16 << 20, transcendentals=0
        ),
        name="open_gate",
    )(off_chip(x), off_chip(zw))


def within_kernel(x_ref, bc_ref, cum_ref, cumt_ref, delta_ref, y_ref, gram_ref):
    d, n = pl.program_id(0), pl.program_id(1)
    rows = x_ref.shape[0]
    heads = TILE // HEAD_DIM

    @pl.when(n == 0)
    def _():
        gram = lax.dot_general(
            bc_ref[:, STATE:], bc_ref[:, :STATE], (((1,), (1,)), ((), ())), preferred_element_type=f32
        )
        t, s = iota((rows, rows), 0), iota((rows, rows), 1)
        seen = jnp.where(d == 0, t - s, s - t) >= 0
        gram_ref[...] = jnp.where(seen, gram, 0.0)

    weighted = x_ref[...].astype(f32) * mm(hi_lo(delta_ref[...]), spread(n * heads, TILE))
    cum = pltpu.roll(cum_ref[...], (LANES - n * heads) % LANES, 1)
    owner = iota((rows, TILE), 1) // HEAD_DIM
    total = jnp.zeros((rows, TILE), f32)
    for k in range(heads):
        behind = cumt_ref[0, pl.ds(n * heads + k, 1), :]
        decay = jnp.exp(jnp.minimum(cum[:, k : k + 1] - behind, 0.0)) * gram_ref[...]
        total = total + mm(decay.astype(bf16), jnp.where(owner == k, weighted, 0.0).astype(bf16))
    y_ref[...] = total


def within(xconv, bc, cum, cumt, delta):
    rows = xconv.shape[0] // 2
    inner = xconv.shape[1]
    return pl.pallas_call(
        within_kernel,
        grid=(2, inner // TILE),
        in_specs=[
            pl.BlockSpec((rows, TILE), lambda d, n: (d, n)),
            pl.BlockSpec((rows, 2 * STATE), lambda d, n: (d, 0)),
            pl.BlockSpec((rows, LANES), lambda d, n: (d, 0)),
            pl.BlockSpec((1, 24, rows), lambda d, n: (d, 0, 0)),
            pl.BlockSpec((rows, LANES), lambda d, n: (d, 0)),
        ],
        out_specs=pl.BlockSpec((rows, TILE), lambda d, n: (d, n)),
        out_shape=pltpu.HBM((2 * rows, inner), f32),
        scratch_shapes=[pltpu.VMEM((rows, rows), f32)],
        compiler_params=pltpu.CompilerParams(
            dimension_semantics=("arbitrary", "arbitrary"), vmem_limit_bytes=12 << 20
        ),
        cost_estimate=pl.CostEstimate(flops=3 << 30, bytes_accessed=5 << 20, transcendentals=3 << 20),
        name="within",
    )(off_chip(xconv), off_chip(bc), cum, cumt, delta)


def scan_kernel(q_ref, pay_ref, out_ref, carry_ref):
    q = q_ref[0]
    half, turned = q % 2, q // 2
    depth = pay_ref.shape[0]

    @pl.when(pl.program_id(0) == 0)
    def _():
        carry_ref[...] = jnp.zeros_like(carry_ref)

    first = half * (5 * LANES // HEAD_DIM)
    place = iota((LANES, 5 * LANES), 0) == first + iota((LANES, 5 * LANES), 1) // HEAD_DIM
    place = place.astype(bf16)
    carry = [carry_ref[16 * j : 16 * j + 16] for j in range(5)]
    for i in range(depth):
        at = jnp.where(turned == 1, depth - 1 - i, i)
        decays = mm(pay_ref[at, 80:88], place)
        decay = decays[0:1] + decays[1:2]
        for j in range(5):
            rows = slice(16 * j, 16 * j + 16)
            out_ref[at, rows] = carry[j].astype(bf16)
            carry[j] = carry[j] * decay[:, j * LANES : (j + 1) * LANES] + pay_ref[at, rows].astype(f32)
    for j in range(5):
        carry_ref[16 * j : 16 * j + 16] = carry[j]


def scan(q, pay):
    slots = pay.shape[0]
    depth = 8
    steps = slots // depth
    chunk = lambda i, q: (jnp.where(q[0] // 2 == 1, steps - 1 - i, i), 0, 0)
    return pl.pallas_call(
        scan_kernel,
        grid_spec=pltpu.PrefetchScalarGridSpec(
            num_scalar_prefetch=1,
            grid=(steps,),
            in_specs=[pl.BlockSpec((depth, 88, LANES), chunk)],
            out_specs=pl.BlockSpec((depth, 80, LANES), chunk),
            scratch_shapes=[pltpu.VMEM((80, LANES), f32)],
        ),
        out_shape=jax.ShapeDtypeStruct((slots, 80, LANES), bf16),
        compiler_params=pltpu.CompilerParams(
            dimension_semantics=("arbitrary",), vmem_limit_bytes=6 << 20
        ),
        name="scan",
    )(q, pay)


def weight_fetches(q, w_ref, near_ref, far_ref, sems):
    chunks, depth, lanes = near_ref.shape
    near = pl.ds(pl.multiple_of(q * lanes, LANES), lanes)
    far = pl.ds(pl.multiple_of((3 - q) * lanes, LANES), lanes)
    copies = []
    for k in range(chunks):
        rows = slice(k * depth, (k + 1) * depth)
        copies.append(
            (
                pltpu.make_async_copy(w_ref.at[rows, near], near_ref.at[k], sems.at[0, k]),
                pltpu.make_async_copy(w_ref.at[rows, far], far_ref.at[k], sems.at[1, k]),
            )
        )
    return copies


def project_into(out_ref, g_ref, copies, near_ref, far_ref, adds):
    chunks, depth, lanes = near_ref.shape
    ahead = behind = None
    for k in range(chunks):
        for copy in copies[k]:
            copy.wait()
        one = mm(g_ref[:, k * depth : (k + 1) * depth], near_ref[k])
        two = mm(g_ref[:, (chunks + k) * depth : (chunks + k + 1) * depth], far_ref[k])
        ahead = one if ahead is None else ahead + one
        behind = two if behind is None else behind + two
    flip = flip_matrix(LANES)
    flip = jnp.concatenate([flip, flip], axis=0)
    blocks = lanes // LANES
    for b in range(blocks):
        at = slice(b * LANES, (b + 1) * LANES)
        source = slice((blocks - 1 - b) * LANES, (blocks - b) * LANES)
        total = ahead[:, at] + mm(hi_lo(behind[:, source]), flip)
        for add in adds:
            total = total + add[:, at].astype(f32)
        out_ref[:, at] = total.astype(out_ref.dtype)


def weight_scratch(inner, lanes):
    chunks = inner // TILE
    return [
        pltpu.VMEM((chunks, TILE, lanes), bf16),
        pltpu.VMEM((chunks, TILE, lanes), bf16),
        pltpu.SemaphoreType.DMA((2, chunks)),
    ]


def gate_kernel(
    target_ref, y_ref, z_ref, bc_ref, cum_ref, st_ref, gain_ref, w_ref,
    g_ref, out_ref,
    near_ref, far_ref, sems,
):
    q = pl.program_id(0)
    rows, lanes = y_ref.shape
    groups = lanes // LANES
    copies = weight_fetches(target_ref[0], w_ref, near_ref, far_ref, sems)

    @pl.when(q == 0)
    def _():
        for pair in copies:
            for copy in pair:
                copy.start()

    state = jnp.concatenate([st_ref[:, 0, j].reshape(STATE, LANES) for j in range(groups)], axis=1)
    carried = mm(bc_ref[:, STATE:], state)
    reach = mm(hi_lo(jnp.exp(cum_ref[...])), spread((q % 2) * (lanes // HEAD_DIM), lanes))
    same = (iota((2 * LANES, LANES), 0) % LANES) // HEAD_DIM == iota((2 * LANES, LANES), 1) // HEAD_DIM
    same = same.astype(bf16)
    for b in range(groups):
        at = slice(b * LANES, (b + 1) * LANES)
        y = y_ref[:, at] + carried[:, at] * reach[:, at]
        part = y * z_ref[:, at].astype(f32)
        mean_sq = mm(hi_lo(part * part), same) * (1.0 / HEAD_DIM)
        gain = gain_ref[pl.ds((q % 2) * groups + b, 1), :]
        column = pl.multiple_of((q * groups + b) * LANES, LANES)
        g_ref[:, pl.ds(column, LANES)] = (part * lax.rsqrt(mean_sq + epsilon) * gain).astype(bf16)

    @pl.when(q == pl.num_programs(0) - 1)
    def _():
        project_into(out_ref, g_ref, copies, near_ref, far_ref, ())


def gate(target, y, z, bc, cum, state, gain, weight):
    rows = y.shape[0] // 2
    inner = y.shape[1]
    lanes = inner // 2
    groups = lanes // LANES
    columns = weight.shape[1] // 4
    return pl.pallas_call(
        gate_kernel,
        grid_spec=pltpu.PrefetchScalarGridSpec(
            num_scalar_prefetch=1,
            grid=(4,),
            in_specs=[
                pl.BlockSpec((rows, lanes), lambda q, t: (q // 2, q % 2)),
                pl.BlockSpec((rows, lanes), lambda q, t: (q // 2, q % 2)),
                pl.BlockSpec((rows, 2 * STATE), lambda q, t: (q // 2, 0)),
                pl.BlockSpec((rows, LANES), lambda q, t: (q // 2, 0)),
                pl.BlockSpec((8, 1, groups, 16, LANES), lambda q, t: (0, q, 0, 0, 0)),
                fixed(2 * groups, LANES),
                pl.BlockSpec(memory_space=pltpu.HBM),
            ],
            out_specs=[fixed(rows, 2 * inner), fixed(rows, columns)],
            scratch_shapes=weight_scratch(inner, columns),
        ),
        out_shape=[
            jax.ShapeDtypeStruct((rows, 2 * inner), bf16),
            jax.ShapeDtypeStruct((rows, columns), bf16),
        ],
        compiler_params=pltpu.CompilerParams(
            dimension_semantics=("arbitrary",), vmem_limit_bytes=20 << 20
        ),
        name="gate",
    )(target, off_chip(y), z, off_chip(bc), cum, state.reshape(8, 4, groups, 16, LANES), off_chip(gain), off_chip(weight))


def project_kernel(has_add, q_ref, g_ref, w_ref, *rest):
    adds, (out_ref, near_ref, far_ref, sems) = rest[:has_add], rest[has_add:]
    copies = weight_fetches(q_ref[0], w_ref, near_ref, far_ref, sems)
    for pair in copies:
        for copy in pair:
            copy.start()
    project_into(out_ref, g_ref, copies, near_ref, far_ref, adds)


def project(q, gated, weight, dtype, *adds):
    rows = gated.shape[0]
    inner, width = weight.shape
    lanes = width // 4
    vmem = pl.BlockSpec(memory_space=pltpu.VMEM)
    return pl.pallas_call(
        functools.partial(project_kernel, len(adds)),
        in_specs=[pl.BlockSpec(memory_space=pltpu.SMEM), vmem, pl.BlockSpec(memory_space=pltpu.HBM)]
        + [vmem for _ in adds],
        out_specs=vmem,
        out_shape=jax.ShapeDtypeStruct((rows, lanes), dtype),
        scratch_shapes=weight_scratch(inner, lanes),
        compiler_params=pltpu.CompilerParams(vmem_limit_bytes=16 << 20),
        cost_estimate=pl.CostEstimate(
            flops=4 * rows * inner * lanes, bytes_accessed=5 << 20, transcendentals=0
        ),
        name="project",
    )(q, gated, off_chip(weight), *adds)


def per_device(
    hidden, norm_gain, x_weight, z_weight, bc_weight, dt_weight, x_kernel, bc_kernel,
    dt_bias, log_rate, out_gain, out_weight,
):
    blocks = lax.axis_size("ctx")
    place = lax.axis_index("ctx")
    head = lax.axis_index("head")
    prev_rows = lax.ppermute(hidden[-HALO:], "ctx", [(i, i + 1) for i in range(blocks - 1)])
    next_rows = lax.ppermute(hidden[:HALO], "ctx", [(i + 1, i) for i in range(blocks - 1)])
    gain = norm_gain.reshape(-1, LANES)
    normed, delta, cum, cumt, wend, dec = norm(hidden, gain, dt_weight.T, dt_bias[None], log_rate[None])
    xconv, bc, pay = entry(
        normed, prev_rows, next_rows, gain, x_weight, bc_weight, x_kernel, bc_kernel, wend, dec, blocks
    )
    pay = lax.all_to_all(pay, "ctx", 0, 0, tiled=True)
    y = within(xconv, bc, cum, cumt, delta)
    pay, y = lax.optimization_barrier((pay, y))
    state = scan((place % 4)[None], pay)
    state = lax.all_to_all(state, "ctx", 0, 0, tiled=True)
    open_z = open_gate(normed, z_weight)
    core, far = head % 2, head // 2
    quarter = lambda f, c: (2 * f + c)[None]
    core_swap = [(0, 1), (1, 0), (2, 3), (3, 2)]
    far_swap = [(0, 2), (2, 0), (1, 3), (3, 1)]
    gated, first = gate(
        quarter(1 - far, 1 - core), y, open_z, bc, cum, state, out_gain.reshape(-1, LANES), out_weight
    )
    first = lax.ppermute(first, "head", core_swap)
    second = project(quarter(1 - far, core), gated, out_weight, bf16, first)
    second, gated = lax.optimization_barrier((second, gated))
    second = lax.ppermute(second, "head", far_swap)
    third = project(quarter(far, 1 - core), gated, out_weight, bf16)
    third = lax.ppermute(third, "head", core_swap)
    lanes = hidden.shape[1] // 4
    residual = lax.dynamic_slice_in_dim(hidden, head * lanes, lanes, 1)
    own = project(quarter(far, core), gated, out_weight, f32, third, residual)
    return (own + second.astype(f32)).astype(bf16)


def solution(mesh):
    return jax.shard_map(
        per_device,
        mesh=mesh,
        in_specs=(
            P("ctx", None), P(), P(None, "head"), P(None, "head"), P(), P(None, "head"),
            P(None, "head"), P(), P("head"), P("head"), P("head"), P("head", None),
        ),
        out_specs=P("ctx", "head"),
        check_vma=False,
    )
```

```python
import functools

import jax
import jax.numpy as jnp
from jax import lax
from jax.experimental import pallas as pl
from jax.experimental.pallas import tpu as pltpu
from jax.sharding import PartitionSpec as P

HEAD_DIM = 64
STATE = 128
HALO = 16
EXTRA = 32
CHUNK = 64
TILE = 256
LANES = 128
epsilon = 1e-05
f32 = jnp.float32
bf16 = jnp.bfloat16


def mm(a, b, precision=None):
    return jnp.dot(a, b, preferred_element_type=f32, precision=precision)


def iota(shape, dim):
    return lax.broadcasted_iota(jnp.int32, shape, dim)


def silu(v):
    return v * jax.nn.sigmoid(v)


def flip_matrix(n):
    return (iota((n, n), 0) + iota((n, n), 1) == n - 1).astype(bf16)


def hi_lo(v):
    hi = v.astype(bf16)
    return jnp.concatenate([hi, (v - hi.astype(f32)).astype(bf16)], axis=1)


def spread(first, width):
    rows = iota((2 * LANES, width), 0) % LANES
    return (rows == first + iota((2 * LANES, width), 1) // HEAD_DIM).astype(bf16)


def time_of(index, rows):
    return (index % 8) * (rows // 8) + index // 8


def conv_rows(ext_ref, taps, direction, rows, first, count):
    base = (EXTRA - 24 if direction == 0 else EXTRA + rows) + first
    total = None
    for k in range(4):
        at = base + 8 * (k if direction == 0 else 3 - k)
        term = taps[k : k + 1] * ext_ref[at : at + count]
        total = term if total is None else total + term
    return silu(total).astype(bf16)


def cumulate(matrix, v, lanes):
    v = jnp.where(iota(v.shape, 1) < lanes, v, 0.0)
    hi = v.astype(bf16).astype(f32)
    mid = (v - hi).astype(bf16).astype(f32)
    low = v - hi - mid
    packed = hi + pltpu.roll(mid, 32, 1) + pltpu.roll(low, 64, 1)
    out = mm(matrix, packed.astype(bf16))
    return out + pltpu.roll(out, LANES - 32, 1) + pltpu.roll(out, LANES - 64, 1)


def off_chip(x):
    return pltpu.with_memory_space_constraint(x, pltpu.HBM)


def fixed(*shape):
    return pl.BlockSpec(shape, lambda *_: (0,) * len(shape), pipeline_mode=pl.Buffered(1))


def scale_of(v):
    return lax.rsqrt(jnp.mean(v * v, axis=-1, keepdims=True) + epsilon)


def scaled(v, scale, gain_ref, first):
    parts = [
        (v[:, g * LANES : (g + 1) * LANES] * scale) * gain_ref[first + g : first + g + 1]
        for g in range(v.shape[1] // LANES)
    ]
    return jnp.concatenate(parts, axis=1).astype(bf16)


def norm_kernel(
    h_ref, gain_ref, dtw_ref, dtb_ref, lr_ref,
    x_ref, delta_ref, cum_ref, cumt_ref, wend_ref, dec_ref,
    raw_ref, dtp_ref,
):
    rows, width = h_ref.shape
    heads = dtb_ref.shape[1]

    order = (iota((rows, rows), 1) == time_of(iota((rows, rows), 0), rows)).astype(bf16)
    flip = flip_matrix(TILE)
    blocks = width // TILE
    squares = jnp.zeros((rows, LANES), f32)
    for b in range(blocks):
        cols = slice(b * TILE, (b + 1) * TILE)
        v = mm(order, h_ref[:, cols])
        raw_ref[:, cols] = v.astype(bf16)
        squares = squares + v[:, :LANES] * v[:, :LANES] + v[:, LANES:] * v[:, LANES:]
    mean_sq = jnp.sum(squares, axis=-1, keepdims=True) * (1.0 / width)
    scale = jnp.broadcast_to(lax.rsqrt(mean_sq + epsilon), (rows, LANES))
    for b in range(blocks):
        cols = slice(b * TILE, (b + 1) * TILE)
        mirror = blocks - 1 - b
        x_ref[:rows, cols] = scaled(raw_ref[:, cols].astype(f32), scale, gain_ref, b * 2)
        turned = mm(raw_ref[:, mirror * TILE : (mirror + 1) * TILE], flip)
        x_ref[rows:, cols] = scaled(turned, scale, gain_ref, b * 2)
    dtp_ref[...] = jnp.zeros_like(dtp_ref)
    dtp_ref[0:heads] = dtw_ref[...]
    bias = jnp.concatenate([dtb_ref[...], jnp.zeros((1, LANES - heads), f32)], axis=1)
    rate = jnp.concatenate([lr_ref[...], jnp.zeros((1, LANES - heads), f32)], axis=1)
    dt = lax.dot_general(
        x_ref[...], dtp_ref[...], (((1,), (1,)), ((), ())), preferred_element_type=f32
    )
    dt = dt + bias
    delta = jnp.maximum(dt, 0.0) + jnp.log1p(jnp.exp(-jnp.abs(dt)))
    delta_ref[...] = delta
    log_decay = -delta * jnp.exp(rate)
    later, sooner = time_of(iota((rows, rows), 0), rows), time_of(iota((rows, rows), 1), rows)
    lower = (later >= sooner).astype(bf16)
    upper = (later <= sooner).astype(bf16)
    for d in range(2):
        at = slice(d * rows, (d + 1) * rows)
        cum = cumulate(upper if d else lower, log_decay[at], heads)
        cum_ref[at] = cum
        cumt_ref[d] = jnp.transpose(cum)[: cumt_ref.shape[1]]
        last = cum[0:1] if d else cum[rows - 1 : rows]
        wend_ref[at] = hi_lo(jnp.exp(jnp.minimum(last - cum, 0.0)) * delta[at])
        dec = jnp.where(iota((1, LANES), 1) < heads, jnp.exp(last), 0.0)
        dec_ref[d : d + 1] = dec


def norm(hidden, gain, dtw, dtb, lr):
    rows, width = hidden.shape
    heads = dtb.shape[1]
    return pl.pallas_call(
        norm_kernel,
        grid=(1,),
        in_specs=[
            fixed(rows, width), fixed(width // LANES, LANES), fixed(heads, width),
            fixed(1, heads), fixed(1, heads),
        ],
        out_specs=[
            fixed(2 * rows, width), fixed(2 * rows, LANES), fixed(2 * rows, LANES),
            fixed(2, 24, rows), fixed(2 * rows, 2 * LANES), fixed(8, LANES),
        ],
        out_shape=[
            jax.ShapeDtypeStruct((2 * rows, width), bf16),
            jax.ShapeDtypeStruct((2 * rows, LANES), f32),
            jax.ShapeDtypeStruct((2 * rows, LANES), f32),
            jax.ShapeDtypeStruct((2, 24, rows), f32),
            jax.ShapeDtypeStruct((2 * rows, 2 * LANES), bf16),
            jax.ShapeDtypeStruct((8, LANES), f32),
        ],
        scratch_shapes=[pltpu.VMEM((rows, width), bf16), pltpu.VMEM((LANES, width), bf16)],
        compiler_params=pltpu.CompilerParams(vmem_limit_bytes=16 << 20),
        cost_estimate=pl.CostEstimate(flops=4 << 30, bytes_accessed=5 << 20, transcendentals=0),
        name="norm",
    )(off_chip(hidden), off_chip(gain), off_chip(dtw), off_chip(dtb), off_chip(lr))


def entry_kernel(
    x_ref, prev_ref, next_ref, gain_ref, xw_ref, bcw_ref, xk_ref, bck_ref, wend_ref, dec_ref,
    xconv_ref, bc_ref, pay_ref,
    ext_ref, xin_ref, bcin_ref, st_ref, bt_ref, rim_ref, weighted_ref,
):
    width = x_ref.shape[1]
    rows = x_ref.shape[0] // 2
    n = pl.program_id(0)
    steps = pl.num_programs(0) - 1

    def prelude():
        ext_ref[EXTRA : EXTRA + 2 * rows] = x_ref[...]
        prev = prev_ref[...].astype(f32)
        rim_ref[0, :EXTRA] = x_ref[rows - EXTRA : rows]
        rim_ref[0, EXTRA:] = scaled(prev, scale_of(prev), gain_ref, 0)
        flip = flip_matrix(TILE)
        blocks = width // TILE
        after = next_ref[...]
        after_scale = scale_of(after.astype(f32))
        stacked = jnp.concatenate([after[:, b * TILE : (b + 1) * TILE] for b in range(blocks)], axis=0)
        stacked = mm(stacked, flip)
        rim_ref[1, :EXTRA] = x_ref[rows : rows + EXTRA]
        for b in range(blocks):
            mirror = blocks - 1 - b
            rim_ref[1, EXTRA:, b * TILE : (b + 1) * TILE] = scaled(
                stacked[mirror * HALO : (mirror + 1) * HALO], after_scale, gain_ref, b * 2
            )
        shape = (EXTRA, EXTRA + HALO)
        r, c = iota(shape, 0), iota(shape, 1)
        s = r % 8
        v = r // 8 - 4
        ahead = jnp.where(s == 0, EXTRA + HALO + v, EXTRA + 8 * v + s - 1)
        ahead = ((c == ahead) & (r >= 8)).astype(bf16)
        j = r // 8
        behind = jnp.where(s == 7, EXTRA + j, 8 * j + s + 1)
        behind = ((c == behind) & (r < 24)).astype(bf16)
        ext_ref[:EXTRA] = mm(ahead, rim_ref[0]).astype(bf16)
        ext_ref[EXTRA + 2 * rows :] = mm(behind, rim_ref[1]).astype(bf16)
        bcin_ref[...] = mm(ext_ref[...], bcw_ref[...]).astype(bf16).astype(f32)
        for d in range(2):
            for first in range(0, rows, CHUNK):
                at = slice(d * rows + first, d * rows + first + CHUNK)
                bc_ref[at] = conv_rows(bcin_ref, bck_ref[...], d, rows, first, CHUNK)
            at = slice(d * rows, (d + 1) * rows)
            bt_ref[d] = jnp.transpose(bc_ref[at, :STATE].astype(f32)).astype(bf16)

    def product():
        return mm(ext_ref[...], xw_ref[...]).astype(bf16).astype(f32)

    def finish():
        tile = n - 1
        spread_n = spread(tile * (TILE // HEAD_DIM), TILE)
        for d in range(2):
            for first in range(0, rows, CHUNK):
                at = slice(d * rows + first, d * rows + first + CHUNK)
                conv = conv_rows(xin_ref, xk_ref[...], d, rows, first, CHUNK)
                xconv_ref[at] = conv
                weighted_ref[at] = (conv.astype(f32) * mm(wend_ref[at], spread_n)).astype(bf16)
            column = pl.multiple_of(d * steps * TILE + tile * TILE, TILE)
            st_ref[:, pl.ds(column, TILE)] = mm(
                bt_ref[d], weighted_ref[d * rows : (d + 1) * rows]
            ).astype(bf16)

    @pl.when(n == 0)
    def _():
        prelude()
        xin_ref[...] = product()

    @pl.when((n > 0) & (n < steps))
    def _():
        finish()
        xin_ref[...] = product()

    @pl.when(n == steps)
    def _():
        finish()
        slots = pay_ref.shape[0]
        row = iota((8, LANES), 0)
        tails = []
        for d in range(2):
            dec = jnp.broadcast_to(dec_ref[d : d + 1], (8, LANES))
            hi = dec.astype(bf16).astype(f32)
            tails.append(jnp.where(row == 0, hi, jnp.where(row == 1, dec - hi, 0.0)).astype(bf16))
        for slot in range(slots):
            i, q = slot // 4, slot % 4
            for j in range(5):
                column = (5 * q + j) * LANES
                pay_ref[slot, 16 * j : 16 * j + 16] = st_ref[16 * i : 16 * i + 16, column : column + LANES]
            pay_ref[slot, 80:88] = tails[q // 2]


def entry(x, prev_rows, next_rows, gain, xw, bcw, xk, bck, wend, dec, slots):
    width = x.shape[1]
    rows = x.shape[0] // 2
    inner = xw.shape[1]
    steps = inner // TILE
    ahead = lambda n: jnp.minimum(n, steps - 1)
    behind = lambda n: jnp.maximum(n - 1, 0)
    whole = lambda *shape: pl.BlockSpec(shape, lambda n: (0,) * len(shape))
    once = lambda *shape: pl.BlockSpec(
        shape, lambda n: (0,) * len(shape), pipeline_mode=pl.Buffered(1)
    )
    vmem = pl.BlockSpec(memory_space=pltpu.VMEM)
    return pl.pallas_call(
        entry_kernel,
        grid=(steps + 1,),
        in_specs=[
            vmem, vmem, vmem, once(width // LANES, LANES),
            pl.BlockSpec((width, TILE), lambda n: (0, ahead(n))),
            once(width, 2 * STATE),
            pl.BlockSpec((4, TILE), lambda n: (0, behind(n))),
            once(4, 2 * STATE), vmem, vmem,
        ],
        out_specs=[
            pl.BlockSpec((2 * rows, TILE), lambda n: (0, behind(n))),
            whole(2 * rows, 2 * STATE), whole(slots, 88, LANES),
        ],
        out_shape=[
            pltpu.HBM((2 * rows, inner), bf16),
            pltpu.HBM((2 * rows, 2 * STATE), bf16),
            pltpu.HBM((slots, 88, LANES), bf16),
        ],
        scratch_shapes=[
            pltpu.VMEM((2 * rows + 2 * EXTRA, width), bf16),
            pltpu.VMEM((2 * rows + 2 * EXTRA, TILE), f32),
            pltpu.VMEM((2 * rows + 2 * EXTRA, TILE), f32),
            pltpu.VMEM((STATE, 2 * inner), bf16),
            pltpu.VMEM((2, STATE, rows), bf16),
            pltpu.VMEM((2, EXTRA + HALO, width), bf16),
            pltpu.VMEM((2 * rows, TILE), bf16),
        ],
        compiler_params=pltpu.CompilerParams(
            dimension_semantics=("arbitrary",), vmem_limit_bytes=26 << 20
        ),
        cost_estimate=pl.CostEstimate(
            flops=2 * 544 * width * (inner + 256), bytes_accessed=12 << 20, transcendentals=0
        ),
        name="entry",
    )(x, prev_rows, next_rows, off_chip(gain), off_chip(xw), off_chip(bcw), off_chip(xk), off_chip(bck), wend, dec)


def open_gate_kernel(x_ref, zw_ref, z_ref):
    z = mm(x_ref[...], zw_ref[...]).astype(bf16).astype(f32)
    z_ref[...] = silu(z).astype(bf16)


def open_gate(x, zw):
    height, width = x.shape
    inner = zw.shape[1]
    return pl.pallas_call(
        open_gate_kernel,
        grid=(inner // TILE,),
        in_specs=[fixed(height, width), pl.BlockSpec((width, TILE), lambda n: (0, n))],
        out_specs=pl.BlockSpec((height, TILE), lambda n: (0, n)),
        out_shape=jax.ShapeDtypeStruct((height, inner), bf16),
        compiler_params=pltpu.CompilerParams(
            dimension_semantics=("arbitrary",), vmem_limit_bytes=16 << 20
        ),
        cost_estimate=pl.CostEstimate(
            flops=2 * height * width * inner, bytes_accessed=16 << 20, transcendentals=0
        ),
        name="open_gate",
    )(off_chip(x), off_chip(zw))


def within_kernel(x_ref, bc_ref, cum_ref, cumt_ref, delta_ref, y_ref, gram_ref):
    d, n = pl.program_id(0), pl.program_id(1)
    rows = x_ref.shape[0]
    heads = TILE // HEAD_DIM

    @pl.when(n == 0)
    def _():
        gram = lax.dot_general(
            bc_ref[:, STATE:], bc_ref[:, :STATE], (((1,), (1,)), ((), ())), preferred_element_type=f32
        )
        t, s = time_of(iota((rows, rows), 0), rows), time_of(iota((rows, rows), 1), rows)
        seen = jnp.where(d == 0, t - s, s - t) >= 0
        gram_ref[...] = jnp.where(seen, gram, 0.0)

    weighted = x_ref[...].astype(f32) * mm(hi_lo(delta_ref[...]), spread(n * heads, TILE))
    cum = pltpu.roll(cum_ref[...], (LANES - n * heads) % LANES, 1)
    owner = iota((rows, TILE), 1) // HEAD_DIM
    total = jnp.zeros((rows, TILE), f32)
    for k in range(heads):
        behind = cumt_ref[0, pl.ds(n * heads + k, 1), :]
        decay = jnp.exp(jnp.minimum(cum[:, k : k + 1] - behind, 0.0)) * gram_ref[...]
        total = total + mm(decay.astype(bf16), jnp.where(owner == k, weighted, 0.0).astype(bf16))
    y_ref[...] = total


def within(xconv, bc, cum, cumt, delta):
    rows = xconv.shape[0] // 2
    inner = xconv.shape[1]
    return pl.pallas_call(
        within_kernel,
        grid=(2, inner // TILE),
        in_specs=[
            pl.BlockSpec((rows, TILE), lambda d, n: (d, n)),
            pl.BlockSpec((rows, 2 * STATE), lambda d, n: (d, 0)),
            pl.BlockSpec((rows, LANES), lambda d, n: (d, 0)),
            pl.BlockSpec((1, 24, rows), lambda d, n: (d, 0, 0)),
            pl.BlockSpec((rows, LANES), lambda d, n: (d, 0)),
        ],
        out_specs=pl.BlockSpec((rows, TILE), lambda d, n: (d, n)),
        out_shape=pltpu.HBM((2 * rows, inner), f32),
        scratch_shapes=[pltpu.VMEM((rows, rows), f32)],
        compiler_params=pltpu.CompilerParams(
            dimension_semantics=("arbitrary", "arbitrary"), vmem_limit_bytes=12 << 20
        ),
        cost_estimate=pl.CostEstimate(flops=3 << 30, bytes_accessed=5 << 20, transcendentals=3 << 20),
        name="within",
    )(off_chip(xconv), off_chip(bc), cum, cumt, delta)


def scan_kernel(q_ref, pay_ref, out_ref, carry_ref):
    q = q_ref[0]
    half, turned = q % 2, q // 2
    depth = pay_ref.shape[0]

    @pl.when(pl.program_id(0) == 0)
    def _():
        carry_ref[...] = jnp.zeros_like(carry_ref)

    first = half * (5 * LANES // HEAD_DIM)
    place = iota((LANES, 5 * LANES), 0) == first + iota((LANES, 5 * LANES), 1) // HEAD_DIM
    place = place.astype(bf16)
    carry = [carry_ref[16 * j : 16 * j + 16] for j in range(5)]
    for i in range(depth):
        at = jnp.where(turned == 1, depth - 1 - i, i)
        decays = mm(pay_ref[at, 80:88], place)
        decay = decays[0:1] + decays[1:2]
        for j in range(5):
            rows = slice(16 * j, 16 * j + 16)
            out_ref[at, rows] = carry[j].astype(bf16)
            carry[j] = carry[j] * decay[:, j * LANES : (j + 1) * LANES] + pay_ref[at, rows].astype(f32)
    for j in range(5):
        carry_ref[16 * j : 16 * j + 16] = carry[j]


def scan(q, pay):
    slots = pay.shape[0]
    depth = 8
    steps = slots // depth
    chunk = lambda i, q: (jnp.where(q[0] // 2 == 1, steps - 1 - i, i), 0, 0)
    return pl.pallas_call(
        scan_kernel,
        grid_spec=pltpu.PrefetchScalarGridSpec(
            num_scalar_prefetch=1,
            grid=(steps,),
            in_specs=[pl.BlockSpec((depth, 88, LANES), chunk)],
            out_specs=pl.BlockSpec((depth, 80, LANES), chunk),
            scratch_shapes=[pltpu.VMEM((80, LANES), f32)],
        ),
        out_shape=jax.ShapeDtypeStruct((slots, 80, LANES), bf16),
        compiler_params=pltpu.CompilerParams(
            dimension_semantics=("arbitrary",), vmem_limit_bytes=6 << 20
        ),
        name="scan",
    )(q, pay)


def weight_fetches(q, w_ref, near_ref, far_ref, sems):
    lanes = near_ref.shape[1]
    near = pl.ds(pl.multiple_of(q * lanes, LANES), lanes)
    far = pl.ds(pl.multiple_of((3 - q) * lanes, LANES), lanes)
    near_copies, far_copies = [], []
    for k in range(near_ref.shape[0] // TILE):
        rows = slice(k * TILE, (k + 1) * TILE)
        near_copies.append(pltpu.make_async_copy(w_ref.at[rows, near], near_ref.at[rows], sems.at[0, k]))
        far_copies.append(pltpu.make_async_copy(w_ref.at[rows, far], far_ref.at[rows], sems.at[1, k]))
    return near_copies, far_copies


def project_into(out_ref, g_ref, copies, near_ref, far_ref, adds):
    inner, lanes = near_ref.shape
    for copy in copies[1]:
        copy.wait()
    behind = mm(g_ref[:, inner:], far_ref[...]).astype(bf16)
    for copy in copies[0]:
        copy.wait()
    ahead = mm(g_ref[:, :inner], near_ref[...])
    flip = flip_matrix(LANES)
    blocks = lanes // LANES
    for b in range(blocks):
        at = slice(b * LANES, (b + 1) * LANES)
        source = slice((blocks - 1 - b) * LANES, (blocks - b) * LANES)
        total = ahead[:, at] + mm(behind[:, source], flip)
        for add in adds:
            total = total + add[:, at].astype(f32)
        out_ref[:, at] = total.astype(out_ref.dtype)


def weight_scratch(inner, lanes):
    return [
        pltpu.VMEM((inner, lanes), bf16),
        pltpu.VMEM((inner, lanes), bf16),
        pltpu.SemaphoreType.DMA((2, inner // TILE)),
    ]


def gate_kernel(
    target_ref, y_ref, z_ref, bc_ref, cum_ref, st_ref, gain_ref, w_ref,
    g_ref, out_ref,
    near_ref, far_ref, sems, held_ref,
):
    q = pl.program_id(0)
    rows, lanes = y_ref.shape
    groups = lanes // LANES
    copies = weight_fetches(target_ref[0], w_ref, near_ref, far_ref, sems)

    @pl.when(q == 0)
    def _():
        for copy in copies[1] + copies[0]:
            copy.start()

    state = jnp.concatenate([st_ref[:, 0, j].reshape(STATE, LANES) for j in range(groups)], axis=1)
    carried = mm(bc_ref[:, STATE:], state)
    reach = mm(hi_lo(jnp.exp(cum_ref[...])), spread((q % 2) * (lanes // HEAD_DIM), lanes))
    same = (iota((2 * LANES, LANES), 0) % LANES) // HEAD_DIM == iota((2 * LANES, LANES), 1) // HEAD_DIM
    same = same.astype(bf16)
    for b in range(groups):
        at = slice(b * LANES, (b + 1) * LANES)
        y = y_ref[:, at] + carried[:, at] * reach[:, at]
        part = y * z_ref[:, at].astype(f32)
        mean_sq = mm(hi_lo(part * part), same) * (1.0 / HEAD_DIM)
        gain = gain_ref[pl.ds((q % 2) * groups + b, 1), :]
        held_ref[:, at] = (part * lax.rsqrt(mean_sq + epsilon) * gain).astype(bf16)
    order = (iota((rows, rows), 0) == time_of(iota((rows, rows), 1), rows)).astype(bf16)
    g_ref[:, pl.ds(pl.multiple_of(q * lanes, LANES), lanes)] = mm(order, held_ref[...]).astype(bf16)

    @pl.when(q == pl.num_programs(0) - 1)
    def _():
        project_into(out_ref, g_ref, copies, near_ref, far_ref, ())


def gate(target, y, z, bc, cum, state, gain, weight):
    rows = y.shape[0] // 2
    inner = y.shape[1]
    lanes = inner // 2
    groups = lanes // LANES
    columns = weight.shape[1] // 4
    return pl.pallas_call(
        gate_kernel,
        grid_spec=pltpu.PrefetchScalarGridSpec(
            num_scalar_prefetch=1,
            grid=(4,),
            in_specs=[
                pl.BlockSpec((rows, lanes), lambda q, t: (q // 2, q % 2)),
                pl.BlockSpec((rows, lanes), lambda q, t: (q // 2, q % 2)),
                pl.BlockSpec((rows, 2 * STATE), lambda q, t: (q // 2, 0)),
                pl.BlockSpec((rows, LANES), lambda q, t: (q // 2, 0)),
                pl.BlockSpec((8, 1, groups, 16, LANES), lambda q, t: (0, q, 0, 0, 0)),
                fixed(2 * groups, LANES),
                pl.BlockSpec(memory_space=pltpu.HBM),
            ],
            out_specs=[fixed(rows, 2 * inner), fixed(rows, columns)],
            scratch_shapes=weight_scratch(inner, columns) + [pltpu.VMEM((rows, lanes), bf16)],
        ),
        out_shape=[
            jax.ShapeDtypeStruct((rows, 2 * inner), bf16),
            jax.ShapeDtypeStruct((rows, columns), bf16),
        ],
        compiler_params=pltpu.CompilerParams(
            dimension_semantics=("arbitrary",), vmem_limit_bytes=20 << 20
        ),
        name="gate",
    )(target, off_chip(y), z, off_chip(bc), cum, state.reshape(8, 4, groups, 16, LANES), off_chip(gain), off_chip(weight))


def project_kernel(has_add, q_ref, g_ref, w_ref, *rest):
    adds, (out_ref, near_ref, far_ref, sems) = rest[:has_add], rest[has_add:]
    copies = weight_fetches(q_ref[0], w_ref, near_ref, far_ref, sems)
    for copy in copies[1] + copies[0]:
        copy.start()
    project_into(out_ref, g_ref, copies, near_ref, far_ref, adds)


def project(q, gated, weight, dtype, *adds):
    rows = gated.shape[0]
    inner, width = weight.shape
    lanes = width // 4
    vmem = pl.BlockSpec(memory_space=pltpu.VMEM)
    return pl.pallas_call(
        functools.partial(project_kernel, len(adds)),
        in_specs=[pl.BlockSpec(memory_space=pltpu.SMEM), vmem, pl.BlockSpec(memory_space=pltpu.HBM)]
        + [vmem for _ in adds],
        out_specs=vmem,
        out_shape=jax.ShapeDtypeStruct((rows, lanes), dtype),
        scratch_shapes=weight_scratch(inner, lanes),
        compiler_params=pltpu.CompilerParams(vmem_limit_bytes=16 << 20),
        cost_estimate=pl.CostEstimate(
            flops=4 * rows * inner * lanes, bytes_accessed=5 << 20, transcendentals=0
        ),
        name="project",
    )(q, gated, off_chip(weight), *adds)


def per_device(
    hidden, norm_gain, x_weight, z_weight, bc_weight, dt_weight, x_kernel, bc_kernel,
    dt_bias, log_rate, out_gain, out_weight,
):
    blocks = lax.axis_size("ctx")
    place = lax.axis_index("ctx")
    head = lax.axis_index("head")
    prev_rows = lax.ppermute(hidden[-HALO:], "ctx", [(i, i + 1) for i in range(blocks - 1)])
    next_rows = lax.ppermute(hidden[:HALO], "ctx", [(i + 1, i) for i in range(blocks - 1)])
    gain = norm_gain.reshape(-1, LANES)
    normed, delta, cum, cumt, wend, dec = norm(hidden, gain, dt_weight.T, dt_bias[None], log_rate[None])
    xconv, bc, pay = entry(
        normed, prev_rows, next_rows, gain, x_weight, bc_weight, x_kernel, bc_kernel, wend, dec, blocks
    )
    pay = lax.all_to_all(pay, "ctx", 0, 0, tiled=True)
    y = within(xconv, bc, cum, cumt, delta)
    pay, y = lax.optimization_barrier((pay, y))
    state = scan((place % 4)[None], pay)
    state = lax.all_to_all(state, "ctx", 0, 0, tiled=True)
    open_z = open_gate(normed, z_weight)
    core, far = head % 2, head // 2
    quarter = lambda f, c: (2 * f + c)[None]
    core_swap = [(0, 1), (1, 0), (2, 3), (3, 2)]
    far_swap = [(0, 2), (2, 0), (1, 3), (3, 1)]
    gated, first = gate(
        quarter(1 - far, 1 - core), y, open_z, bc, cum, state, out_gain.reshape(-1, LANES), out_weight
    )
    first = lax.ppermute(first, "head", core_swap)
    second = project(quarter(1 - far, core), gated, out_weight, bf16, first)
    second, gated = lax.optimization_barrier((second, gated))
    second = lax.ppermute(second, "head", far_swap)
    third = project(quarter(far, 1 - core), gated, out_weight, bf16)
    third = lax.ppermute(third, "head", core_swap)
    lanes = hidden.shape[1] // 4
    residual = lax.dynamic_slice_in_dim(hidden, head * lanes, lanes, 1)
    own = project(quarter(far, core), gated, out_weight, f32, third, residual)
    return (own + second.astype(f32)).astype(bf16)


def solution(mesh):
    return jax.shard_map(
        per_device,
        mesh=mesh,
        in_specs=(
            P("ctx", None), P(), P(None, "head"), P(None, "head"), P(), P(None, "head"),
            P(None, "head"), P(), P("head"), P("head"), P("head"), P("head", None),
        ),
        out_specs=P("ctx", "head"),
        check_vma=False,
    )
```

```python
import functools

import jax
import jax.numpy as jnp
from jax import lax
from jax.experimental import pallas as pl
from jax.experimental.pallas import tpu as pltpu
from jax.sharding import PartitionSpec as P

HEAD_DIM = 64
STATE = 128
HALO = 16
EXTRA = 32
CHUNK = 64
FETCHES = 5
TILE = 256
LANES = 128
epsilon = 1e-05
f32 = jnp.float32
bf16 = jnp.bfloat16


def mm(a, b, precision=None):
    return jnp.dot(a, b, preferred_element_type=f32, precision=precision)


def iota(shape, dim):
    return lax.broadcasted_iota(jnp.int32, shape, dim)


def silu(v):
    return v * jax.nn.sigmoid(v)


def flip_matrix(n):
    return (iota((n, n), 0) + iota((n, n), 1) == n - 1).astype(bf16)


def hi_lo(v):
    hi = v.astype(bf16)
    return jnp.concatenate([hi, (v - hi.astype(f32)).astype(bf16)], axis=1)


def spread(first, width):
    rows = iota((2 * LANES, width), 0) % LANES
    return (rows == first + iota((2 * LANES, width), 1) // HEAD_DIM).astype(bf16)


def time_of(index, rows):
    return (index % 8) * (rows // 8) + index // 8


def conv_rows(ext_ref, taps, direction, rows, first, count):
    base = (EXTRA - 24 if direction == 0 else EXTRA + rows) + first
    total = None
    for k in range(4):
        at = base + 8 * (k if direction == 0 else 3 - k)
        term = taps[k : k + 1] * ext_ref[at : at + count]
        total = term if total is None else total + term
    return silu(total).astype(bf16)


def cumulate(matrix, v, lanes):
    v = jnp.where(iota(v.shape, 1) < lanes, v, 0.0)
    hi = v.astype(bf16).astype(f32)
    mid = (v - hi).astype(bf16).astype(f32)
    low = v - hi - mid
    packed = hi + pltpu.roll(mid, 32, 1) + pltpu.roll(low, 64, 1)
    out = mm(matrix, packed.astype(bf16))
    return out + pltpu.roll(out, LANES - 32, 1) + pltpu.roll(out, LANES - 64, 1)


def off_chip(x):
    return pltpu.with_memory_space_constraint(x, pltpu.HBM)


def fixed(*shape):
    return pl.BlockSpec(shape, lambda *_: (0,) * len(shape), pipeline_mode=pl.Buffered(1))


def scale_of(v):
    return lax.rsqrt(jnp.mean(v * v, axis=-1, keepdims=True) + epsilon)


def scaled(v, scale, gain_ref, first):
    parts = [
        (v[:, g * LANES : (g + 1) * LANES] * scale) * gain_ref[first + g : first + g + 1]
        for g in range(v.shape[1] // LANES)
    ]
    return jnp.concatenate(parts, axis=1).astype(bf16)


def norm_kernel(
    h_ref, gain_ref, dtw_ref, dtb_ref, lr_ref, xw_ref, bcw_ref,
    x_ref, delta_ref, cum_ref, cumt_ref, wend_ref, dec_ref, xw_kept, bcw_kept,
    raw_ref, dtp_ref, sems,
):
    rows, width = h_ref.shape
    heads = dtb_ref.shape[1]
    copies = [pltpu.make_async_copy(bcw_ref, bcw_kept, sems.at[0])]
    for k in range(FETCHES):
        part = slice(k * width // FETCHES, (k + 1) * width // FETCHES)
        copies.append(pltpu.make_async_copy(xw_ref.at[part], xw_kept.at[part], sems.at[1 + k]))
    for copy in copies:
        copy.start()

    order = (iota((rows, rows), 1) == time_of(iota((rows, rows), 0), rows)).astype(bf16)
    flip = flip_matrix(TILE)
    blocks = width // TILE
    squares = jnp.zeros((rows, LANES), f32)
    for b in range(blocks):
        cols = slice(b * TILE, (b + 1) * TILE)
        v = mm(order, h_ref[:, cols])
        raw_ref[:, cols] = v.astype(bf16)
        squares = squares + v[:, :LANES] * v[:, :LANES] + v[:, LANES:] * v[:, LANES:]
    mean_sq = jnp.sum(squares, axis=-1, keepdims=True) * (1.0 / width)
    scale = jnp.broadcast_to(lax.rsqrt(mean_sq + epsilon), (rows, LANES))
    for b in range(blocks):
        cols = slice(b * TILE, (b + 1) * TILE)
        mirror = blocks - 1 - b
        x_ref[:rows, cols] = scaled(raw_ref[:, cols].astype(f32), scale, gain_ref, b * 2)
        turned = mm(raw_ref[:, mirror * TILE : (mirror + 1) * TILE], flip)
        x_ref[rows:, cols] = scaled(turned, scale, gain_ref, b * 2)
    dtp_ref[...] = jnp.zeros_like(dtp_ref)
    dtp_ref[0:heads] = dtw_ref[...]
    bias = jnp.concatenate([dtb_ref[...], jnp.zeros((1, LANES - heads), f32)], axis=1)
    rate = jnp.concatenate([lr_ref[...], jnp.zeros((1, LANES - heads), f32)], axis=1)
    dt = lax.dot_general(
        x_ref[...], dtp_ref[...], (((1,), (1,)), ((), ())), preferred_element_type=f32
    )
    dt = dt + bias
    delta = jnp.maximum(dt, 0.0) + jnp.log1p(jnp.exp(-jnp.abs(dt)))
    delta_ref[...] = delta
    log_decay = -delta * jnp.exp(rate)
    later, sooner = time_of(iota((rows, rows), 0), rows), time_of(iota((rows, rows), 1), rows)
    lower = (later >= sooner).astype(bf16)
    upper = (later <= sooner).astype(bf16)
    for d in range(2):
        at = slice(d * rows, (d + 1) * rows)
        cum = cumulate(upper if d else lower, log_decay[at], heads)
        cum_ref[at] = cum
        cumt_ref[d] = jnp.transpose(cum)[: cumt_ref.shape[1]]
        last = cum[0:1] if d else cum[rows - 1 : rows]
        wend_ref[at] = hi_lo(jnp.exp(jnp.minimum(last - cum, 0.0)) * delta[at])
        dec = jnp.where(iota((1, LANES), 1) < heads, jnp.exp(last), 0.0)
        dec_ref[d : d + 1] = dec
    for copy in copies:
        copy.wait()


def norm(hidden, gain, dtw, dtb, lr, xw, bcw):
    rows, width = hidden.shape
    heads = dtb.shape[1]
    return pl.pallas_call(
        norm_kernel,
        grid=(1,),
        in_specs=[
            fixed(rows, width), fixed(width // LANES, LANES), fixed(heads, width),
            fixed(1, heads), fixed(1, heads),
            pl.BlockSpec(memory_space=pltpu.HBM), pl.BlockSpec(memory_space=pltpu.HBM),
        ],
        out_specs=[
            fixed(2 * rows, width), fixed(2 * rows, LANES), fixed(2 * rows, LANES),
            fixed(2, 24, rows), fixed(2 * rows, 2 * LANES), fixed(8, LANES),
            pl.BlockSpec(memory_space=pltpu.VMEM), pl.BlockSpec(memory_space=pltpu.VMEM),
        ],
        out_shape=[
            jax.ShapeDtypeStruct((2 * rows, width), bf16),
            jax.ShapeDtypeStruct((2 * rows, LANES), f32),
            jax.ShapeDtypeStruct((2 * rows, LANES), f32),
            jax.ShapeDtypeStruct((2, 24, rows), f32),
            jax.ShapeDtypeStruct((2 * rows, 2 * LANES), bf16),
            jax.ShapeDtypeStruct((8, LANES), f32),
            jax.ShapeDtypeStruct(xw.shape, bf16),
            jax.ShapeDtypeStruct(bcw.shape, bf16),
        ],
        scratch_shapes=[
            pltpu.VMEM((rows, width), bf16),
            pltpu.VMEM((LANES, width), bf16),
            pltpu.SemaphoreType.DMA((1 + FETCHES,)),
        ],
        compiler_params=pltpu.CompilerParams(vmem_limit_bytes=28 << 20),
        cost_estimate=pl.CostEstimate(flops=4 << 30, bytes_accessed=5 << 20, transcendentals=0),
        name="norm",
    )(
        off_chip(hidden), off_chip(gain), off_chip(dtw), off_chip(dtb), off_chip(lr), off_chip(xw), off_chip(bcw)
    )


def entry_kernel(
    x_ref, prev_ref, next_ref, gain_ref, xw_ref, bcw_ref, xk_ref, bck_ref, wend_ref, dec_ref,
    xconv_ref, bc_ref, pay_ref,
    ext_ref, xin_ref, bcin_ref, st_ref, bt_ref, rim_ref, weighted_ref,
):
    width = x_ref.shape[1]
    rows = x_ref.shape[0] // 2
    n = pl.program_id(0)
    steps = pl.num_programs(0) - 1

    def prelude():
        ext_ref[EXTRA : EXTRA + 2 * rows] = x_ref[...]
        prev = prev_ref[...].astype(f32)
        rim_ref[0, :EXTRA] = x_ref[rows - EXTRA : rows]
        rim_ref[0, EXTRA:] = scaled(prev, scale_of(prev), gain_ref, 0)
        flip = flip_matrix(TILE)
        blocks = width // TILE
        after = next_ref[...]
        after_scale = scale_of(after.astype(f32))
        stacked = jnp.concatenate([after[:, b * TILE : (b + 1) * TILE] for b in range(blocks)], axis=0)
        stacked = mm(stacked, flip)
        rim_ref[1, :EXTRA] = x_ref[rows : rows + EXTRA]
        for b in range(blocks):
            mirror = blocks - 1 - b
            rim_ref[1, EXTRA:, b * TILE : (b + 1) * TILE] = scaled(
                stacked[mirror * HALO : (mirror + 1) * HALO], after_scale, gain_ref, b * 2
            )
        shape = (EXTRA, EXTRA + HALO)
        r, c = iota(shape, 0), iota(shape, 1)
        s = r % 8
        v = r // 8 - 4
        ahead = jnp.where(s == 0, EXTRA + HALO + v, EXTRA + 8 * v + s - 1)
        ahead = ((c == ahead) & (r >= 8)).astype(bf16)
        j = r // 8
        behind = jnp.where(s == 7, EXTRA + j, 8 * j + s + 1)
        behind = ((c == behind) & (r < 24)).astype(bf16)
        ext_ref[:EXTRA] = mm(ahead, rim_ref[0]).astype(bf16)
        ext_ref[EXTRA + 2 * rows :] = mm(behind, rim_ref[1]).astype(bf16)
        bcin_ref[...] = mm(ext_ref[...], bcw_ref[...]).astype(bf16).astype(f32)
        for d in range(2):
            for first in range(0, rows, CHUNK):
                at = slice(d * rows + first, d * rows + first + CHUNK)
                bc_ref[at] = conv_rows(bcin_ref, bck_ref[...], d, rows, first, CHUNK)
            at = slice(d * rows, (d + 1) * rows)
            bt_ref[d] = jnp.transpose(bc_ref[at, :STATE].astype(f32)).astype(bf16)

    def product():
        column = pl.multiple_of(jnp.minimum(n, steps - 1) * TILE, TILE)
        return mm(ext_ref[...], xw_ref[:, pl.ds(column, TILE)]).astype(bf16).astype(f32)

    def finish():
        tile = n - 1
        spread_n = spread(tile * (TILE // HEAD_DIM), TILE)
        for d in range(2):
            for first in range(0, rows, CHUNK):
                at = slice(d * rows + first, d * rows + first + CHUNK)
                conv = conv_rows(xin_ref, xk_ref[...], d, rows, first, CHUNK)
                xconv_ref[at] = conv
                weighted_ref[at] = (conv.astype(f32) * mm(wend_ref[at], spread_n)).astype(bf16)
            column = pl.multiple_of(d * steps * TILE + tile * TILE, TILE)
            st_ref[:, pl.ds(column, TILE)] = mm(
                bt_ref[d], weighted_ref[d * rows : (d + 1) * rows]
            ).astype(bf16)

    @pl.when(n == 0)
    def _():
        prelude()
        xin_ref[...] = product()

    @pl.when((n > 0) & (n < steps))
    def _():
        finish()
        xin_ref[...] = product()

    @pl.when(n == steps)
    def _():
        finish()
        slots = pay_ref.shape[0]
        row = iota((8, LANES), 0)
        tails = []
        for d in range(2):
            dec = jnp.broadcast_to(dec_ref[d : d + 1], (8, LANES))
            hi = dec.astype(bf16).astype(f32)
            tails.append(jnp.where(row == 0, hi, jnp.where(row == 1, dec - hi, 0.0)).astype(bf16))
        for slot in range(slots):
            i, q = slot // 4, slot % 4
            for j in range(5):
                column = (5 * q + j) * LANES
                pay_ref[slot, 16 * j : 16 * j + 16] = st_ref[16 * i : 16 * i + 16, column : column + LANES]
            pay_ref[slot, 80:88] = tails[q // 2]


def entry(x, prev_rows, next_rows, gain, xw, bcw, xk, bck, wend, dec, slots):
    width = x.shape[1]
    rows = x.shape[0] // 2
    inner = xw.shape[1]
    steps = inner // TILE
    behind = lambda n: jnp.maximum(n - 1, 0)
    whole = lambda *shape: pl.BlockSpec(shape, lambda n: (0,) * len(shape))
    once = lambda *shape: pl.BlockSpec(
        shape, lambda n: (0,) * len(shape), pipeline_mode=pl.Buffered(1)
    )
    vmem = pl.BlockSpec(memory_space=pltpu.VMEM)
    return pl.pallas_call(
        entry_kernel,
        grid=(steps + 1,),
        in_specs=[
            vmem, vmem, vmem, once(width // LANES, LANES),
            vmem, vmem,
            pl.BlockSpec((4, TILE), lambda n: (0, behind(n))),
            once(4, 2 * STATE), vmem, vmem,
        ],
        out_specs=[
            pl.BlockSpec((2 * rows, TILE), lambda n: (0, behind(n))),
            whole(2 * rows, 2 * STATE), whole(slots, 88, LANES),
        ],
        out_shape=[
            pltpu.HBM((2 * rows, inner), bf16),
            pltpu.HBM((2 * rows, 2 * STATE), bf16),
            pltpu.HBM((slots, 88, LANES), bf16),
        ],
        scratch_shapes=[
            pltpu.VMEM((2 * rows + 2 * EXTRA, width), bf16),
            pltpu.VMEM((2 * rows + 2 * EXTRA, TILE), f32),
            pltpu.VMEM((2 * rows + 2 * EXTRA, TILE), f32),
            pltpu.VMEM((STATE, 2 * inner), bf16),
            pltpu.VMEM((2, STATE, rows), bf16),
            pltpu.VMEM((2, EXTRA + HALO, width), bf16),
            pltpu.VMEM((2 * rows, TILE), bf16),
        ],
        compiler_params=pltpu.CompilerParams(
            dimension_semantics=("arbitrary",), vmem_limit_bytes=26 << 20
        ),
        cost_estimate=pl.CostEstimate(
            flops=2 * 544 * width * (inner + 256), bytes_accessed=12 << 20, transcendentals=0
        ),
        name="entry",
    )(x, prev_rows, next_rows, off_chip(gain), xw, bcw, off_chip(xk), off_chip(bck), wend, dec)


def open_gate_kernel(x_ref, zw_ref, z_ref):
    z = mm(x_ref[...], zw_ref[...]).astype(bf16).astype(f32)
    z_ref[...] = silu(z).astype(bf16)


def open_gate(x, zw):
    height, width = x.shape
    inner = zw.shape[1]
    return pl.pallas_call(
        open_gate_kernel,
        grid=(inner // TILE,),
        in_specs=[fixed(height, width), pl.BlockSpec((width, TILE), lambda n: (0, n))],
        out_specs=pl.BlockSpec((height, TILE), lambda n: (0, n)),
        out_shape=jax.ShapeDtypeStruct((height, inner), bf16),
        compiler_params=pltpu.CompilerParams(
            dimension_semantics=("arbitrary",), vmem_limit_bytes=16 << 20
        ),
        cost_estimate=pl.CostEstimate(
            flops=2 * height * width * inner, bytes_accessed=16 << 20, transcendentals=0
        ),
        name="open_gate",
    )(off_chip(x), off_chip(zw))


def within_kernel(x_ref, bc_ref, cum_ref, cumt_ref, delta_ref, y_ref, gram_ref):
    d, n = pl.program_id(0), pl.program_id(1)
    rows = x_ref.shape[0]
    heads = TILE // HEAD_DIM

    @pl.when(n == 0)
    def _():
        gram = lax.dot_general(
            bc_ref[:, STATE:], bc_ref[:, :STATE], (((1,), (1,)), ((), ())), preferred_element_type=f32
        )
        t, s = time_of(iota((rows, rows), 0), rows), time_of(iota((rows, rows), 1), rows)
        seen = jnp.where(d == 0, t - s, s - t) >= 0
        gram_ref[...] = jnp.where(seen, gram, 0.0)

    weighted = x_ref[...].astype(f32) * mm(hi_lo(delta_ref[...]), spread(n * heads, TILE))
    cum = pltpu.roll(cum_ref[...], (LANES - n * heads) % LANES, 1)
    owner = iota((rows, TILE), 1) // HEAD_DIM
    total = jnp.zeros((rows, TILE), f32)
    for k in range(heads):
        behind = cumt_ref[0, pl.ds(n * heads + k, 1), :]
        decay = jnp.exp(jnp.minimum(cum[:, k : k + 1] - behind, 0.0)) * gram_ref[...]
        total = total + mm(decay.astype(bf16), jnp.where(owner == k, weighted, 0.0).astype(bf16))
    y_ref[...] = total.astype(bf16)


def within(xconv, bc, cum, cumt, delta):
    rows = xconv.shape[0] // 2
    inner = xconv.shape[1]
    return pl.pallas_call(
        within_kernel,
        grid=(2, inner // TILE),
        in_specs=[
            pl.BlockSpec((rows, TILE), lambda d, n: (d, n)),
            pl.BlockSpec((rows, 2 * STATE), lambda d, n: (d, 0)),
            pl.BlockSpec((rows, LANES), lambda d, n: (d, 0)),
            pl.BlockSpec((1, 24, rows), lambda d, n: (d, 0, 0)),
            pl.BlockSpec((rows, LANES), lambda d, n: (d, 0)),
        ],
        out_specs=pl.BlockSpec((rows, TILE), lambda d, n: (d, n)),
        out_shape=pltpu.HBM((2 * rows, inner), bf16),
        scratch_shapes=[pltpu.VMEM((rows, rows), f32)],
        compiler_params=pltpu.CompilerParams(
            dimension_semantics=("arbitrary", "arbitrary"), vmem_limit_bytes=12 << 20
        ),
        cost_estimate=pl.CostEstimate(flops=3 << 30, bytes_accessed=5 << 20, transcendentals=3 << 20),
        name="within",
    )(off_chip(xconv), off_chip(bc), cum, cumt, delta)


def scan_kernel(q_ref, pay_ref, out_ref, carry_ref, dec_ref):
    q = q_ref[0]
    half, turned = q % 2, q // 2
    depth = pay_ref.shape[0]

    @pl.when(pl.program_id(0) == 0)
    def _():
        carry_ref[...] = jnp.zeros_like(carry_ref)

    first = half * (5 * LANES // HEAD_DIM)
    place = iota((LANES, 5 * LANES), 0) == first + iota((LANES, 5 * LANES), 1) // HEAD_DIM
    place = place.astype(bf16)
    tails = pay_ref[:, 80:88].astype(f32).reshape(8 * depth, LANES).astype(bf16)
    dec_ref[...] = mm(tails, place)
    carry = [carry_ref[16 * j : 16 * j + 16] for j in range(5)]
    for i in range(depth):
        at = jnp.where(turned == 1, depth - 1 - i, i)
        decays = dec_ref[pl.ds(pl.multiple_of(8 * at, 8), 8)]
        decay = decays[0:1] + decays[1:2]
        for j in range(5):
            rows = slice(16 * j, 16 * j + 16)
            out_ref[at, rows] = carry[j].astype(bf16)
            carry[j] = carry[j] * decay[:, j * LANES : (j + 1) * LANES] + pay_ref[at, rows].astype(f32)
    for j in range(5):
        carry_ref[16 * j : 16 * j + 16] = carry[j]


def scan(q, pay):
    slots = pay.shape[0]
    depth = 8
    steps = slots // depth
    chunk = lambda i, q: (jnp.where(q[0] // 2 == 1, steps - 1 - i, i), 0, 0)
    return pl.pallas_call(
        scan_kernel,
        grid_spec=pltpu.PrefetchScalarGridSpec(
            num_scalar_prefetch=1,
            grid=(steps,),
            in_specs=[pl.BlockSpec((depth, 88, LANES), chunk)],
            out_specs=pl.BlockSpec((depth, 80, LANES), chunk),
            scratch_shapes=[pltpu.VMEM((80, LANES), f32), pltpu.VMEM((8 * depth, 5 * LANES), f32)],
        ),
        out_shape=jax.ShapeDtypeStruct((slots, 80, LANES), bf16),
        compiler_params=pltpu.CompilerParams(
            dimension_semantics=("arbitrary",), vmem_limit_bytes=6 << 20
        ),
        name="scan",
    )(q, pay)


def weight_fetches(q, w_ref, near_ref, far_ref, sems):
    lanes = near_ref.shape[1]
    near = pl.ds(pl.multiple_of(q * lanes, LANES), lanes)
    far = pl.ds(pl.multiple_of((3 - q) * lanes, LANES), lanes)
    near_copies, far_copies = [], []
    for k in range(near_ref.shape[0] // TILE):
        rows = slice(k * TILE, (k + 1) * TILE)
        near_copies.append(pltpu.make_async_copy(w_ref.at[rows, near], near_ref.at[rows], sems.at[0, k]))
        far_copies.append(pltpu.make_async_copy(w_ref.at[rows, far], far_ref.at[rows], sems.at[1, k]))
    return near_copies, far_copies


def project_into(out_ref, g_ref, copies, near_ref, far_ref, adds):
    inner, lanes = near_ref.shape
    for copy in copies[1]:
        copy.wait()
    behind = mm(g_ref[:, inner:], far_ref[...]).astype(bf16)
    for copy in copies[0]:
        copy.wait()
    ahead = mm(g_ref[:, :inner], near_ref[...])
    flip = flip_matrix(LANES)
    blocks = lanes // LANES
    for b in range(blocks):
        at = slice(b * LANES, (b + 1) * LANES)
        source = slice((blocks - 1 - b) * LANES, (blocks - b) * LANES)
        total = ahead[:, at] + mm(behind[:, source], flip)
        for add in adds:
            total = total + add[:, at].astype(f32)
        out_ref[:, at] = total.astype(out_ref.dtype)


def weight_scratch(inner, lanes):
    return [
        pltpu.VMEM((inner, lanes), bf16),
        pltpu.VMEM((inner, lanes), bf16),
        pltpu.SemaphoreType.DMA((2, inner // TILE)),
    ]


def gate_kernel(
    target_ref, y_ref, z_ref, bc_ref, cum_ref, st_ref, gain_ref, w_ref,
    g_ref, out_ref,
    near_ref, far_ref, sems, held_ref,
):
    q = pl.program_id(0)
    rows, lanes = y_ref.shape
    groups = lanes // LANES
    copies = weight_fetches(target_ref[0], w_ref, near_ref, far_ref, sems)

    @pl.when(q == 0)
    def _():
        for copy in copies[1] + copies[0]:
            copy.start()

    state = jnp.concatenate([st_ref[:, 0, j].reshape(STATE, LANES) for j in range(groups)], axis=1)
    carried = mm(bc_ref[:, STATE:], state)
    reach = mm(hi_lo(jnp.exp(cum_ref[...])), spread((q % 2) * (lanes // HEAD_DIM), lanes))
    same = iota((LANES, LANES), 0) // HEAD_DIM == iota((LANES, LANES), 1) // HEAD_DIM
    same = same.astype(bf16)
    for b in range(groups):
        at = slice(b * LANES, (b + 1) * LANES)
        y = y_ref[:, at].astype(f32) + carried[:, at] * reach[:, at]
        part = y * z_ref[:, at].astype(f32)
        mean_sq = mm((part * part).astype(bf16), same) * (1.0 / HEAD_DIM)
        gain = gain_ref[pl.ds((q % 2) * groups + b, 1), :]
        held_ref[:, at] = (part * lax.rsqrt(mean_sq + epsilon) * gain).astype(bf16)
    order = (iota((rows, rows), 0) == time_of(iota((rows, rows), 1), rows)).astype(bf16)
    g_ref[:, pl.ds(pl.multiple_of(q * lanes, LANES), lanes)] = mm(order, held_ref[...]).astype(bf16)

    @pl.when(q == pl.num_programs(0) - 1)
    def _():
        project_into(out_ref, g_ref, copies, near_ref, far_ref, ())


def gate(target, y, z, bc, cum, state, gain, weight):
    rows = y.shape[0] // 2
    inner = y.shape[1]
    lanes = inner // 2
    groups = lanes // LANES
    columns = weight.shape[1] // 4
    return pl.pallas_call(
        gate_kernel,
        grid_spec=pltpu.PrefetchScalarGridSpec(
            num_scalar_prefetch=1,
            grid=(4,),
            in_specs=[
                pl.BlockSpec((rows, lanes), lambda q, t: (q // 2, q % 2)),
                pl.BlockSpec((rows, lanes), lambda q, t: (q // 2, q % 2)),
                pl.BlockSpec((rows, 2 * STATE), lambda q, t: (q // 2, 0)),
                pl.BlockSpec((rows, LANES), lambda q, t: (q // 2, 0)),
                pl.BlockSpec((8, 1, groups, 16, LANES), lambda q, t: (0, q, 0, 0, 0)),
                fixed(2 * groups, LANES),
                pl.BlockSpec(memory_space=pltpu.HBM),
            ],
            out_specs=[fixed(rows, 2 * inner), fixed(rows, columns)],
            scratch_shapes=weight_scratch(inner, columns) + [pltpu.VMEM((rows, lanes), bf16)],
        ),
        out_shape=[
            jax.ShapeDtypeStruct((rows, 2 * inner), bf16),
            jax.ShapeDtypeStruct((rows, columns), bf16),
        ],
        compiler_params=pltpu.CompilerParams(
            dimension_semantics=("arbitrary",), vmem_limit_bytes=20 << 20
        ),
        name="gate",
    )(target, off_chip(y), z, off_chip(bc), cum, state.reshape(8, 4, groups, 16, LANES), off_chip(gain), off_chip(weight))


def project_kernel(has_add, q_ref, g_ref, w_ref, *rest):
    adds, (out_ref, near_ref, far_ref, sems) = rest[:has_add], rest[has_add:]
    copies = weight_fetches(q_ref[0], w_ref, near_ref, far_ref, sems)
    for copy in copies[1] + copies[0]:
        copy.start()
    project_into(out_ref, g_ref, copies, near_ref, far_ref, adds)


def project(q, gated, weight, dtype, *adds):
    rows = gated.shape[0]
    inner, width = weight.shape
    lanes = width // 4
    vmem = pl.BlockSpec(memory_space=pltpu.VMEM)
    return pl.pallas_call(
        functools.partial(project_kernel, len(adds)),
        in_specs=[pl.BlockSpec(memory_space=pltpu.SMEM), vmem, pl.BlockSpec(memory_space=pltpu.HBM)]
        + [vmem for _ in adds],
        out_specs=vmem,
        out_shape=jax.ShapeDtypeStruct((rows, lanes), dtype),
        scratch_shapes=weight_scratch(inner, lanes),
        compiler_params=pltpu.CompilerParams(vmem_limit_bytes=16 << 20),
        cost_estimate=pl.CostEstimate(
            flops=4 * rows * inner * lanes, bytes_accessed=5 << 20, transcendentals=0
        ),
        name="project",
    )(q, gated, off_chip(weight), *adds)


def per_device(
    hidden, norm_gain, x_weight, z_weight, bc_weight, dt_weight, x_kernel, bc_kernel,
    dt_bias, log_rate, out_gain, out_weight,
):
    blocks = lax.axis_size("ctx")
    place = lax.axis_index("ctx")
    head = lax.axis_index("head")
    prev_rows = lax.ppermute(hidden[-HALO:], "ctx", [(i, i + 1) for i in range(blocks - 1)])
    next_rows = lax.ppermute(hidden[:HALO], "ctx", [(i + 1, i) for i in range(blocks - 1)])
    gain = norm_gain.reshape(-1, LANES)
    normed, delta, cum, cumt, wend, dec, x_kept, bc_kept = norm(
        hidden, gain, dt_weight.T, dt_bias[None], log_rate[None], x_weight, bc_weight
    )
    xconv, bc, pay = entry(
        normed, prev_rows, next_rows, gain, x_kept, bc_kept, x_kernel, bc_kernel, wend, dec, blocks
    )
    pay = lax.all_to_all(pay, "ctx", 0, 0, tiled=True)
    y = within(xconv, bc, cum, cumt, delta)
    pay, y = lax.optimization_barrier((pay, y))
    state = scan((place % 4)[None], pay)
    state = lax.all_to_all(state, "ctx", 0, 0, tiled=True)
    open_z = open_gate(normed, z_weight)
    core, far = head % 2, head // 2
    quarter = lambda f, c: (2 * f + c)[None]
    core_swap = [(0, 1), (1, 0), (2, 3), (3, 2)]
    far_swap = [(0, 2), (2, 0), (1, 3), (3, 1)]
    gated, first = gate(
        quarter(1 - far, 1 - core), y, open_z, bc, cum, state, out_gain.reshape(-1, LANES), out_weight
    )
    first = lax.ppermute(first, "head", core_swap)
    second = project(quarter(1 - far, core), gated, out_weight, f32)
    second = (second + first.astype(f32)).astype(bf16)
    second, gated = lax.optimization_barrier((second, gated))
    second = lax.ppermute(second, "head", far_swap)
    third = project(quarter(far, 1 - core), gated, out_weight, bf16)
    third = lax.ppermute(third, "head", core_swap)
    lanes = hidden.shape[1] // 4
    residual = lax.dynamic_slice_in_dim(hidden, head * lanes, lanes, 1)
    own = project(quarter(far, core), gated, out_weight, f32, third, residual)
    return (own + second.astype(f32)).astype(bf16)


def solution(mesh):
    return jax.shard_map(
        per_device,
        mesh=mesh,
        in_specs=(
            P("ctx", None), P(), P(None, "head"), P(None, "head"), P(), P(None, "head"),
            P(None, "head"), P(), P("head"), P("head"), P("head"), P("head", None),
        ),
        out_specs=P("ctx", "head"),
        check_vma=False,
    )
```

```python
import functools

import jax
import jax.numpy as jnp
from jax import lax
from jax.experimental import pallas as pl
from jax.experimental.pallas import tpu as pltpu
from jax.sharding import PartitionSpec as P

HEAD_DIM = 64
STATE = 128
HALO = 16
EXTRA = 32
CHUNK = 64
DEPTHS = 5
TILE = 256
LANES = 128
epsilon = 1e-05
f32 = jnp.float32
bf16 = jnp.bfloat16


def mm(a, b, precision=None):
    return jnp.dot(a, b, preferred_element_type=f32, precision=precision)


def iota(shape, dim):
    return lax.broadcasted_iota(jnp.int32, shape, dim)


def silu(v):
    return v * jax.nn.sigmoid(v)


def flip_matrix(n):
    return (iota((n, n), 0) + iota((n, n), 1) == n - 1).astype(bf16)


def hi_lo(v):
    hi = v.astype(bf16)
    return jnp.concatenate([hi, (v - hi.astype(f32)).astype(bf16)], axis=1)


def spread(first, width):
    rows = iota((2 * LANES, width), 0) % LANES
    return (rows == first + iota((2 * LANES, width), 1) // HEAD_DIM).astype(bf16)


def time_of(index, rows):
    return (index % 8) * (rows // 8) + index // 8


def conv_rows(ext_ref, taps, direction, rows, first, count):
    base = (EXTRA - 24 if direction == 0 else EXTRA + rows) + first
    total = None
    for k in range(4):
        at = base + 8 * (k if direction == 0 else 3 - k)
        term = taps[k : k + 1] * ext_ref[at : at + count]
        total = term if total is None else total + term
    return silu(total).astype(bf16)


def cumulate(matrix, v, lanes):
    v = jnp.where(iota(v.shape, 1) < lanes, v, 0.0)
    hi = v.astype(bf16).astype(f32)
    mid = (v - hi).astype(bf16).astype(f32)
    low = v - hi - mid
    packed = hi + pltpu.roll(mid, 32, 1) + pltpu.roll(low, 64, 1)
    out = mm(matrix, packed.astype(bf16))
    return out + pltpu.roll(out, LANES - 32, 1) + pltpu.roll(out, LANES - 64, 1)


def off_chip(x):
    return pltpu.with_memory_space_constraint(x, pltpu.HBM)


def fixed(*shape):
    return pl.BlockSpec(shape, lambda *_: (0,) * len(shape), pipeline_mode=pl.Buffered(1))


def scale_of(v):
    return lax.rsqrt(jnp.mean(v * v, axis=-1, keepdims=True) + epsilon)


def scaled(v, scale, gain_ref, first):
    parts = [
        (v[:, g * LANES : (g + 1) * LANES] * scale) * gain_ref[first + g : first + g + 1]
        for g in range(v.shape[1] // LANES)
    ]
    return jnp.concatenate(parts, axis=1).astype(bf16)


def norm_kernel(
    h_ref, gain_ref, dtw_ref, dtb_ref, lr_ref, xw_ref, bcw_ref,
    x_ref, delta_ref, cum_ref, cumt_ref, wend_ref, dec_ref, xw_kept, bcw_kept,
    raw_ref, dtp_ref, sems,
):
    rows, width = h_ref.shape
    heads = dtb_ref.shape[1]
    copies = [pltpu.make_async_copy(bcw_ref, bcw_kept, sems.at[0])]
    copies.append(pltpu.make_async_copy(xw_ref.at[:, :TILE], xw_kept, sems.at[1]))
    for copy in copies:
        copy.start()

    order = (iota((rows, rows), 1) == time_of(iota((rows, rows), 0), rows)).astype(bf16)
    flip = flip_matrix(TILE)
    blocks = width // TILE
    squares = jnp.zeros((rows, LANES), f32)
    for b in range(blocks):
        cols = slice(b * TILE, (b + 1) * TILE)
        v = mm(order, h_ref[:, cols])
        raw_ref[:, cols] = v.astype(bf16)
        squares = squares + v[:, :LANES] * v[:, :LANES] + v[:, LANES:] * v[:, LANES:]
    mean_sq = jnp.sum(squares, axis=-1, keepdims=True) * (1.0 / width)
    scale = jnp.broadcast_to(lax.rsqrt(mean_sq + epsilon), (rows, LANES))
    for b in range(blocks):
        cols = slice(b * TILE, (b + 1) * TILE)
        mirror = blocks - 1 - b
        x_ref[:rows, cols] = scaled(raw_ref[:, cols].astype(f32), scale, gain_ref, b * 2)
        turned = mm(raw_ref[:, mirror * TILE : (mirror + 1) * TILE], flip)
        x_ref[rows:, cols] = scaled(turned, scale, gain_ref, b * 2)
    dtp_ref[...] = jnp.zeros_like(dtp_ref)
    dtp_ref[0:heads] = dtw_ref[...]
    bias = jnp.concatenate([dtb_ref[...], jnp.zeros((1, LANES - heads), f32)], axis=1)
    rate = jnp.concatenate([lr_ref[...], jnp.zeros((1, LANES - heads), f32)], axis=1)
    dt = lax.dot_general(
        x_ref[...], dtp_ref[...], (((1,), (1,)), ((), ())), preferred_element_type=f32
    )
    dt = dt + bias
    delta = jnp.maximum(dt, 0.0) + jnp.log1p(jnp.exp(-jnp.abs(dt)))
    delta_ref[...] = delta
    log_decay = -delta * jnp.exp(rate)
    later, sooner = time_of(iota((rows, rows), 0), rows), time_of(iota((rows, rows), 1), rows)
    lower = (later >= sooner).astype(bf16)
    upper = (later <= sooner).astype(bf16)
    for d in range(2):
        at = slice(d * rows, (d + 1) * rows)
        cum = cumulate(upper if d else lower, log_decay[at], heads)
        cum_ref[at] = cum
        cumt_ref[d] = jnp.transpose(cum)[: cumt_ref.shape[1]]
        last = cum[0:1] if d else cum[rows - 1 : rows]
        wend_ref[at] = hi_lo(jnp.exp(jnp.minimum(last - cum, 0.0)) * delta[at])
        dec = jnp.where(iota((1, LANES), 1) < heads, jnp.exp(last), 0.0)
        dec_ref[d : d + 1] = dec
    for copy in copies:
        copy.wait()


def norm(hidden, gain, dtw, dtb, lr, xw, bcw):
    rows, width = hidden.shape
    heads = dtb.shape[1]
    return pl.pallas_call(
        norm_kernel,
        grid=(1,),
        in_specs=[
            fixed(rows, width), fixed(width // LANES, LANES), fixed(heads, width),
            fixed(1, heads), fixed(1, heads),
            pl.BlockSpec(memory_space=pltpu.HBM), pl.BlockSpec(memory_space=pltpu.HBM),
        ],
        out_specs=[
            fixed(2 * rows, width), fixed(2 * rows, LANES), fixed(2 * rows, LANES),
            fixed(2, 24, rows), fixed(2 * rows, 2 * LANES), fixed(8, LANES),
            pl.BlockSpec(memory_space=pltpu.VMEM), pl.BlockSpec(memory_space=pltpu.VMEM),
        ],
        out_shape=[
            jax.ShapeDtypeStruct((2 * rows, width), bf16),
            jax.ShapeDtypeStruct((2 * rows, LANES), f32),
            jax.ShapeDtypeStruct((2 * rows, LANES), f32),
            jax.ShapeDtypeStruct((2, 24, rows), f32),
            jax.ShapeDtypeStruct((2 * rows, 2 * LANES), bf16),
            jax.ShapeDtypeStruct((8, LANES), f32),
            jax.ShapeDtypeStruct((width, TILE), bf16),
            jax.ShapeDtypeStruct(bcw.shape, bf16),
        ],
        scratch_shapes=[
            pltpu.VMEM((rows, width), bf16),
            pltpu.VMEM((LANES, width), bf16),
            pltpu.SemaphoreType.DMA((2,)),
        ],
        compiler_params=pltpu.CompilerParams(vmem_limit_bytes=20 << 20),
        cost_estimate=pl.CostEstimate(flops=4 << 30, bytes_accessed=5 << 20, transcendentals=0),
        name="norm",
    )(
        off_chip(hidden), off_chip(gain), off_chip(dtw), off_chip(dtb), off_chip(lr), off_chip(xw), off_chip(bcw)
    )


def entry_kernel(
    x_ref, prev_ref, next_ref, gain_ref, first_ref, bcw_ref, xk_ref, bck_ref, wend_ref, dec_ref, xw_hbm,
    xconv_ref, bc_ref, pay_ref,
    ext_ref, xin_ref, bcin_ref, bt_ref, rim_ref, weighted_ref, acc_ref, reach_ref, xw_ref, sems,
):
    width = x_ref.shape[1]
    rows = x_ref.shape[0] // 2
    n = pl.program_id(0)
    steps = pl.num_programs(0) - 1

    def prelude():
        ext_ref[EXTRA : EXTRA + 2 * rows] = x_ref[...]
        prev = prev_ref[...].astype(f32)
        rim_ref[0, :EXTRA] = x_ref[rows - EXTRA : rows]
        rim_ref[0, EXTRA:] = scaled(prev, scale_of(prev), gain_ref, 0)
        flip = flip_matrix(TILE)
        blocks = width // TILE
        after = next_ref[...]
        after_scale = scale_of(after.astype(f32))
        stacked = jnp.concatenate([after[:, b * TILE : (b + 1) * TILE] for b in range(blocks)], axis=0)
        stacked = mm(stacked, flip)
        rim_ref[1, :EXTRA] = x_ref[rows : rows + EXTRA]
        for b in range(blocks):
            mirror = blocks - 1 - b
            rim_ref[1, EXTRA:, b * TILE : (b + 1) * TILE] = scaled(
                stacked[mirror * HALO : (mirror + 1) * HALO], after_scale, gain_ref, b * 2
            )
        shape = (EXTRA, EXTRA + HALO)
        r, c = iota(shape, 0), iota(shape, 1)
        s = r % 8
        v = r // 8 - 4
        ahead = jnp.where(s == 0, EXTRA + HALO + v, EXTRA + 8 * v + s - 1)
        ahead = ((c == ahead) & (r >= 8)).astype(bf16)
        j = r // 8
        behind = jnp.where(s == 7, EXTRA + j, 8 * j + s + 1)
        behind = ((c == behind) & (r < 24)).astype(bf16)
        ext_ref[:EXTRA] = mm(ahead, rim_ref[0]).astype(bf16)
        ext_ref[EXTRA + 2 * rows :] = mm(behind, rim_ref[1]).astype(bf16)
        bcin_ref[...] = mm(ext_ref[...], bcw_ref[...]).astype(bf16).astype(f32)

    def bc_piece(d, first):
        at = slice(d * rows + first, d * rows + first + CHUNK)
        bc_ref[at] = conv_rows(bcin_ref, bck_ref[...], d, rows, first, CHUNK)

    def x_piece(d, first):
        at = slice(d * rows + first, d * rows + first + CHUNK)
        conv = conv_rows(xin_ref, xk_ref[...], d, rows, first, CHUNK)
        xconv_ref[at] = conv
        weighted_ref[at] = (conv.astype(f32) * reach_ref[at]).astype(bf16)

    def states(d):
        part = mm(bt_ref[d], weighted_ref[d * rows : (d + 1) * rows]).astype(bf16)
        for g in range(TILE // LANES):
            group = d * steps * (TILE // LANES) + (n - 1) * (TILE // LANES) + g
            q, j = group // 5, group % 5
            at = pl.ds(pl.multiple_of(16 * j, 16), 16)
            for i in range(STATE // 16):
                pay_ref[4 * i + q, at] = part[16 * i : 16 * i + 16, g * LANES : (g + 1) * LANES]

    def product(k, weight):
        depth = width // DEPTHS
        at = slice(k * depth, (k + 1) * depth)
        part = mm(ext_ref[:, at], weight(at))
        if k == 0:
            acc_ref[...] = part
        elif k < DEPTHS - 1:
            acc_ref[...] += part
        else:
            xin_ref[...] = (acc_ref[...] + part).astype(bf16).astype(f32)

    def reach():
        reach_ref[...] = mm(wend_ref[...], spread((n - 1) * (TILE // HEAD_DIM), TILE))

    def fetch(tile):
        at = pl.multiple_of(tile * TILE, TILE)
        return pltpu.make_async_copy(
            xw_hbm.at[:, pl.ds(at + TILE, TILE)], xw_ref.at[:, pl.ds(at, TILE)], sems.at[tile]
        )

    pieces = [(d, first) for d in range(2) for first in range(0, rows, CHUNK)]

    @pl.when(n == 0)
    def _():
        for tile in range(xw_ref.shape[1] // TILE):
            fetch(tile).start()
        prelude()
        weight = lambda at: first_ref[at]
        for k in range(DEPTHS - 1):
            product(k, weight)
            for piece in pieces[2 * k : 2 * k + 2]:
                bc_piece(*piece)
        product(DEPTHS - 1, weight)
        for d in range(2):
            at = slice(d * rows, (d + 1) * rows)
            bt_ref[d] = jnp.transpose(bc_ref[at, :STATE].astype(f32)).astype(bf16)
        row = iota((8, LANES), 0)
        for d in range(2):
            dec = jnp.broadcast_to(dec_ref[d : d + 1], (8, LANES))
            hi = dec.astype(bf16).astype(f32)
            tail = jnp.where(row == 0, hi, jnp.where(row == 1, dec - hi, 0.0)).astype(bf16)
            for slot in range(pay_ref.shape[0]):
                if slot % 4 // 2 == d:
                    pay_ref[slot, 80:88] = tail

    @pl.when((n > 0) & (n < steps))
    def _():
        fetch(n - 1).wait()
        column = pl.multiple_of((n - 1) * TILE, TILE)
        weight = lambda at: xw_ref[at, pl.ds(column, TILE)]
        reach()
        for k in range(DEPTHS - 1):
            product(k, weight)
            for piece in pieces[2 * k : 2 * k + 2]:
                x_piece(*piece)
            if k % 2 == 1:
                states(k // 2)
        product(DEPTHS - 1, weight)

    @pl.when(n == steps)
    def _():
        reach()
        for piece in pieces:
            x_piece(*piece)
        for d in range(2):
            states(d)


def entry(x, prev_rows, next_rows, gain, first, bcw, xk, bck, wend, dec, xw, slots):
    width = x.shape[1]
    rows = x.shape[0] // 2
    inner = xw.shape[1]
    steps = inner // TILE
    behind = lambda n: jnp.maximum(n - 1, 0)
    whole = lambda *shape: pl.BlockSpec(shape, lambda n: (0,) * len(shape))
    once = lambda *shape: pl.BlockSpec(
        shape, lambda n: (0,) * len(shape), pipeline_mode=pl.Buffered(1)
    )
    vmem = pl.BlockSpec(memory_space=pltpu.VMEM)
    return pl.pallas_call(
        entry_kernel,
        grid=(steps + 1,),
        in_specs=[
            vmem, vmem, vmem, once(width // LANES, LANES),
            vmem, vmem,
            pl.BlockSpec((4, TILE), lambda n: (0, behind(n))),
            once(4, 2 * STATE), vmem, vmem, pl.BlockSpec(memory_space=pltpu.HBM),
        ],
        out_specs=[
            pl.BlockSpec((2 * rows, TILE), lambda n: (0, behind(n))),
            whole(2 * rows, 2 * STATE), whole(slots, 88, LANES),
        ],
        out_shape=[
            pltpu.HBM((2 * rows, inner), bf16),
            pltpu.HBM((2 * rows, 2 * STATE), bf16),
            pltpu.HBM((slots, 88, LANES), bf16),
        ],
        scratch_shapes=[
            pltpu.VMEM((2 * rows + 2 * EXTRA, width), bf16),
            pltpu.VMEM((2 * rows + 2 * EXTRA, TILE), f32),
            pltpu.VMEM((2 * rows + 2 * EXTRA, TILE), f32),
            pltpu.VMEM((2, STATE, rows), bf16),
            pltpu.VMEM((2, EXTRA + HALO, width), bf16),
            pltpu.VMEM((2 * rows, TILE), bf16),
            pltpu.VMEM((2 * rows + 2 * EXTRA, TILE), f32),
            pltpu.VMEM((2 * rows, TILE), f32),
            pltpu.VMEM((width, inner - TILE), bf16),
            pltpu.SemaphoreType.DMA((inner // TILE - 1,)),
        ],
        compiler_params=pltpu.CompilerParams(
            dimension_semantics=("arbitrary",), vmem_limit_bytes=26 << 20
        ),
        cost_estimate=pl.CostEstimate(
            flops=2 * 544 * width * (inner + 256), bytes_accessed=12 << 20, transcendentals=0
        ),
        name="entry",
    )(x, prev_rows, next_rows, off_chip(gain), first, bcw, off_chip(xk), off_chip(bck), wend, dec, off_chip(xw))


def open_gate_kernel(x_ref, zw_ref, z_ref):
    z = mm(x_ref[...], zw_ref[...]).astype(bf16).astype(f32)
    z_ref[...] = silu(z).astype(bf16)


def open_gate(x, zw):
    height, width = x.shape
    inner = zw.shape[1]
    return pl.pallas_call(
        open_gate_kernel,
        grid=(inner // TILE,),
        in_specs=[fixed(height, width), pl.BlockSpec((width, TILE), lambda n: (0, n))],
        out_specs=pl.BlockSpec((height, TILE), lambda n: (0, n)),
        out_shape=jax.ShapeDtypeStruct((height, inner), bf16),
        compiler_params=pltpu.CompilerParams(
            dimension_semantics=("arbitrary",), vmem_limit_bytes=16 << 20
        ),
        cost_estimate=pl.CostEstimate(
            flops=2 * height * width * inner, bytes_accessed=16 << 20, transcendentals=0
        ),
        name="open_gate",
    )(off_chip(x), off_chip(zw))


def within_kernel(x_ref, bc_ref, cum_ref, cumt_ref, delta_ref, y_ref, gram_ref):
    d, n = pl.program_id(0), pl.program_id(1)
    rows = x_ref.shape[0]
    heads = TILE // HEAD_DIM

    @pl.when(n == 0)
    def _():
        gram = lax.dot_general(
            bc_ref[:, STATE:], bc_ref[:, :STATE], (((1,), (1,)), ((), ())), preferred_element_type=f32
        )
        t, s = time_of(iota((rows, rows), 0), rows), time_of(iota((rows, rows), 1), rows)
        seen = jnp.where(d == 0, t - s, s - t) >= 0
        gram_ref[...] = jnp.where(seen, gram, 0.0)

    weighted = x_ref[...].astype(f32) * mm(hi_lo(delta_ref[...]), spread(n * heads, TILE))
    cum = pltpu.roll(cum_ref[...], (LANES - n * heads) % LANES, 1)
    owner = iota((rows, TILE), 1) // HEAD_DIM
    total = jnp.zeros((rows, TILE), f32)
    for k in range(heads):
        behind = cumt_ref[0, pl.ds(n * heads + k, 1), :]
        decay = jnp.exp(jnp.minimum(cum[:, k : k + 1] - behind, 0.0)) * gram_ref[...]
        total = total + mm(decay.astype(bf16), jnp.where(owner == k, weighted, 0.0).astype(bf16))
    y_ref[...] = total.astype(bf16)


def within(xconv, bc, cum, cumt, delta):
    rows = xconv.shape[0] // 2
    inner = xconv.shape[1]
    return pl.pallas_call(
        within_kernel,
        grid=(2, inner // TILE),
        in_specs=[
            pl.BlockSpec((rows, TILE), lambda d, n: (d, n)),
            pl.BlockSpec((rows, 2 * STATE), lambda d, n: (d, 0)),
            pl.BlockSpec((rows, LANES), lambda d, n: (d, 0)),
            pl.BlockSpec((1, 24, rows), lambda d, n: (d, 0, 0)),
            pl.BlockSpec((rows, LANES), lambda d, n: (d, 0)),
        ],
        out_specs=pl.BlockSpec((rows, TILE), lambda d, n: (d, n)),
        out_shape=pltpu.HBM((2 * rows, inner), bf16),
        scratch_shapes=[pltpu.VMEM((rows, rows), f32)],
        compiler_params=pltpu.CompilerParams(
            dimension_semantics=("arbitrary", "arbitrary"), vmem_limit_bytes=12 << 20
        ),
        cost_estimate=pl.CostEstimate(flops=3 << 30, bytes_accessed=5 << 20, transcendentals=3 << 20),
        name="within",
    )(off_chip(xconv), off_chip(bc), cum, cumt, delta)


def scan_kernel(q_ref, pay_ref, out_ref, carry_ref, dec_ref):
    q = q_ref[0]
    half, turned = q % 2, q // 2
    depth = pay_ref.shape[0]

    @pl.when(pl.program_id(0) == 0)
    def _():
        carry_ref[...] = jnp.zeros_like(carry_ref)

    first = half * (5 * LANES // HEAD_DIM)
    place = iota((LANES, 5 * LANES), 0) == first + iota((LANES, 5 * LANES), 1) // HEAD_DIM
    place = place.astype(bf16)
    tails = pay_ref[:, 80:88].astype(f32).reshape(8 * depth, LANES).astype(bf16)
    dec_ref[...] = mm(tails, place)
    carry = [carry_ref[16 * j : 16 * j + 16] for j in range(5)]
    for i in range(depth):
        at = jnp.where(turned == 1, depth - 1 - i, i)
        decays = dec_ref[pl.ds(pl.multiple_of(8 * at, 8), 8)]
        decay = decays[0:1] + decays[1:2]
        for j in range(5):
            rows = slice(16 * j, 16 * j + 16)
            out_ref[at, rows] = carry[j].astype(bf16)
            carry[j] = carry[j] * decay[:, j * LANES : (j + 1) * LANES] + pay_ref[at, rows].astype(f32)
    for j in range(5):
        carry_ref[16 * j : 16 * j + 16] = carry[j]


def scan(q, pay):
    slots = pay.shape[0]
    depth = 8
    steps = slots // depth
    chunk = lambda i, q: (jnp.where(q[0] // 2 == 1, steps - 1 - i, i), 0, 0)
    return pl.pallas_call(
        scan_kernel,
        grid_spec=pltpu.PrefetchScalarGridSpec(
            num_scalar_prefetch=1,
            grid=(steps,),
            in_specs=[pl.BlockSpec((depth, 88, LANES), chunk)],
            out_specs=pl.BlockSpec((depth, 80, LANES), chunk),
            scratch_shapes=[pltpu.VMEM((80, LANES), f32), pltpu.VMEM((8 * depth, 5 * LANES), f32)],
        ),
        out_shape=jax.ShapeDtypeStruct((slots, 80, LANES), bf16),
        compiler_params=pltpu.CompilerParams(
            dimension_semantics=("arbitrary",), vmem_limit_bytes=6 << 20
        ),
        name="scan",
    )(q, pay)


def weight_fetches(q, w_ref, near_ref, far_ref, sems):
    lanes = near_ref.shape[1]
    near = pl.ds(pl.multiple_of(q * lanes, LANES), lanes)
    far = pl.ds(pl.multiple_of((3 - q) * lanes, LANES), lanes)
    near_copies, far_copies = [], []
    for k in range(near_ref.shape[0] // TILE):
        rows = slice(k * TILE, (k + 1) * TILE)
        near_copies.append(pltpu.make_async_copy(w_ref.at[rows, near], near_ref.at[rows], sems.at[0, k]))
        far_copies.append(pltpu.make_async_copy(w_ref.at[rows, far], far_ref.at[rows], sems.at[1, k]))
    return near_copies, far_copies


def project_into(out_ref, g_ref, copies, near_ref, far_ref, adds):
    inner, lanes = near_ref.shape
    for copy in copies[1]:
        copy.wait()
    behind = mm(g_ref[:, inner:], far_ref[...]).astype(bf16)
    for copy in copies[0]:
        copy.wait()
    ahead = mm(g_ref[:, :inner], near_ref[...])
    flip = flip_matrix(LANES)
    blocks = lanes // LANES
    for b in range(blocks):
        at = slice(b * LANES, (b + 1) * LANES)
        source = slice((blocks - 1 - b) * LANES, (blocks - b) * LANES)
        total = ahead[:, at] + mm(behind[:, source], flip)
        for add in adds:
            total = total + add[:, at].astype(f32)
        out_ref[:, at] = total.astype(out_ref.dtype)


def weight_scratch(inner, lanes):
    return [
        pltpu.VMEM((inner, lanes), bf16),
        pltpu.VMEM((inner, lanes), bf16),
        pltpu.SemaphoreType.DMA((2, inner // TILE)),
    ]


def gate_kernel(
    target_ref, y_ref, z_ref, bc_ref, cum_ref, st_ref, gain_ref, w_ref,
    g_ref, out_ref,
    near_ref, far_ref, sems, held_ref,
):
    q = pl.program_id(0)
    rows, lanes = y_ref.shape
    groups = lanes // LANES
    copies = weight_fetches(target_ref[0], w_ref, near_ref, far_ref, sems)

    @pl.when(q == 0)
    def _():
        for copy in copies[1] + copies[0]:
            copy.start()

    state = jnp.concatenate([st_ref[:, 0, j].reshape(STATE, LANES) for j in range(groups)], axis=1)
    carried = mm(bc_ref[:, STATE:], state)
    reach = mm(hi_lo(jnp.exp(cum_ref[...])), spread((q % 2) * (lanes // HEAD_DIM), lanes))
    same = iota((LANES, LANES), 0) // HEAD_DIM == iota((LANES, LANES), 1) // HEAD_DIM
    same = same.astype(bf16)
    for b in range(groups):
        at = slice(b * LANES, (b + 1) * LANES)
        y = y_ref[:, at].astype(f32) + carried[:, at] * reach[:, at]
        part = y * z_ref[:, at].astype(f32)
        mean_sq = mm((part * part).astype(bf16), same) * (1.0 / HEAD_DIM)
        gain = gain_ref[pl.ds((q % 2) * groups + b, 1), :]
        held_ref[:, at] = (part * lax.rsqrt(mean_sq + epsilon) * gain).astype(bf16)
    order = (iota((rows, rows), 0) == time_of(iota((rows, rows), 1), rows)).astype(bf16)
    g_ref[:, pl.ds(pl.multiple_of(q * lanes, LANES), lanes)] = mm(order, held_ref[...]).astype(bf16)

    @pl.when(q == pl.num_programs(0) - 1)
    def _():
        project_into(out_ref, g_ref, copies, near_ref, far_ref, ())


def gate(target, y, z, bc, cum, state, gain, weight):
    rows = y.shape[0] // 2
    inner = y.shape[1]
    lanes = inner // 2
    groups = lanes // LANES
    columns = weight.shape[1] // 4
    return pl.pallas_call(
        gate_kernel,
        grid_spec=pltpu.PrefetchScalarGridSpec(
            num_scalar_prefetch=1,
            grid=(4,),
            in_specs=[
                pl.BlockSpec((rows, lanes), lambda q, t: (q // 2, q % 2)),
                pl.BlockSpec((rows, lanes), lambda q, t: (q // 2, q % 2)),
                pl.BlockSpec((rows, 2 * STATE), lambda q, t: (q // 2, 0)),
                pl.BlockSpec((rows, LANES), lambda q, t: (q // 2, 0)),
                pl.BlockSpec((8, 1, groups, 16, LANES), lambda q, t: (0, q, 0, 0, 0)),
                fixed(2 * groups, LANES),
                pl.BlockSpec(memory_space=pltpu.HBM),
            ],
            out_specs=[fixed(rows, 2 * inner), fixed(rows, columns)],
            scratch_shapes=weight_scratch(inner, columns) + [pltpu.VMEM((rows, lanes), bf16)],
        ),
        out_shape=[
            jax.ShapeDtypeStruct((rows, 2 * inner), bf16),
            jax.ShapeDtypeStruct((rows, columns), bf16),
        ],
        compiler_params=pltpu.CompilerParams(
            dimension_semantics=("arbitrary",), vmem_limit_bytes=20 << 20
        ),
        name="gate",
    )(target, off_chip(y), z, off_chip(bc), cum, state.reshape(8, 4, groups, 16, LANES), off_chip(gain), off_chip(weight))


def project_kernel(has_add, q_ref, g_ref, w_ref, *rest):
    adds, (out_ref, near_ref, far_ref, sems) = rest[:has_add], rest[has_add:]
    copies = weight_fetches(q_ref[0], w_ref, near_ref, far_ref, sems)
    for copy in copies[1] + copies[0]:
        copy.start()
    project_into(out_ref, g_ref, copies, near_ref, far_ref, adds)


def project(q, gated, weight, dtype, *adds):
    rows = gated.shape[0]
    inner, width = weight.shape
    lanes = width // 4
    vmem = pl.BlockSpec(memory_space=pltpu.VMEM)
    return pl.pallas_call(
        functools.partial(project_kernel, len(adds)),
        in_specs=[pl.BlockSpec(memory_space=pltpu.SMEM), vmem, pl.BlockSpec(memory_space=pltpu.HBM)]
        + [vmem for _ in adds],
        out_specs=vmem,
        out_shape=jax.ShapeDtypeStruct((rows, lanes), dtype),
        scratch_shapes=weight_scratch(inner, lanes),
        compiler_params=pltpu.CompilerParams(vmem_limit_bytes=16 << 20),
        cost_estimate=pl.CostEstimate(
            flops=4 * rows * inner * lanes, bytes_accessed=5 << 20, transcendentals=0
        ),
        name="project",
    )(q, gated, off_chip(weight), *adds)


def per_device(
    hidden, norm_gain, x_weight, z_weight, bc_weight, dt_weight, x_kernel, bc_kernel,
    dt_bias, log_rate, out_gain, out_weight,
):
    blocks = lax.axis_size("ctx")
    place = lax.axis_index("ctx")
    head = lax.axis_index("head")
    prev_rows = lax.ppermute(hidden[-HALO:], "ctx", [(i, i + 1) for i in range(blocks - 1)])
    next_rows = lax.ppermute(hidden[:HALO], "ctx", [(i + 1, i) for i in range(blocks - 1)])
    gain = norm_gain.reshape(-1, LANES)
    normed, delta, cum, cumt, wend, dec, x_kept, bc_kept = norm(
        hidden, gain, dt_weight.T, dt_bias[None], log_rate[None], x_weight, bc_weight
    )
    xconv, bc, pay = entry(
        normed, prev_rows, next_rows, gain, x_kept, bc_kept, x_kernel, bc_kernel, wend, dec,
        x_weight, blocks,
    )
    pay = lax.all_to_all(pay, "ctx", 0, 0, tiled=True)
    y = within(xconv, bc, cum, cumt, delta)
    pay, y = lax.optimization_barrier((pay, y))
    state = scan((place % 4)[None], pay)
    state = lax.all_to_all(state, "ctx", 0, 0, tiled=True)
    open_z = open_gate(normed, z_weight)
    core, far = head % 2, head // 2
    quarter = lambda f, c: (2 * f + c)[None]
    core_swap = [(0, 1), (1, 0), (2, 3), (3, 2)]
    far_swap = [(0, 2), (2, 0), (1, 3), (3, 1)]
    gated, first = gate(
        quarter(1 - far, 1 - core), y, open_z, bc, cum, state, out_gain.reshape(-1, LANES), out_weight
    )
    first = lax.ppermute(first, "head", core_swap)
    second = project(quarter(1 - far, core), gated, out_weight, f32)
    second = (second + first.astype(f32)).astype(bf16)
    second, gated = lax.optimization_barrier((second, gated))
    second = lax.ppermute(second, "head", far_swap)
    third = project(quarter(far, 1 - core), gated, out_weight, bf16)
    third = lax.ppermute(third, "head", core_swap)
    lanes = hidden.shape[1] // 4
    residual = lax.dynamic_slice_in_dim(hidden, head * lanes, lanes, 1)
    own = project(quarter(far, core), gated, out_weight, f32, third, residual)
    return (own + second.astype(f32)).astype(bf16)


def solution(mesh):
    return jax.shard_map(
        per_device,
        mesh=mesh,
        in_specs=(
            P("ctx", None), P(), P(None, "head"), P(None, "head"), P(), P(None, "head"),
            P(None, "head"), P(), P("head"), P("head"), P("head"), P("head", None),
        ),
        out_specs=P("ctx", "head"),
        check_vma=False,
    )
```

```python
import functools

import jax
import jax.numpy as jnp
from jax import lax
from jax.experimental import pallas as pl
from jax.experimental.pallas import tpu as pltpu
from jax.sharding import PartitionSpec as P

HEAD_DIM = 64
STATE = 128
HALO = 16
EXTRA = 32
CHUNK = 64
DEPTHS = 5
TILE = 256
LANES = 128
epsilon = 1e-05
f32 = jnp.float32
bf16 = jnp.bfloat16


def mm(a, b, precision=None):
    return jnp.dot(a, b, preferred_element_type=f32, precision=precision)


def iota(shape, dim):
    return lax.broadcasted_iota(jnp.int32, shape, dim)


def silu(v):
    return v * jax.nn.sigmoid(v)


def flip_matrix(n):
    return (iota((n, n), 0) + iota((n, n), 1) == n - 1).astype(bf16)


def hi_lo(v):
    hi = v.astype(bf16)
    return jnp.concatenate([hi, (v - hi.astype(f32)).astype(bf16)], axis=1)


def spread(first, width):
    rows = iota((2 * LANES, width), 0) % LANES
    return (rows == first + iota((2 * LANES, width), 1) // HEAD_DIM).astype(bf16)


def time_of(index, rows):
    return (index % 8) * (rows // 8) + index // 8


def conv_rows(ext_ref, taps, direction, rows, first, count):
    base = (EXTRA - 24 if direction == 0 else EXTRA + rows) + first
    total = None
    for k in range(4):
        at = base + 8 * (k if direction == 0 else 3 - k)
        term = taps[k : k + 1] * ext_ref[at : at + count]
        total = term if total is None else total + term
    return silu(total).astype(bf16)


def cumulate(matrix, v, lanes):
    v = jnp.where(iota(v.shape, 1) < lanes, v, 0.0)
    hi = v.astype(bf16).astype(f32)
    mid = (v - hi).astype(bf16).astype(f32)
    low = v - hi - mid
    packed = hi + pltpu.roll(mid, 32, 1) + pltpu.roll(low, 64, 1)
    out = mm(matrix, packed.astype(bf16))
    return out + pltpu.roll(out, LANES - 32, 1) + pltpu.roll(out, LANES - 64, 1)


def off_chip(x):
    return pltpu.with_memory_space_constraint(x, pltpu.HBM)


def fixed(*shape):
    return pl.BlockSpec(shape, lambda *_: (0,) * len(shape), pipeline_mode=pl.Buffered(1))


def scale_of(v):
    return lax.rsqrt(jnp.mean(v * v, axis=-1, keepdims=True) + epsilon)


def scaled(v, scale, gain_ref, first):
    parts = [
        (v[:, g * LANES : (g + 1) * LANES] * scale) * gain_ref[first + g : first + g + 1]
        for g in range(v.shape[1] // LANES)
    ]
    return jnp.concatenate(parts, axis=1).astype(bf16)


def norm_kernel(
    h_ref, gain_ref, dtw_ref, dtb_ref, lr_ref, xw_ref, bcw_ref,
    x_ref, delta_ref, cum_ref, cumt_ref, wend_ref, dec_ref, xw_kept, bcw_kept,
    raw_ref, dtp_ref, sems,
):
    rows, width = h_ref.shape
    heads = dtb_ref.shape[1]

    def fetch(k):
        part = pl.ds(pl.multiple_of(k * (width // DEPTHS), TILE), width // DEPTHS)
        return (
            pltpu.make_async_copy(bcw_ref.at[part], bcw_kept.at[part], sems.at[0, k]),
            pltpu.make_async_copy(xw_ref.at[part, :TILE], xw_kept.at[part], sems.at[1, k]),
        )

    def start(k, _):
        for copy in fetch(k):
            copy.start()
        return 0

    lax.fori_loop(0, DEPTHS, start, 0)

    order = (iota((rows, rows), 1) == time_of(iota((rows, rows), 0), rows)).astype(bf16)
    flip = flip_matrix(TILE)
    blocks = width // TILE
    squares = jnp.zeros((rows, LANES), f32)
    for b in range(blocks):
        cols = slice(b * TILE, (b + 1) * TILE)
        v = mm(order, h_ref[:, cols])
        raw_ref[:, cols] = v.astype(bf16)
        squares = squares + v[:, :LANES] * v[:, :LANES] + v[:, LANES:] * v[:, LANES:]
    mean_sq = jnp.sum(squares, axis=-1, keepdims=True) * (1.0 / width)
    scale = jnp.broadcast_to(lax.rsqrt(mean_sq + epsilon), (rows, LANES))
    for b in range(blocks):
        cols = slice(b * TILE, (b + 1) * TILE)
        mirror = blocks - 1 - b
        x_ref[:rows, cols] = scaled(raw_ref[:, cols].astype(f32), scale, gain_ref, b * 2)
        turned = mm(raw_ref[:, mirror * TILE : (mirror + 1) * TILE], flip)
        x_ref[rows:, cols] = scaled(turned, scale, gain_ref, b * 2)
    dtp_ref[...] = jnp.zeros_like(dtp_ref)
    dtp_ref[0:heads] = dtw_ref[...]
    bias = jnp.concatenate([dtb_ref[...], jnp.zeros((1, LANES - heads), f32)], axis=1)
    rate = jnp.concatenate([lr_ref[...], jnp.zeros((1, LANES - heads), f32)], axis=1)
    dt = lax.dot_general(
        x_ref[...], dtp_ref[...], (((1,), (1,)), ((), ())), preferred_element_type=f32
    )
    dt = dt + bias
    delta = jnp.maximum(dt, 0.0) + jnp.log1p(jnp.exp(-jnp.abs(dt)))
    delta_ref[...] = delta
    log_decay = -delta * jnp.exp(rate)
    later, sooner = time_of(iota((rows, rows), 0), rows), time_of(iota((rows, rows), 1), rows)
    lower = (later >= sooner).astype(bf16)
    upper = (later <= sooner).astype(bf16)
    for d in range(2):
        at = slice(d * rows, (d + 1) * rows)
        cum = cumulate(upper if d else lower, log_decay[at], heads)
        cum_ref[at] = cum
        cumt_ref[d] = jnp.transpose(cum)[: cumt_ref.shape[1]]
        last = cum[0:1] if d else cum[rows - 1 : rows]
        wend_ref[at] = hi_lo(jnp.exp(jnp.minimum(last - cum, 0.0)) * delta[at])
        dec = jnp.where(iota((1, LANES), 1) < heads, jnp.exp(last), 0.0)
        dec_ref[d : d + 1] = dec
    for k in range(DEPTHS):
        for copy in fetch(k):
            copy.wait()


def norm(hidden, gain, dtw, dtb, lr, xw, bcw):
    rows, width = hidden.shape
    heads = dtb.shape[1]
    return pl.pallas_call(
        norm_kernel,
        grid=(1,),
        in_specs=[
            fixed(rows, width), fixed(width // LANES, LANES), fixed(heads, width),
            fixed(1, heads), fixed(1, heads),
            pl.BlockSpec(memory_space=pltpu.HBM), pl.BlockSpec(memory_space=pltpu.HBM),
        ],
        out_specs=[
            fixed(2 * rows, width), fixed(2 * rows, LANES), fixed(2 * rows, LANES),
            fixed(2, 24, rows), fixed(2 * rows, 2 * LANES), fixed(8, LANES),
            pl.BlockSpec(memory_space=pltpu.VMEM), pl.BlockSpec(memory_space=pltpu.VMEM),
        ],
        out_shape=[
            jax.ShapeDtypeStruct((2 * rows, width), bf16),
            jax.ShapeDtypeStruct((2 * rows, LANES), f32),
            jax.ShapeDtypeStruct((2 * rows, LANES), f32),
            jax.ShapeDtypeStruct((2, 24, rows), f32),
            jax.ShapeDtypeStruct((2 * rows, 2 * LANES), bf16),
            jax.ShapeDtypeStruct((8, LANES), f32),
            jax.ShapeDtypeStruct((width, TILE), bf16),
            jax.ShapeDtypeStruct(bcw.shape, bf16),
        ],
        scratch_shapes=[
            pltpu.VMEM((rows, width), bf16),
            pltpu.VMEM((LANES, width), bf16),
            pltpu.SemaphoreType.DMA((2, DEPTHS)),
        ],
        compiler_params=pltpu.CompilerParams(vmem_limit_bytes=20 << 20),
        cost_estimate=pl.CostEstimate(flops=4 << 30, bytes_accessed=5 << 20, transcendentals=0),
        name="norm",
    )(
        off_chip(hidden), off_chip(gain), off_chip(dtw), off_chip(dtb), off_chip(lr), off_chip(xw), off_chip(bcw)
    )


def entry_kernel(
    x_ref, prev_ref, next_ref, gain_ref, first_ref, bcw_ref, xk_ref, bck_ref, wend_ref, dec_ref, xw_hbm,
    xconv_ref, bc_ref, pay_ref,
    ext_ref, xin_ref, bcin_ref, bt_ref, rim_ref, weighted_ref, acc_ref, reach_ref, xw_ref, sems,
):
    width = x_ref.shape[1]
    rows = x_ref.shape[0] // 2
    n = pl.program_id(0)
    steps = pl.num_programs(0) - 1

    def prelude():
        ext_ref[EXTRA : EXTRA + 2 * rows] = x_ref[...]
        prev = prev_ref[...].astype(f32)
        rim_ref[0, :EXTRA] = x_ref[rows - EXTRA : rows]
        rim_ref[0, EXTRA:] = scaled(prev, scale_of(prev), gain_ref, 0)
        flip = flip_matrix(TILE)
        blocks = width // TILE
        after = next_ref[...]
        after_scale = scale_of(after.astype(f32))
        stacked = jnp.concatenate([after[:, b * TILE : (b + 1) * TILE] for b in range(blocks)], axis=0)
        stacked = mm(stacked, flip)
        rim_ref[1, :EXTRA] = x_ref[rows : rows + EXTRA]
        for b in range(blocks):
            mirror = blocks - 1 - b
            rim_ref[1, EXTRA:, b * TILE : (b + 1) * TILE] = scaled(
                stacked[mirror * HALO : (mirror + 1) * HALO], after_scale, gain_ref, b * 2
            )
        shape = (EXTRA, EXTRA + HALO)
        r, c = iota(shape, 0), iota(shape, 1)
        s = r % 8
        v = r // 8 - 4
        ahead = jnp.where(s == 0, EXTRA + HALO + v, EXTRA + 8 * v + s - 1)
        ahead = ((c == ahead) & (r >= 8)).astype(bf16)
        j = r // 8
        behind = jnp.where(s == 7, EXTRA + j, 8 * j + s + 1)
        behind = ((c == behind) & (r < 24)).astype(bf16)
        ext_ref[:EXTRA] = mm(ahead, rim_ref[0]).astype(bf16)
        ext_ref[EXTRA + 2 * rows :] = mm(behind, rim_ref[1]).astype(bf16)
        bcin_ref[...] = mm(ext_ref[...], bcw_ref[...]).astype(bf16).astype(f32)

    def bc_piece(d, first):
        at = slice(d * rows + first, d * rows + first + CHUNK)
        bc_ref[at] = conv_rows(bcin_ref, bck_ref[...], d, rows, first, CHUNK)

    def x_piece(d, first):
        at = slice(d * rows + first, d * rows + first + CHUNK)
        conv = conv_rows(xin_ref, xk_ref[...], d, rows, first, CHUNK)
        xconv_ref[at] = conv
        weighted_ref[at] = (conv.astype(f32) * reach_ref[at]).astype(bf16)

    def states(d):
        part = mm(bt_ref[d], weighted_ref[d * rows : (d + 1) * rows]).astype(bf16)
        for g in range(TILE // LANES):
            group = d * steps * (TILE // LANES) + (n - 1) * (TILE // LANES) + g
            q, j = group // 5, group % 5
            at = pl.ds(pl.multiple_of(16 * j, 16), 16)
            for i in range(STATE // 16):
                pay_ref[4 * i + q, at] = part[16 * i : 16 * i + 16, g * LANES : (g + 1) * LANES]

    def product(k, weight):
        depth = width // DEPTHS
        at = slice(k * depth, (k + 1) * depth)
        part = mm(ext_ref[:, at], weight(at))
        if k == 0:
            acc_ref[...] = part
        elif k < DEPTHS - 1:
            acc_ref[...] += part
        else:
            xin_ref[...] = (acc_ref[...] + part).astype(bf16).astype(f32)

    def reach():
        reach_ref[...] = mm(wend_ref[...], spread((n - 1) * (TILE // HEAD_DIM), TILE))

    def fetch(tile):
        at = pl.multiple_of(tile * TILE, TILE)
        return pltpu.make_async_copy(
            xw_hbm.at[:, pl.ds(at + TILE, TILE)], xw_ref.at[:, pl.ds(at, TILE)], sems.at[tile]
        )

    pieces = [(d, first) for d in range(2) for first in range(0, rows, CHUNK)]

    def start(tile, _):
        fetch(tile).start()
        return 0

    @pl.when(n == 0)
    def _():
        lax.fori_loop(0, xw_ref.shape[1] // TILE, start, 0)
        prelude()
        weight = lambda at: first_ref[at]
        for k in range(DEPTHS - 1):
            product(k, weight)
            for piece in pieces[2 * k : 2 * k + 2]:
                bc_piece(*piece)
        product(DEPTHS - 1, weight)
        for d in range(2):
            at = slice(d * rows, (d + 1) * rows)
            bt_ref[d] = jnp.transpose(bc_ref[at, :STATE].astype(f32)).astype(bf16)
        row = iota((8, LANES), 0)
        for d in range(2):
            dec = jnp.broadcast_to(dec_ref[d : d + 1], (8, LANES))
            hi = dec.astype(bf16).astype(f32)
            tail = jnp.where(row == 0, hi, jnp.where(row == 1, dec - hi, 0.0)).astype(bf16)
            for slot in range(pay_ref.shape[0]):
                if slot % 4 // 2 == d:
                    pay_ref[slot, 80:88] = tail

    @pl.when((n > 0) & (n < steps))
    def _():
        fetch(n - 1).wait()
        column = pl.multiple_of((n - 1) * TILE, TILE)
        weight = lambda at: xw_ref[at, pl.ds(column, TILE)]
        reach()
        for k in range(DEPTHS - 1):
            product(k, weight)
            for piece in pieces[2 * k : 2 * k + 2]:
                x_piece(*piece)
            if k % 2 == 1:
                states(k // 2)
        product(DEPTHS - 1, weight)

    @pl.when(n == steps)
    def _():
        reach()
        for piece in pieces:
            x_piece(*piece)
        for d in range(2):
            states(d)


def entry(x, prev_rows, next_rows, gain, first, bcw, xk, bck, wend, dec, xw, slots):
    width = x.shape[1]
    rows = x.shape[0] // 2
    inner = xw.shape[1]
    steps = inner // TILE
    behind = lambda n: jnp.maximum(n - 1, 0)
    whole = lambda *shape: pl.BlockSpec(shape, lambda n: (0,) * len(shape))
    once = lambda *shape: pl.BlockSpec(
        shape, lambda n: (0,) * len(shape), pipeline_mode=pl.Buffered(1)
    )
    vmem = pl.BlockSpec(memory_space=pltpu.VMEM)
    return pl.pallas_call(
        entry_kernel,
        grid=(steps + 1,),
        in_specs=[
            vmem, vmem, vmem, once(width // LANES, LANES),
            vmem, vmem,
            pl.BlockSpec((4, TILE), lambda n: (0, behind(n))),
            once(4, 2 * STATE), vmem, vmem, pl.BlockSpec(memory_space=pltpu.HBM),
        ],
        out_specs=[
            pl.BlockSpec((2 * rows, TILE), lambda n: (0, behind(n))),
            whole(2 * rows, 2 * STATE), whole(slots, 88, LANES),
        ],
        out_shape=[
            pltpu.HBM((2 * rows, inner), bf16),
            pltpu.HBM((2 * rows, 2 * STATE), bf16),
            pltpu.HBM((slots, 88, LANES), bf16),
        ],
        scratch_shapes=[
            pltpu.VMEM((2 * rows + 2 * EXTRA, width), bf16),
            pltpu.VMEM((2 * rows + 2 * EXTRA, TILE), f32),
            pltpu.VMEM((2 * rows + 2 * EXTRA, TILE), f32),
            pltpu.VMEM((2, STATE, rows), bf16),
            pltpu.VMEM((2, EXTRA + HALO, width), bf16),
            pltpu.VMEM((2 * rows, TILE), bf16),
            pltpu.VMEM((2 * rows + 2 * EXTRA, TILE), f32),
            pltpu.VMEM((2 * rows, TILE), f32),
            pltpu.VMEM((width, inner - TILE), bf16),
            pltpu.SemaphoreType.DMA((inner // TILE - 1,)),
        ],
        compiler_params=pltpu.CompilerParams(
            dimension_semantics=("arbitrary",), vmem_limit_bytes=26 << 20
        ),
        cost_estimate=pl.CostEstimate(
            flops=2 * 544 * width * (inner + 256), bytes_accessed=12 << 20, transcendentals=0
        ),
        name="entry",
    )(x, prev_rows, next_rows, off_chip(gain), first, bcw, off_chip(xk), off_chip(bck), wend, dec, off_chip(xw))


def open_gate_kernel(x_ref, zw_ref, z_ref):
    z = mm(x_ref[...], zw_ref[...]).astype(bf16).astype(f32)
    z_ref[...] = silu(z).astype(bf16)


def open_gate(x, zw):
    height, width = x.shape
    inner = zw.shape[1]
    return pl.pallas_call(
        open_gate_kernel,
        grid=(inner // TILE,),
        in_specs=[fixed(height, width), pl.BlockSpec((width, TILE), lambda n: (0, n))],
        out_specs=pl.BlockSpec((height, TILE), lambda n: (0, n)),
        out_shape=jax.ShapeDtypeStruct((height, inner), bf16),
        compiler_params=pltpu.CompilerParams(
            dimension_semantics=("arbitrary",), vmem_limit_bytes=16 << 20
        ),
        cost_estimate=pl.CostEstimate(
            flops=2 * height * width * inner, bytes_accessed=16 << 20, transcendentals=0
        ),
        name="open_gate",
    )(off_chip(x), off_chip(zw))


def within_kernel(x_ref, bc_ref, cum_ref, cumt_ref, delta_ref, y_ref, gram_ref):
    d, n = pl.program_id(0), pl.program_id(1)
    rows = x_ref.shape[0]
    heads = TILE // HEAD_DIM

    @pl.when(n == 0)
    def _():
        gram = lax.dot_general(
            bc_ref[:, STATE:], bc_ref[:, :STATE], (((1,), (1,)), ((), ())), preferred_element_type=f32
        )
        t, s = time_of(iota((rows, rows), 0), rows), time_of(iota((rows, rows), 1), rows)
        seen = jnp.where(d == 0, t - s, s - t) >= 0
        gram_ref[...] = jnp.where(seen, gram, 0.0)

    weighted = x_ref[...].astype(f32) * mm(hi_lo(delta_ref[...]), spread(n * heads, TILE))
    cum = pltpu.roll(cum_ref[...], (LANES - n * heads) % LANES, 1)
    owner = iota((rows, TILE), 1) // HEAD_DIM
    total = jnp.zeros((rows, TILE), f32)
    for k in range(heads):
        behind = cumt_ref[0, pl.ds(n * heads + k, 1), :]
        decay = jnp.exp(jnp.minimum(cum[:, k : k + 1] - behind, 0.0)) * gram_ref[...]
        total = total + mm(decay.astype(bf16), jnp.where(owner == k, weighted, 0.0).astype(bf16))
    y_ref[...] = total.astype(bf16)


def within(xconv, bc, cum, cumt, delta):
    rows = xconv.shape[0] // 2
    inner = xconv.shape[1]
    return pl.pallas_call(
        within_kernel,
        grid=(2, inner // TILE),
        in_specs=[
            pl.BlockSpec((rows, TILE), lambda d, n: (d, n)),
            pl.BlockSpec((rows, 2 * STATE), lambda d, n: (d, 0)),
            pl.BlockSpec((rows, LANES), lambda d, n: (d, 0)),
            pl.BlockSpec((1, 24, rows), lambda d, n: (d, 0, 0)),
            pl.BlockSpec((rows, LANES), lambda d, n: (d, 0)),
        ],
        out_specs=pl.BlockSpec((rows, TILE), lambda d, n: (d, n)),
        out_shape=pltpu.HBM((2 * rows, inner), bf16),
        scratch_shapes=[pltpu.VMEM((rows, rows), f32)],
        compiler_params=pltpu.CompilerParams(
            dimension_semantics=("arbitrary", "arbitrary"), vmem_limit_bytes=12 << 20
        ),
        cost_estimate=pl.CostEstimate(flops=3 << 30, bytes_accessed=5 << 20, transcendentals=3 << 20),
        name="within",
    )(off_chip(xconv), off_chip(bc), cum, cumt, delta)


def scan_kernel(q_ref, pay_ref, out_ref, carry_ref, dec_ref):
    q = q_ref[0]
    half, turned = q % 2, q // 2
    depth = out_ref.shape[0]
    step = pl.program_id(0)
    base = depth * jnp.where(turned == 1, pl.num_programs(0) - 1 - step, step)

    @pl.when(pl.program_id(0) == 0)
    def _():
        carry_ref[...] = jnp.zeros_like(carry_ref)

    first = half * (5 * LANES // HEAD_DIM)
    place = iota((LANES, 5 * LANES), 0) == first + iota((LANES, 5 * LANES), 1) // HEAD_DIM
    place = place.astype(bf16)
    tails = pay_ref[pl.ds(base, depth), 80:88].astype(f32).reshape(8 * depth, LANES).astype(bf16)
    dec_ref[...] = mm(tails, place)
    carry = [carry_ref[16 * j : 16 * j + 16] for j in range(5)]
    for i in range(depth):
        at = jnp.where(turned == 1, depth - 1 - i, i)
        decays = dec_ref[pl.ds(pl.multiple_of(8 * at, 8), 8)]
        decay = decays[0:1] + decays[1:2]
        for j in range(5):
            rows = slice(16 * j, 16 * j + 16)
            out_ref[at, rows] = carry[j].astype(bf16)
            carry[j] = carry[j] * decay[:, j * LANES : (j + 1) * LANES] + pay_ref[base + at, rows].astype(f32)
    for j in range(5):
        carry_ref[16 * j : 16 * j + 16] = carry[j]


def scan(q, pay):
    slots = pay.shape[0]
    depth = 8
    steps = slots // depth
    chunk = lambda i, q: (jnp.where(q[0] // 2 == 1, steps - 1 - i, i), 0, 0)
    return pl.pallas_call(
        scan_kernel,
        grid_spec=pltpu.PrefetchScalarGridSpec(
            num_scalar_prefetch=1,
            grid=(steps,),
            in_specs=[pl.BlockSpec(memory_space=pltpu.VMEM)],
            out_specs=pl.BlockSpec((depth, 80, LANES), chunk),
            scratch_shapes=[pltpu.VMEM((80, LANES), f32), pltpu.VMEM((8 * depth, 5 * LANES), f32)],
        ),
        out_shape=jax.ShapeDtypeStruct((slots, 80, LANES), bf16),
        compiler_params=pltpu.CompilerParams(
            dimension_semantics=("arbitrary",), vmem_limit_bytes=6 << 20
        ),
        name="scan",
    )(q, pay)


def weight_fetches(q, w_ref, near_ref, far_ref, sems):
    lanes = near_ref.shape[1]
    near = pl.ds(pl.multiple_of(q * lanes, LANES), lanes)
    far = pl.ds(pl.multiple_of((3 - q) * lanes, LANES), lanes)
    near_copies, far_copies = [], []
    for k in range(near_ref.shape[0] // TILE):
        rows = slice(k * TILE, (k + 1) * TILE)
        near_copies.append(pltpu.make_async_copy(w_ref.at[rows, near], near_ref.at[rows], sems.at[0, k]))
        far_copies.append(pltpu.make_async_copy(w_ref.at[rows, far], far_ref.at[rows], sems.at[1, k]))
    return near_copies, far_copies


def project_into(out_ref, g_ref, copies, near_ref, far_ref, adds):
    inner, lanes = near_ref.shape
    for copy in copies[1]:
        copy.wait()
    behind = mm(g_ref[:, inner:], far_ref[...]).astype(bf16)
    for copy in copies[0]:
        copy.wait()
    ahead = mm(g_ref[:, :inner], near_ref[...])
    flip = flip_matrix(LANES)
    blocks = lanes // LANES
    for b in range(blocks):
        at = slice(b * LANES, (b + 1) * LANES)
        source = slice((blocks - 1 - b) * LANES, (blocks - b) * LANES)
        total = ahead[:, at] + mm(behind[:, source], flip)
        for add in adds:
            total = total + add[:, at].astype(f32)
        out_ref[:, at] = total.astype(out_ref.dtype)


def weight_scratch(inner, lanes):
    return [
        pltpu.VMEM((inner, lanes), bf16),
        pltpu.VMEM((inner, lanes), bf16),
        pltpu.SemaphoreType.DMA((2, inner // TILE)),
    ]


def gate_kernel(
    target_ref, y_ref, z_ref, bc_ref, cum_ref, st_ref, gain_ref, w_ref,
    g_ref, out_ref,
    near_ref, far_ref, sems, held_ref,
):
    q = pl.program_id(0)
    rows, lanes = y_ref.shape
    groups = lanes // LANES
    copies = weight_fetches(target_ref[0], w_ref, near_ref, far_ref, sems)

    @pl.when(q == 0)
    def _():
        for copy in copies[1] + copies[0]:
            copy.start()

    state = jnp.concatenate([st_ref[:, 0, j].reshape(STATE, LANES) for j in range(groups)], axis=1)
    carried = mm(bc_ref[:, STATE:], state)
    reach = mm(hi_lo(jnp.exp(cum_ref[...])), spread((q % 2) * (lanes // HEAD_DIM), lanes))
    same = iota((LANES, LANES), 0) // HEAD_DIM == iota((LANES, LANES), 1) // HEAD_DIM
    same = same.astype(bf16)
    for b in range(groups):
        at = slice(b * LANES, (b + 1) * LANES)
        y = y_ref[:, at].astype(f32) + carried[:, at] * reach[:, at]
        part = y * z_ref[:, at].astype(f32)
        mean_sq = mm((part * part).astype(bf16), same) * (1.0 / HEAD_DIM)
        gain = gain_ref[pl.ds((q % 2) * groups + b, 1), :]
        held_ref[:, at] = (part * lax.rsqrt(mean_sq + epsilon) * gain).astype(bf16)
    order = (iota((rows, rows), 0) == time_of(iota((rows, rows), 1), rows)).astype(bf16)
    g_ref[:, pl.ds(pl.multiple_of(q * lanes, LANES), lanes)] = mm(order, held_ref[...]).astype(bf16)

    @pl.when(q == pl.num_programs(0) - 1)
    def _():
        project_into(out_ref, g_ref, copies, near_ref, far_ref, ())


def gate(target, y, z, bc, cum, state, gain, weight):
    rows = y.shape[0] // 2
    inner = y.shape[1]
    lanes = inner // 2
    groups = lanes // LANES
    columns = weight.shape[1] // 4
    return pl.pallas_call(
        gate_kernel,
        grid_spec=pltpu.PrefetchScalarGridSpec(
            num_scalar_prefetch=1,
            grid=(4,),
            in_specs=[
                pl.BlockSpec((rows, lanes), lambda q, t: (q // 2, q % 2)),
                pl.BlockSpec((rows, lanes), lambda q, t: (q // 2, q % 2)),
                pl.BlockSpec((rows, 2 * STATE), lambda q, t: (q // 2, 0)),
                pl.BlockSpec((rows, LANES), lambda q, t: (q // 2, 0)),
                pl.BlockSpec((8, 1, groups, 16, LANES), lambda q, t: (0, q, 0, 0, 0)),
                fixed(2 * groups, LANES),
                pl.BlockSpec(memory_space=pltpu.HBM),
            ],
            out_specs=[fixed(rows, 2 * inner), fixed(rows, columns)],
            scratch_shapes=weight_scratch(inner, columns) + [pltpu.VMEM((rows, lanes), bf16)],
        ),
        out_shape=[
            jax.ShapeDtypeStruct((rows, 2 * inner), bf16),
            jax.ShapeDtypeStruct((rows, columns), bf16),
        ],
        compiler_params=pltpu.CompilerParams(
            dimension_semantics=("arbitrary",), vmem_limit_bytes=20 << 20
        ),
        name="gate",
    )(target, off_chip(y), z, off_chip(bc), cum, state.reshape(8, 4, groups, 16, LANES), off_chip(gain), off_chip(weight))


def project_kernel(has_add, q_ref, g_ref, w_ref, *rest):
    adds, (out_ref, near_ref, far_ref, sems) = rest[:has_add], rest[has_add:]
    copies = weight_fetches(q_ref[0], w_ref, near_ref, far_ref, sems)
    for copy in copies[1] + copies[0]:
        copy.start()
    project_into(out_ref, g_ref, copies, near_ref, far_ref, adds)


def project(q, gated, weight, dtype, *adds):
    rows = gated.shape[0]
    inner, width = weight.shape
    lanes = width // 4
    vmem = pl.BlockSpec(memory_space=pltpu.VMEM)
    return pl.pallas_call(
        functools.partial(project_kernel, len(adds)),
        in_specs=[pl.BlockSpec(memory_space=pltpu.SMEM), vmem, pl.BlockSpec(memory_space=pltpu.HBM)]
        + [vmem for _ in adds],
        out_specs=vmem,
        out_shape=jax.ShapeDtypeStruct((rows, lanes), dtype),
        scratch_shapes=weight_scratch(inner, lanes),
        compiler_params=pltpu.CompilerParams(vmem_limit_bytes=16 << 20),
        cost_estimate=pl.CostEstimate(
            flops=4 * rows * inner * lanes, bytes_accessed=5 << 20, transcendentals=0
        ),
        name="project",
    )(q, gated, off_chip(weight), *adds)


def per_device(
    hidden, norm_gain, x_weight, z_weight, bc_weight, dt_weight, x_kernel, bc_kernel,
    dt_bias, log_rate, out_gain, out_weight,
):
    blocks = lax.axis_size("ctx")
    place = lax.axis_index("ctx")
    head = lax.axis_index("head")
    prev_rows = lax.ppermute(hidden[-HALO:], "ctx", [(i, i + 1) for i in range(blocks - 1)])
    next_rows = lax.ppermute(hidden[:HALO], "ctx", [(i + 1, i) for i in range(blocks - 1)])
    gain = norm_gain.reshape(-1, LANES)
    normed, delta, cum, cumt, wend, dec, x_kept, bc_kept = norm(
        hidden, gain, dt_weight.T, dt_bias[None], log_rate[None], x_weight, bc_weight
    )
    xconv, bc, pay = entry(
        normed, prev_rows, next_rows, gain, x_kept, bc_kept, x_kernel, bc_kernel, wend, dec,
        x_weight, blocks,
    )
    pay = lax.all_to_all(pay, "ctx", 0, 0, tiled=True)
    y = within(xconv, bc, cum, cumt, delta)
    pay, y = lax.optimization_barrier((pay, y))
    state = scan((place % 4)[None], pay)
    state = lax.all_to_all(state, "ctx", 0, 0, tiled=True)
    open_z = open_gate(normed, z_weight)
    core, far = head % 2, head // 2
    quarter = lambda f, c: (2 * f + c)[None]
    core_swap = [(0, 1), (1, 0), (2, 3), (3, 2)]
    far_swap = [(0, 2), (2, 0), (1, 3), (3, 1)]
    gated, first = gate(
        quarter(1 - far, 1 - core), y, open_z, bc, cum, state, out_gain.reshape(-1, LANES), out_weight
    )
    first = lax.ppermute(first, "head", core_swap)
    second = project(quarter(1 - far, core), gated, out_weight, f32)
    second = (second + first.astype(f32)).astype(bf16)
    second, gated = lax.optimization_barrier((second, gated))
    second = lax.ppermute(second, "head", far_swap)
    third = project(quarter(far, 1 - core), gated, out_weight, bf16)
    third = lax.ppermute(third, "head", core_swap)
    lanes = hidden.shape[1] // 4
    residual = lax.dynamic_slice_in_dim(hidden, head * lanes, lanes, 1)
    own = project(quarter(far, core), gated, out_weight, f32, third, residual)
    return (own + second.astype(f32)).astype(bf16)


def solution(mesh):
    return jax.shard_map(
        per_device,
        mesh=mesh,
        in_specs=(
            P("ctx", None), P(), P(None, "head"), P(None, "head"), P(), P(None, "head"),
            P(None, "head"), P(), P("head"), P("head"), P("head"), P("head", None),
        ),
        out_specs=P("ctx", "head"),
        check_vma=False,
    )
```

```python
import functools

import jax
import jax.numpy as jnp
from jax import lax
from jax.experimental import pallas as pl
from jax.experimental.pallas import tpu as pltpu
from jax.sharding import PartitionSpec as P

HEAD_DIM = 64
STATE = 128
HALO = 16
EXTRA = 32
CHUNK = 64
DEPTHS = 5
FETCHES = 5
TILE = 256
LANES = 128
epsilon = 1e-05
f32 = jnp.float32
bf16 = jnp.bfloat16


def mm(a, b, precision=None):
    return jnp.dot(a, b, preferred_element_type=f32, precision=precision)


def iota(shape, dim):
    return lax.broadcasted_iota(jnp.int32, shape, dim)


def silu(v):
    return v * jax.nn.sigmoid(v)


def flip_matrix(n):
    return (iota((n, n), 0) + iota((n, n), 1) == n - 1).astype(bf16)


def hi_lo(v):
    hi = v.astype(bf16)
    return jnp.concatenate([hi, (v - hi.astype(f32)).astype(bf16)], axis=1)


def spread(first, width):
    rows = iota((2 * LANES, width), 0) % LANES
    return (rows == first + iota((2 * LANES, width), 1) // HEAD_DIM).astype(bf16)


def time_of(index, rows):
    return (index % 8) * (rows // 8) + index // 8


def conv_rows(ext_ref, taps, direction, rows, first, count):
    base = (EXTRA - 24 if direction == 0 else EXTRA + rows) + first
    total = None
    for k in range(4):
        at = base + 8 * (k if direction == 0 else 3 - k)
        term = taps[k : k + 1] * ext_ref[at : at + count]
        total = term if total is None else total + term
    return silu(total).astype(bf16)


def cumulate(matrix, v, lanes):
    v = jnp.where(iota(v.shape, 1) < lanes, v, 0.0)
    hi = v.astype(bf16).astype(f32)
    mid = (v - hi).astype(bf16).astype(f32)
    low = v - hi - mid
    packed = hi + pltpu.roll(mid, 32, 1) + pltpu.roll(low, 64, 1)
    out = mm(matrix, packed.astype(bf16))
    return out + pltpu.roll(out, LANES - 32, 1) + pltpu.roll(out, LANES - 64, 1)


def off_chip(x):
    return pltpu.with_memory_space_constraint(x, pltpu.HBM)


def fixed(*shape):
    return pl.BlockSpec(shape, lambda *_: (0,) * len(shape), pipeline_mode=pl.Buffered(1))


def scale_of(v):
    return lax.rsqrt(jnp.mean(v * v, axis=-1, keepdims=True) + epsilon)


def scaled(v, scale, gain_ref, first):
    parts = [
        (v[:, g * LANES : (g + 1) * LANES] * scale) * gain_ref[first + g : first + g + 1]
        for g in range(v.shape[1] // LANES)
    ]
    return jnp.concatenate(parts, axis=1).astype(bf16)


def norm_kernel(
    h_ref, gain_ref, dtw_ref, dtb_ref, lr_ref, xw_ref, bcw_ref,
    x_ref, delta_ref, cum_ref, cumt_ref, wend_ref, dec_ref, xw_kept, bcw_kept,
    raw_ref, dtp_ref, sems,
):
    rows, width = h_ref.shape
    heads = dtb_ref.shape[1]

    def fetch(k):
        part = pl.ds(pl.multiple_of(k * (width // FETCHES), TILE), width // FETCHES)
        return (
            pltpu.make_async_copy(bcw_ref.at[part], bcw_kept.at[part], sems.at[0, k]),
            pltpu.make_async_copy(xw_ref.at[part, :TILE], xw_kept.at[part], sems.at[1, k]),
        )

    def start(k, _):
        for copy in fetch(k):
            copy.start()
        return 0

    lax.fori_loop(0, FETCHES, start, 0)

    order = (iota((rows, rows), 1) == time_of(iota((rows, rows), 0), rows)).astype(bf16)
    flip = flip_matrix(TILE)
    blocks = width // TILE
    squares = jnp.zeros((rows, LANES), f32)
    for b in range(blocks):
        cols = slice(b * TILE, (b + 1) * TILE)
        v = mm(order, h_ref[:, cols])
        raw_ref[:, cols] = v.astype(bf16)
        squares = squares + v[:, :LANES] * v[:, :LANES] + v[:, LANES:] * v[:, LANES:]
    mean_sq = jnp.sum(squares, axis=-1, keepdims=True) * (1.0 / width)
    scale = jnp.broadcast_to(lax.rsqrt(mean_sq + epsilon), (rows, LANES))
    for b in range(blocks):
        cols = slice(b * TILE, (b + 1) * TILE)
        mirror = blocks - 1 - b
        x_ref[:rows, cols] = scaled(raw_ref[:, cols].astype(f32), scale, gain_ref, b * 2)
        turned = mm(raw_ref[:, mirror * TILE : (mirror + 1) * TILE], flip)
        x_ref[rows:, cols] = scaled(turned, scale, gain_ref, b * 2)
    dtp_ref[...] = jnp.zeros_like(dtp_ref)
    dtp_ref[0:heads] = dtw_ref[...]
    bias = jnp.concatenate([dtb_ref[...], jnp.zeros((1, LANES - heads), f32)], axis=1)
    rate = jnp.concatenate([lr_ref[...], jnp.zeros((1, LANES - heads), f32)], axis=1)
    dt = lax.dot_general(
        x_ref[...], dtp_ref[...], (((1,), (1,)), ((), ())), preferred_element_type=f32
    )
    dt = dt + bias
    delta = jnp.maximum(dt, 0.0) + jnp.log1p(jnp.exp(-jnp.abs(dt)))
    delta_ref[...] = delta
    log_decay = -delta * jnp.exp(rate)
    later, sooner = time_of(iota((rows, rows), 0), rows), time_of(iota((rows, rows), 1), rows)
    lower = (later >= sooner).astype(bf16)
    upper = (later <= sooner).astype(bf16)
    for d in range(2):
        at = slice(d * rows, (d + 1) * rows)
        cum = cumulate(upper if d else lower, log_decay[at], heads)
        cum_ref[at] = cum
        cumt_ref[d] = jnp.transpose(cum)[: cumt_ref.shape[1]]
        last = cum[0:1] if d else cum[rows - 1 : rows]
        wend_ref[at] = hi_lo(jnp.exp(jnp.minimum(last - cum, 0.0)) * delta[at])
        dec = jnp.where(iota((1, LANES), 1) < heads, jnp.exp(last), 0.0)
        dec_ref[d : d + 1] = dec
    for k in range(FETCHES):
        for copy in fetch(k):
            copy.wait()


def norm(hidden, gain, dtw, dtb, lr, xw, bcw):
    rows, width = hidden.shape
    heads = dtb.shape[1]
    return pl.pallas_call(
        norm_kernel,
        grid=(1,),
        in_specs=[
            fixed(rows, width), fixed(width // LANES, LANES), fixed(heads, width),
            fixed(1, heads), fixed(1, heads),
            pl.BlockSpec(memory_space=pltpu.HBM), pl.BlockSpec(memory_space=pltpu.HBM),
        ],
        out_specs=[
            fixed(2 * rows, width), fixed(2 * rows, LANES), fixed(2 * rows, LANES),
            fixed(2, 24, rows), fixed(2 * rows, 2 * LANES), fixed(8, LANES),
            pl.BlockSpec(memory_space=pltpu.VMEM), pl.BlockSpec(memory_space=pltpu.VMEM),
        ],
        out_shape=[
            jax.ShapeDtypeStruct((2 * rows, width), bf16),
            jax.ShapeDtypeStruct((2 * rows, LANES), f32),
            jax.ShapeDtypeStruct((2 * rows, LANES), f32),
            jax.ShapeDtypeStruct((2, 24, rows), f32),
            jax.ShapeDtypeStruct((2 * rows, 2 * LANES), bf16),
            jax.ShapeDtypeStruct((8, LANES), f32),
            jax.ShapeDtypeStruct((width, TILE), bf16),
            jax.ShapeDtypeStruct(bcw.shape, bf16),
        ],
        scratch_shapes=[
            pltpu.VMEM((rows, width), bf16),
            pltpu.VMEM((LANES, width), bf16),
            pltpu.SemaphoreType.DMA((2, FETCHES)),
        ],
        compiler_params=pltpu.CompilerParams(vmem_limit_bytes=20 << 20),
        cost_estimate=pl.CostEstimate(flops=4 << 30, bytes_accessed=5 << 20, transcendentals=0),
        name="norm",
    )(
        off_chip(hidden), off_chip(gain), off_chip(dtw), off_chip(dtb), off_chip(lr), off_chip(xw), off_chip(bcw)
    )


def entry_kernel(
    x_ref, prev_ref, next_ref, gain_ref, first_ref, bcw_ref, xk_ref, bck_ref, wend_ref, dec_ref, xw_hbm,
    xconv_ref, bc_ref, pay_ref,
    ext_ref, xin_ref, bcin_ref, bt_ref, rim_ref, weighted_ref, acc_ref, reach_ref, xw_ref, sems,
):
    width = x_ref.shape[1]
    rows = x_ref.shape[0] // 2
    n = pl.program_id(0)
    steps = pl.num_programs(0) - 1

    def prelude():
        ext_ref[EXTRA : EXTRA + 2 * rows] = x_ref[...]
        prev = prev_ref[...].astype(f32)
        rim_ref[0, :EXTRA] = x_ref[rows - EXTRA : rows]
        rim_ref[0, EXTRA:] = scaled(prev, scale_of(prev), gain_ref, 0)
        flip = flip_matrix(TILE)
        blocks = width // TILE
        after = next_ref[...]
        after_scale = scale_of(after.astype(f32))
        stacked = jnp.concatenate([after[:, b * TILE : (b + 1) * TILE] for b in range(blocks)], axis=0)
        stacked = mm(stacked, flip)
        rim_ref[1, :EXTRA] = x_ref[rows : rows + EXTRA]
        for b in range(blocks):
            mirror = blocks - 1 - b
            rim_ref[1, EXTRA:, b * TILE : (b + 1) * TILE] = scaled(
                stacked[mirror * HALO : (mirror + 1) * HALO], after_scale, gain_ref, b * 2
            )
        shape = (EXTRA, EXTRA + HALO)
        r, c = iota(shape, 0), iota(shape, 1)
        s = r % 8
        v = r // 8 - 4
        ahead = jnp.where(s == 0, EXTRA + HALO + v, EXTRA + 8 * v + s - 1)
        ahead = ((c == ahead) & (r >= 8)).astype(bf16)
        j = r // 8
        behind = jnp.where(s == 7, EXTRA + j, 8 * j + s + 1)
        behind = ((c == behind) & (r < 24)).astype(bf16)
        ext_ref[:EXTRA] = mm(ahead, rim_ref[0]).astype(bf16)
        ext_ref[EXTRA + 2 * rows :] = mm(behind, rim_ref[1]).astype(bf16)
        bcin_ref[...] = mm(ext_ref[...], bcw_ref[...]).astype(bf16).astype(f32)

    def bc_piece(d, first):
        at = slice(d * rows + first, d * rows + first + CHUNK)
        bc_ref[at] = conv_rows(bcin_ref, bck_ref[...], d, rows, first, CHUNK)

    def x_piece(d, first):
        at = slice(d * rows + first, d * rows + first + CHUNK)
        conv = conv_rows(xin_ref, xk_ref[...], d, rows, first, CHUNK)
        xconv_ref[at] = conv
        weighted_ref[at] = (conv.astype(f32) * reach_ref[at]).astype(bf16)

    def states(d):
        part = mm(bt_ref[d], weighted_ref[d * rows : (d + 1) * rows]).astype(bf16)
        for g in range(TILE // LANES):
            group = d * steps * (TILE // LANES) + (n - 1) * (TILE // LANES) + g
            q, j = group // 5, group % 5
            at = pl.ds(pl.multiple_of(16 * j, 16), 16)
            for i in range(STATE // 16):
                pay_ref[4 * i + q, at] = part[16 * i : 16 * i + 16, g * LANES : (g + 1) * LANES]

    def product(k, weight):
        depth = width // DEPTHS
        at = slice(k * depth, (k + 1) * depth)
        part = mm(ext_ref[:, at], weight(at))
        if k == 0:
            acc_ref[...] = part
        elif k < DEPTHS - 1:
            acc_ref[...] += part
        else:
            xin_ref[...] = (acc_ref[...] + part).astype(bf16).astype(f32)

    def reach():
        reach_ref[...] = mm(wend_ref[...], spread((n - 1) * (TILE // HEAD_DIM), TILE))

    def fetch(tile):
        at = pl.multiple_of(tile * TILE, TILE)
        return pltpu.make_async_copy(
            xw_hbm.at[:, pl.ds(at + TILE, TILE)], xw_ref.at[:, pl.ds(at, TILE)], sems.at[tile]
        )

    pieces = [(d, first) for d in range(2) for first in range(0, rows, CHUNK)]
    share = [k * len(pieces) // (DEPTHS - 1) for k in range(DEPTHS)]

    def start(tile, _):
        fetch(tile).start()
        return 0

    @pl.when(n == 0)
    def _():
        lax.fori_loop(0, xw_ref.shape[1] // TILE, start, 0)
        prelude()
        weight = lambda at: first_ref[at]
        for k in range(DEPTHS - 1):
            product(k, weight)
            for piece in pieces[share[k] : share[k + 1]]:
                bc_piece(*piece)
        product(DEPTHS - 1, weight)
        for d in range(2):
            at = slice(d * rows, (d + 1) * rows)
            bt_ref[d] = jnp.transpose(bc_ref[at, :STATE].astype(f32)).astype(bf16)
        row = iota((8, LANES), 0)
        for d in range(2):
            dec = jnp.broadcast_to(dec_ref[d : d + 1], (8, LANES))
            hi = dec.astype(bf16).astype(f32)
            tail = jnp.where(row == 0, hi, jnp.where(row == 1, dec - hi, 0.0)).astype(bf16)
            for slot in range(pay_ref.shape[0]):
                if slot % 4 // 2 == d:
                    pay_ref[slot, 80:88] = tail

    @pl.when((n > 0) & (n < steps))
    def _():
        fetch(n - 1).wait()
        column = pl.multiple_of((n - 1) * TILE, TILE)
        weight = lambda at: xw_ref[at, pl.ds(column, TILE)]
        reach()
        for k in range(DEPTHS - 1):
            product(k, weight)
            for i in range(share[k], share[k + 1]):
                x_piece(*pieces[i])
                if (i + 1) % (len(pieces) // 2) == 0:
                    states(pieces[i][0])
        product(DEPTHS - 1, weight)

    @pl.when(n == steps)
    def _():
        reach()
        for piece in pieces:
            x_piece(*piece)
        for d in range(2):
            states(d)


def entry(x, prev_rows, next_rows, gain, first, bcw, xk, bck, wend, dec, xw, slots):
    width = x.shape[1]
    rows = x.shape[0] // 2
    inner = xw.shape[1]
    steps = inner // TILE
    behind = lambda n: jnp.maximum(n - 1, 0)
    whole = lambda *shape: pl.BlockSpec(shape, lambda n: (0,) * len(shape))
    once = lambda *shape: pl.BlockSpec(
        shape, lambda n: (0,) * len(shape), pipeline_mode=pl.Buffered(1)
    )
    vmem = pl.BlockSpec(memory_space=pltpu.VMEM)
    return pl.pallas_call(
        entry_kernel,
        grid=(steps + 1,),
        in_specs=[
            vmem, vmem, vmem, once(width // LANES, LANES),
            vmem, vmem,
            pl.BlockSpec((4, TILE), lambda n: (0, behind(n))),
            once(4, 2 * STATE), vmem, vmem, pl.BlockSpec(memory_space=pltpu.HBM),
        ],
        out_specs=[
            pl.BlockSpec((2 * rows, TILE), lambda n: (0, behind(n))),
            whole(2 * rows, 2 * STATE), whole(slots, 88, LANES),
        ],
        out_shape=[
            pltpu.HBM((2 * rows, inner), bf16),
            pltpu.HBM((2 * rows, 2 * STATE), bf16),
            pltpu.HBM((slots, 88, LANES), bf16),
        ],
        scratch_shapes=[
            pltpu.VMEM((2 * rows + 2 * EXTRA, width), bf16),
            pltpu.VMEM((2 * rows + 2 * EXTRA, TILE), f32),
            pltpu.VMEM((2 * rows + 2 * EXTRA, TILE), f32),
            pltpu.VMEM((2, STATE, rows), bf16),
            pltpu.VMEM((2, EXTRA + HALO, width), bf16),
            pltpu.VMEM((2 * rows, TILE), bf16),
            pltpu.VMEM((2 * rows + 2 * EXTRA, TILE), f32),
            pltpu.VMEM((2 * rows, TILE), f32),
            pltpu.VMEM((width, inner - TILE), bf16),
            pltpu.SemaphoreType.DMA((inner // TILE - 1,)),
        ],
        compiler_params=pltpu.CompilerParams(
            dimension_semantics=("arbitrary",), vmem_limit_bytes=26 << 20
        ),
        cost_estimate=pl.CostEstimate(
            flops=2 * 544 * width * (inner + 256), bytes_accessed=12 << 20, transcendentals=0
        ),
        name="entry",
    )(x, prev_rows, next_rows, off_chip(gain), first, bcw, off_chip(xk), off_chip(bck), wend, dec, off_chip(xw))


def open_gate_kernel(x_ref, zw_ref, z_ref):
    z = mm(x_ref[...], zw_ref[...]).astype(bf16).astype(f32)
    z_ref[...] = silu(z).astype(bf16)


def open_gate(x, zw):
    height, width = x.shape
    inner = zw.shape[1]
    return pl.pallas_call(
        open_gate_kernel,
        grid=(inner // TILE,),
        in_specs=[fixed(height, width), pl.BlockSpec((width, TILE), lambda n: (0, n))],
        out_specs=pl.BlockSpec((height, TILE), lambda n: (0, n)),
        out_shape=jax.ShapeDtypeStruct((height, inner), bf16),
        compiler_params=pltpu.CompilerParams(
            dimension_semantics=("arbitrary",), vmem_limit_bytes=16 << 20
        ),
        cost_estimate=pl.CostEstimate(
            flops=2 * height * width * inner, bytes_accessed=16 << 20, transcendentals=0
        ),
        name="open_gate",
    )(off_chip(x), off_chip(zw))


def within_kernel(x_ref, bc_ref, cum_ref, cumt_ref, delta_ref, y_ref, gram_ref):
    d, n = pl.program_id(0), pl.program_id(1)
    rows = x_ref.shape[0]
    heads = TILE // HEAD_DIM

    @pl.when(n == 0)
    def _():
        gram = lax.dot_general(
            bc_ref[:, STATE:], bc_ref[:, :STATE], (((1,), (1,)), ((), ())), preferred_element_type=f32
        )
        t, s = time_of(iota((rows, rows), 0), rows), time_of(iota((rows, rows), 1), rows)
        seen = jnp.where(d == 0, t - s, s - t) >= 0
        gram_ref[...] = jnp.where(seen, gram, 0.0)

    weighted = x_ref[...].astype(f32) * mm(hi_lo(delta_ref[...]), spread(n * heads, TILE))
    cum = pltpu.roll(cum_ref[...], (LANES - n * heads) % LANES, 1)
    owner = iota((rows, TILE), 1) // HEAD_DIM
    total = jnp.zeros((rows, TILE), f32)
    for k in range(heads):
        behind = cumt_ref[0, pl.ds(n * heads + k, 1), :]
        decay = jnp.exp(jnp.minimum(cum[:, k : k + 1] - behind, 0.0)) * gram_ref[...]
        total = total + mm(decay.astype(bf16), jnp.where(owner == k, weighted, 0.0).astype(bf16))
    y_ref[...] = total.astype(bf16)


def within(xconv, bc, cum, cumt, delta):
    rows = xconv.shape[0] // 2
    inner = xconv.shape[1]
    return pl.pallas_call(
        within_kernel,
        grid=(2, inner // TILE),
        in_specs=[
            pl.BlockSpec((rows, TILE), lambda d, n: (d, n)),
            pl.BlockSpec((rows, 2 * STATE), lambda d, n: (d, 0)),
            pl.BlockSpec((rows, LANES), lambda d, n: (d, 0)),
            pl.BlockSpec((1, 24, rows), lambda d, n: (d, 0, 0)),
            pl.BlockSpec((rows, LANES), lambda d, n: (d, 0)),
        ],
        out_specs=pl.BlockSpec((rows, TILE), lambda d, n: (d, n)),
        out_shape=pltpu.HBM((2 * rows, inner), bf16),
        scratch_shapes=[pltpu.VMEM((rows, rows), f32)],
        compiler_params=pltpu.CompilerParams(
            dimension_semantics=("arbitrary", "arbitrary"), vmem_limit_bytes=12 << 20
        ),
        cost_estimate=pl.CostEstimate(flops=3 << 30, bytes_accessed=5 << 20, transcendentals=3 << 20),
        name="within",
    )(off_chip(xconv), off_chip(bc), cum, cumt, delta)


def scan_kernel(q_ref, pay_ref, out_ref, carry_ref, dec_ref):
    q = q_ref[0]
    half, turned = q % 2, q // 2
    depth = out_ref.shape[0]
    step = pl.program_id(0)
    base = depth * jnp.where(turned == 1, pl.num_programs(0) - 1 - step, step)

    @pl.when(pl.program_id(0) == 0)
    def _():
        carry_ref[...] = jnp.zeros_like(carry_ref)

    first = half * (5 * LANES // HEAD_DIM)
    place = iota((LANES, 5 * LANES), 0) == first + iota((LANES, 5 * LANES), 1) // HEAD_DIM
    place = place.astype(bf16)
    tails = pay_ref[pl.ds(base, depth), 80:88].astype(f32).reshape(8 * depth, LANES).astype(bf16)
    dec_ref[...] = mm(tails, place)
    carry = [carry_ref[16 * j : 16 * j + 16] for j in range(5)]
    for i in range(depth):
        at = jnp.where(turned == 1, depth - 1 - i, i)
        decays = dec_ref[pl.ds(pl.multiple_of(8 * at, 8), 8)]
        decay = decays[0:1] + decays[1:2]
        for j in range(5):
            rows = slice(16 * j, 16 * j + 16)
            out_ref[at, rows] = carry[j].astype(bf16)
            carry[j] = carry[j] * decay[:, j * LANES : (j + 1) * LANES] + pay_ref[base + at, rows].astype(f32)
    for j in range(5):
        carry_ref[16 * j : 16 * j + 16] = carry[j]


def scan(q, pay):
    slots = pay.shape[0]
    depth = 8
    steps = slots // depth
    chunk = lambda i, q: (jnp.where(q[0] // 2 == 1, steps - 1 - i, i), 0, 0)
    return pl.pallas_call(
        scan_kernel,
        grid_spec=pltpu.PrefetchScalarGridSpec(
            num_scalar_prefetch=1,
            grid=(steps,),
            in_specs=[pl.BlockSpec(memory_space=pltpu.VMEM)],
            out_specs=pl.BlockSpec((depth, 80, LANES), chunk),
            scratch_shapes=[pltpu.VMEM((80, LANES), f32), pltpu.VMEM((8 * depth, 5 * LANES), f32)],
        ),
        out_shape=jax.ShapeDtypeStruct((slots, 80, LANES), bf16),
        compiler_params=pltpu.CompilerParams(
            dimension_semantics=("arbitrary",), vmem_limit_bytes=6 << 20
        ),
        name="scan",
    )(q, pay)


def weight_fetches(q, w_ref, near_ref, far_ref, sems):
    lanes = near_ref.shape[1]
    near = pl.ds(pl.multiple_of(q * lanes, LANES), lanes)
    far = pl.ds(pl.multiple_of((3 - q) * lanes, LANES), lanes)
    near_copies, far_copies = [], []
    for k in range(near_ref.shape[0] // TILE):
        rows = slice(k * TILE, (k + 1) * TILE)
        near_copies.append(pltpu.make_async_copy(w_ref.at[rows, near], near_ref.at[rows], sems.at[0, k]))
        far_copies.append(pltpu.make_async_copy(w_ref.at[rows, far], far_ref.at[rows], sems.at[1, k]))
    return near_copies, far_copies


def project_into(out_ref, g_ref, copies, near_ref, far_ref, adds):
    inner, lanes = near_ref.shape
    for copy in copies[1]:
        copy.wait()
    behind = mm(g_ref[:, inner:], far_ref[...]).astype(bf16)
    for copy in copies[0]:
        copy.wait()
    ahead = mm(g_ref[:, :inner], near_ref[...])
    flip = flip_matrix(LANES)
    blocks = lanes // LANES
    for b in range(blocks):
        at = slice(b * LANES, (b + 1) * LANES)
        source = slice((blocks - 1 - b) * LANES, (blocks - b) * LANES)
        total = ahead[:, at] + mm(behind[:, source], flip)
        for add in adds:
            total = total + add[:, at].astype(f32)
        out_ref[:, at] = total.astype(out_ref.dtype)


def weight_scratch(inner, lanes):
    return [
        pltpu.VMEM((inner, lanes), bf16),
        pltpu.VMEM((inner, lanes), bf16),
        pltpu.SemaphoreType.DMA((2, inner // TILE)),
    ]


def gate_kernel(
    target_ref, y_ref, z_ref, bc_ref, cum_ref, st_ref, gain_ref, w_ref,
    g_ref, out_ref,
    kept_ref, acc_ref, held_ref, reach_ref, sems,
):
    n = pl.program_id(0)
    rows, lanes = y_ref.shape
    columns = out_ref.shape[1]
    groups = lanes // LANES
    target = target_ref[0]

    def fetch(p):
        quarter = jnp.where(p < 2, target, 3 - target)
        source = pl.ds(pl.multiple_of((p % 2) * lanes, LANES), lanes)
        cols = pl.ds(pl.multiple_of(quarter * columns, LANES), columns)
        to = pl.ds(pl.multiple_of(p * lanes, LANES), lanes)
        return pltpu.make_async_copy(w_ref.at[source, cols], kept_ref.at[to], sems.at[p])

    def start(p, _):
        fetch(p).start()
        return 0

    @pl.when(n == 0)
    def _():
        lax.fori_loop(0, 4, start, 0)

    order = (iota((rows, rows), 0) == time_of(iota((rows, rows), 1), rows)).astype(bf16)
    same = (iota((LANES, LANES), 0) // HEAD_DIM == iota((LANES, LANES), 1) // HEAD_DIM).astype(bf16)

    def gate_group(q, b, carried, reach):
        at = slice(b * LANES, (b + 1) * LANES)
        y = y_ref[:, at].astype(f32) + carried[:, at] * reach[:, at]
        part = y * z_ref[:, at].astype(f32)
        mean_sq = mm((part * part).astype(bf16), same) * (1.0 / HEAD_DIM)
        row = (q % 2) * groups + b
        scaled_part = part * lax.rsqrt(mean_sq + epsilon) * gain_ref[row : row + 1]
        held_ref[:, at] = scaled_part.astype(bf16)

    def settle(q):
        g_ref[:, q * lanes : (q + 1) * lanes] = mm(order, held_ref[...]).astype(bf16)

    def partial(p, first, last):
        at = slice(p * lanes, (p + 1) * lanes)
        part = mm(g_ref[:, at], kept_ref[at, first:last])
        if p % 2:
            acc_ref[p // 2, :, first:last] += part
        else:
            acc_ref[p // 2, :, first:last] = part

    pieces = {0: (0, TILE), 2: (TILE, 2 * TILE), 3: (2 * TILE, columns)}

    def step(k):
        if k < 4 and k % 2 == 0:
            reach_ref[...] = hi_lo(jnp.exp(cum_ref[...]))
        if k > 0:
            fetch(k - 1).wait()
        if k < 4:
            state = [st_ref[:, 0, j].reshape(STATE, LANES) for j in range(groups)]
            carried = mm(bc_ref[:, STATE:], jnp.concatenate(state, axis=1))
            reach = mm(reach_ref[...], spread((k % 2) * (lanes // HEAD_DIM), lanes))
        for b in range(groups):
            if k < 4:
                gate_group(k, b, carried, reach)
            if k > 0 and b in pieces:
                partial(k - 1, *pieces[b])
        if k < 4:
            settle(k)
            return
        flip = flip_matrix(LANES)
        blocks = columns // LANES
        for b in range(blocks):
            at = slice(b * LANES, (b + 1) * LANES)
            source = slice((blocks - 1 - b) * LANES, (blocks - b) * LANES)
            turned = mm(acc_ref[1, :, source].astype(bf16), flip)
            out_ref[:, at] = (acc_ref[0, :, at] + turned).astype(bf16)

    for k in range(5):
        pl.when(n == k)(functools.partial(step, k))


def gate(target, y, z, bc, cum, state, gain, weight):
    rows = y.shape[0] // 2
    inner = y.shape[1]
    lanes = inner // 2
    groups = lanes // LANES
    columns = weight.shape[1] // 4
    part = lambda n: jnp.minimum(n, 3)
    return pl.pallas_call(
        gate_kernel,
        grid_spec=pltpu.PrefetchScalarGridSpec(
            num_scalar_prefetch=1,
            grid=(5,),
            in_specs=[
                pl.BlockSpec((rows, lanes), lambda n, t: (part(n) // 2, part(n) % 2)),
                pl.BlockSpec((rows, lanes), lambda n, t: (part(n) // 2, part(n) % 2)),
                pl.BlockSpec((rows, 2 * STATE), lambda n, t: (part(n) // 2, 0)),
                pl.BlockSpec((rows, LANES), lambda n, t: (part(n) // 2, 0)),
                pl.BlockSpec((8, 1, groups, 16, LANES), lambda n, t: (0, part(n), 0, 0, 0)),
                fixed(2 * groups, LANES),
                pl.BlockSpec(memory_space=pltpu.HBM),
            ],
            out_specs=[fixed(rows, 2 * inner), fixed(rows, columns)],
            scratch_shapes=[
                pltpu.VMEM((2 * inner, columns), bf16),
                pltpu.VMEM((2, rows, columns), f32),
                pltpu.VMEM((rows, lanes), bf16),
                pltpu.VMEM((rows, 2 * LANES), bf16),
                pltpu.SemaphoreType.DMA((4,)),
            ],
        ),
        out_shape=[
            jax.ShapeDtypeStruct((rows, 2 * inner), bf16),
            jax.ShapeDtypeStruct((rows, columns), bf16),
        ],
        compiler_params=pltpu.CompilerParams(
            dimension_semantics=("arbitrary",), vmem_limit_bytes=20 << 20
        ),
        name="gate",
    )(target, off_chip(y), z, off_chip(bc), cum, state.reshape(8, 4, groups, 16, LANES), off_chip(gain), off_chip(weight))


def project_kernel(has_add, q_ref, g_ref, w_ref, *rest):
    adds, (out_ref, near_ref, far_ref, sems) = rest[:has_add], rest[has_add:]
    copies = weight_fetches(q_ref[0], w_ref, near_ref, far_ref, sems)
    for copy in copies[1] + copies[0]:
        copy.start()
    project_into(out_ref, g_ref, copies, near_ref, far_ref, adds)


def project(q, gated, weight, dtype, *adds):
    rows = gated.shape[0]
    inner, width = weight.shape
    lanes = width // 4
    vmem = pl.BlockSpec(memory_space=pltpu.VMEM)
    return pl.pallas_call(
        functools.partial(project_kernel, len(adds)),
        in_specs=[pl.BlockSpec(memory_space=pltpu.SMEM), vmem, pl.BlockSpec(memory_space=pltpu.HBM)]
        + [vmem for _ in adds],
        out_specs=vmem,
        out_shape=jax.ShapeDtypeStruct((rows, lanes), dtype),
        scratch_shapes=weight_scratch(inner, lanes),
        compiler_params=pltpu.CompilerParams(vmem_limit_bytes=16 << 20),
        cost_estimate=pl.CostEstimate(
            flops=4 * rows * inner * lanes, bytes_accessed=5 << 20, transcendentals=0
        ),
        name="project",
    )(q, gated, off_chip(weight), *adds)


def per_device(
    hidden, norm_gain, x_weight, z_weight, bc_weight, dt_weight, x_kernel, bc_kernel,
    dt_bias, log_rate, out_gain, out_weight,
):
    blocks = lax.axis_size("ctx")
    place = lax.axis_index("ctx")
    head = lax.axis_index("head")
    prev_rows = lax.ppermute(hidden[-HALO:], "ctx", [(i, i + 1) for i in range(blocks - 1)])
    next_rows = lax.ppermute(hidden[:HALO], "ctx", [(i + 1, i) for i in range(blocks - 1)])
    gain = norm_gain.reshape(-1, LANES)
    normed, delta, cum, cumt, wend, dec, x_kept, bc_kept = norm(
        hidden, gain, dt_weight.T, dt_bias[None], log_rate[None], x_weight, bc_weight
    )
    xconv, bc, pay = entry(
        normed, prev_rows, next_rows, gain, x_kept, bc_kept, x_kernel, bc_kernel, wend, dec,
        x_weight, blocks,
    )
    pay = lax.all_to_all(pay, "ctx", 0, 0, tiled=True)
    y = within(xconv, bc, cum, cumt, delta)
    pay, y = lax.optimization_barrier((pay, y))
    state = scan((place % 4)[None], pay)
    state = lax.all_to_all(state, "ctx", 0, 0, tiled=True)
    open_z = open_gate(normed, z_weight)
    core, far = head % 2, head // 2
    quarter = lambda f, c: (2 * f + c)[None]
    core_swap = [(0, 1), (1, 0), (2, 3), (3, 2)]
    far_swap = [(0, 2), (2, 0), (1, 3), (3, 1)]
    gated, first = gate(
        quarter(1 - far, 1 - core), y, open_z, bc, cum, state, out_gain.reshape(-1, LANES), out_weight
    )
    first = lax.ppermute(first, "head", core_swap)
    second = project(quarter(1 - far, core), gated, out_weight, f32)
    second = (second + first.astype(f32)).astype(bf16)
    second, gated = lax.optimization_barrier((second, gated))
    second = lax.ppermute(second, "head", far_swap)
    third = project(quarter(far, 1 - core), gated, out_weight, bf16)
    third = lax.ppermute(third, "head", core_swap)
    lanes = hidden.shape[1] // 4
    residual = lax.dynamic_slice_in_dim(hidden, head * lanes, lanes, 1)
    own = project(quarter(far, core), gated, out_weight, f32, third, residual)
    return (own + second.astype(f32)).astype(bf16)


def solution(mesh):
    return jax.shard_map(
        per_device,
        mesh=mesh,
        in_specs=(
            P("ctx", None), P(), P(None, "head"), P(None, "head"), P(), P(None, "head"),
            P(None, "head"), P(), P("head"), P("head"), P("head"), P("head", None),
        ),
        out_specs=P("ctx", "head"),
        check_vma=False,
    )
```

```python
import functools

import jax
import jax.numpy as jnp
from jax import lax
from jax.experimental import pallas as pl
from jax.experimental.pallas import tpu as pltpu
from jax.sharding import PartitionSpec as P

HEAD_DIM = 64
STATE = 128
HALO = 16
EXTRA = 32
CHUNK = 64
DEPTHS = 5
FETCHES = 5
TILE = 256
LANES = 128
epsilon = 1e-05
f32 = jnp.float32
bf16 = jnp.bfloat16


def mm(a, b, precision=None):
    return jnp.dot(a, b, preferred_element_type=f32, precision=precision)


def iota(shape, dim):
    return lax.broadcasted_iota(jnp.int32, shape, dim)


def silu(v):
    return v * jax.nn.sigmoid(v)


def flip_matrix(n):
    return (iota((n, n), 0) + iota((n, n), 1) == n - 1).astype(bf16)


def hi_lo(v):
    hi = v.astype(bf16)
    return jnp.concatenate([hi, (v - hi.astype(f32)).astype(bf16)], axis=1)


def spread(first, width):
    rows = iota((2 * LANES, width), 0) % LANES
    return (rows == first + iota((2 * LANES, width), 1) // HEAD_DIM).astype(bf16)


def time_of(index, rows):
    return (index % 8) * (rows // 8) + index // 8


def conv_rows(ext_ref, taps, direction, rows, first, count):
    base = (EXTRA - 24 if direction == 0 else EXTRA + rows) + first
    total = None
    for k in range(4):
        at = base + 8 * (k if direction == 0 else 3 - k)
        term = taps[k : k + 1] * ext_ref[at : at + count]
        total = term if total is None else total + term
    return silu(total).astype(bf16)


def cumulate(matrix, v, lanes):
    v = jnp.where(iota(v.shape, 1) < lanes, v, 0.0)
    hi = v.astype(bf16).astype(f32)
    mid = (v - hi).astype(bf16).astype(f32)
    low = v - hi - mid
    packed = hi + pltpu.roll(mid, 32, 1) + pltpu.roll(low, 64, 1)
    out = mm(matrix, packed.astype(bf16))
    return out + pltpu.roll(out, LANES - 32, 1) + pltpu.roll(out, LANES - 64, 1)


def off_chip(x):
    return pltpu.with_memory_space_constraint(x, pltpu.HBM)


def fixed(*shape):
    return pl.BlockSpec(shape, lambda *_: (0,) * len(shape), pipeline_mode=pl.Buffered(1))


def scale_of(v):
    return lax.rsqrt(jnp.mean(v * v, axis=-1, keepdims=True) + epsilon)


def scaled(v, scale, gain_ref, first):
    parts = [
        (v[:, g * LANES : (g + 1) * LANES] * scale) * gain_ref[first + g : first + g + 1]
        for g in range(v.shape[1] // LANES)
    ]
    return jnp.concatenate(parts, axis=1).astype(bf16)


def norm_kernel(
    h_ref, gain_ref, dtw_ref, dtb_ref, lr_ref, xw_ref, bcw_ref,
    x_ref, delta_ref, cum_ref, cumt_ref, wend_ref, dec_ref, xw_kept, bcw_kept,
    raw_ref, dtp_ref, sems,
):
    rows, width = h_ref.shape
    heads = dtb_ref.shape[1]

    def fetch(k):
        part = pl.ds(pl.multiple_of(k * (width // FETCHES), TILE), width // FETCHES)
        return (
            pltpu.make_async_copy(bcw_ref.at[part], bcw_kept.at[part], sems.at[0, k]),
            pltpu.make_async_copy(xw_ref.at[part, :TILE], xw_kept.at[part], sems.at[1, k]),
        )

    def start(k, _):
        for copy in fetch(k):
            copy.start()
        return 0

    lax.fori_loop(0, FETCHES, start, 0)

    order = (iota((rows, rows), 1) == time_of(iota((rows, rows), 0), rows)).astype(bf16)
    flip = flip_matrix(TILE)
    blocks = width // TILE
    squares = jnp.zeros((rows, LANES), f32)
    for b in range(blocks):
        cols = slice(b * TILE, (b + 1) * TILE)
        v = mm(order, h_ref[:, cols])
        raw_ref[:, cols] = v.astype(bf16)
        squares = squares + v[:, :LANES] * v[:, :LANES] + v[:, LANES:] * v[:, LANES:]
    mean_sq = jnp.sum(squares, axis=-1, keepdims=True) * (1.0 / width)
    scale = jnp.broadcast_to(lax.rsqrt(mean_sq + epsilon), (rows, LANES))
    for b in range(blocks):
        cols = slice(b * TILE, (b + 1) * TILE)
        mirror = blocks - 1 - b
        x_ref[:rows, cols] = scaled(raw_ref[:, cols].astype(f32), scale, gain_ref, b * 2)
        turned = mm(raw_ref[:, mirror * TILE : (mirror + 1) * TILE], flip)
        x_ref[rows:, cols] = scaled(turned, scale, gain_ref, b * 2)
    dtp_ref[...] = jnp.zeros_like(dtp_ref)
    dtp_ref[0:heads] = dtw_ref[...]
    bias = jnp.concatenate([dtb_ref[...], jnp.zeros((1, LANES - heads), f32)], axis=1)
    rate = jnp.concatenate([lr_ref[...], jnp.zeros((1, LANES - heads), f32)], axis=1)
    dt = lax.dot_general(
        x_ref[...], dtp_ref[...], (((1,), (1,)), ((), ())), preferred_element_type=f32
    )
    dt = dt + bias
    delta = jnp.maximum(dt, 0.0) + jnp.log1p(jnp.exp(-jnp.abs(dt)))
    delta_ref[...] = delta
    log_decay = -delta * jnp.exp(rate)
    later, sooner = time_of(iota((rows, rows), 0), rows), time_of(iota((rows, rows), 1), rows)
    lower = (later >= sooner).astype(bf16)
    upper = (later <= sooner).astype(bf16)
    for d in range(2):
        at = slice(d * rows, (d + 1) * rows)
        cum = cumulate(upper if d else lower, log_decay[at], heads)
        cum_ref[at] = cum
        cumt_ref[d] = jnp.transpose(cum)[: cumt_ref.shape[1]]
        last = cum[0:1] if d else cum[rows - 1 : rows]
        wend_ref[at] = hi_lo(jnp.exp(jnp.minimum(last - cum, 0.0)) * delta[at])
        dec = jnp.where(iota((1, LANES), 1) < heads, jnp.exp(last), 0.0)
        dec_ref[d : d + 1] = dec
    for k in range(FETCHES):
        for copy in fetch(k):
            copy.wait()


def norm(hidden, gain, dtw, dtb, lr, xw, bcw):
    rows, width = hidden.shape
    heads = dtb.shape[1]
    return pl.pallas_call(
        norm_kernel,
        grid=(1,),
        in_specs=[
            fixed(rows, width), fixed(width // LANES, LANES), fixed(heads, width),
            fixed(1, heads), fixed(1, heads),
            pl.BlockSpec(memory_space=pltpu.HBM), pl.BlockSpec(memory_space=pltpu.HBM),
        ],
        out_specs=[
            fixed(2 * rows, width), fixed(2 * rows, LANES), fixed(2 * rows, LANES),
            fixed(2, 24, rows), fixed(2 * rows, 2 * LANES), fixed(8, LANES),
            pl.BlockSpec(memory_space=pltpu.VMEM), pl.BlockSpec(memory_space=pltpu.VMEM),
        ],
        out_shape=[
            jax.ShapeDtypeStruct((2 * rows, width), bf16),
            jax.ShapeDtypeStruct((2 * rows, LANES), f32),
            jax.ShapeDtypeStruct((2 * rows, LANES), f32),
            jax.ShapeDtypeStruct((2, 24, rows), f32),
            jax.ShapeDtypeStruct((2 * rows, 2 * LANES), bf16),
            jax.ShapeDtypeStruct((8, LANES), f32),
            jax.ShapeDtypeStruct((width, TILE), bf16),
            jax.ShapeDtypeStruct(bcw.shape, bf16),
        ],
        scratch_shapes=[
            pltpu.VMEM((rows, width), bf16),
            pltpu.VMEM((LANES, width), bf16),
            pltpu.SemaphoreType.DMA((2, FETCHES)),
        ],
        compiler_params=pltpu.CompilerParams(vmem_limit_bytes=20 << 20),
        cost_estimate=pl.CostEstimate(flops=4 << 30, bytes_accessed=5 << 20, transcendentals=0),
        name="norm",
    )(
        off_chip(hidden), off_chip(gain), off_chip(dtw), off_chip(dtb), off_chip(lr), off_chip(xw), off_chip(bcw)
    )


def entry_kernel(
    x_ref, prev_ref, next_ref, gain_ref, first_ref, bcw_ref, xk_ref, bck_ref, wend_ref, dec_ref, xw_hbm,
    xconv_ref, bc_ref, pay_ref,
    ext_ref, xin_ref, bcin_ref, bt_ref, rim_ref, weighted_ref, acc_ref, reach_ref, xw_ref, sems,
):
    width = x_ref.shape[1]
    rows = x_ref.shape[0] // 2
    n = pl.program_id(0)
    steps = pl.num_programs(0) - 1

    def prelude():
        ext_ref[EXTRA : EXTRA + 2 * rows] = x_ref[...]
        prev = prev_ref[...].astype(f32)
        rim_ref[0, :EXTRA] = x_ref[rows - EXTRA : rows]
        rim_ref[0, EXTRA:] = scaled(prev, scale_of(prev), gain_ref, 0)
        flip = flip_matrix(TILE)
        blocks = width // TILE
        after = next_ref[...]
        after_scale = scale_of(after.astype(f32))
        stacked = jnp.concatenate([after[:, b * TILE : (b + 1) * TILE] for b in range(blocks)], axis=0)
        stacked = mm(stacked, flip)
        rim_ref[1, :EXTRA] = x_ref[rows : rows + EXTRA]
        for b in range(blocks):
            mirror = blocks - 1 - b
            rim_ref[1, EXTRA:, b * TILE : (b + 1) * TILE] = scaled(
                stacked[mirror * HALO : (mirror + 1) * HALO], after_scale, gain_ref, b * 2
            )
        shape = (EXTRA, EXTRA + HALO)
        r, c = iota(shape, 0), iota(shape, 1)
        s = r % 8
        v = r // 8 - 4
        ahead = jnp.where(s == 0, EXTRA + HALO + v, EXTRA + 8 * v + s - 1)
        ahead = ((c == ahead) & (r >= 8)).astype(bf16)
        j = r // 8
        behind = jnp.where(s == 7, EXTRA + j, 8 * j + s + 1)
        behind = ((c == behind) & (r < 24)).astype(bf16)
        ext_ref[:EXTRA] = mm(ahead, rim_ref[0]).astype(bf16)
        ext_ref[EXTRA + 2 * rows :] = mm(behind, rim_ref[1]).astype(bf16)
        bcin_ref[...] = mm(ext_ref[...], bcw_ref[...]).astype(bf16).astype(f32)

    def bc_piece(d, first):
        at = slice(d * rows + first, d * rows + first + CHUNK)
        bc_ref[at] = conv_rows(bcin_ref, bck_ref[...], d, rows, first, CHUNK)

    def x_piece(d, first):
        at = slice(d * rows + first, d * rows + first + CHUNK)
        conv = conv_rows(xin_ref, xk_ref[...], d, rows, first, CHUNK)
        xconv_ref[at] = conv
        weighted_ref[at] = (conv.astype(f32) * reach_ref[at]).astype(bf16)

    def states(d):
        part = mm(bt_ref[d], weighted_ref[d * rows : (d + 1) * rows]).astype(bf16)
        for g in range(TILE // LANES):
            group = d * steps * (TILE // LANES) + (n - 1) * (TILE // LANES) + g
            q, j = group // 5, group % 5
            at = pl.ds(pl.multiple_of(16 * j, 16), 16)
            for i in range(STATE // 16):
                pay_ref[4 * i + q, at] = part[16 * i : 16 * i + 16, g * LANES : (g + 1) * LANES]

    def product(k, weight):
        depth = width // DEPTHS
        at = slice(k * depth, (k + 1) * depth)
        part = mm(ext_ref[:, at], weight(at))
        if k == 0:
            acc_ref[...] = part
        elif k < DEPTHS - 1:
            acc_ref[...] += part
        else:
            xin_ref[...] = (acc_ref[...] + part).astype(bf16).astype(f32)

    def reach():
        reach_ref[...] = mm(wend_ref[...], spread((n - 1) * (TILE // HEAD_DIM), TILE))

    def fetch(tile):
        at = pl.multiple_of(tile * TILE, TILE)
        return pltpu.make_async_copy(
            xw_hbm.at[:, pl.ds(at + TILE, TILE)], xw_ref.at[:, pl.ds(at, TILE)], sems.at[tile]
        )

    pieces = [(d, first) for d in range(2) for first in range(0, rows, CHUNK)]
    share = [k * len(pieces) // (DEPTHS - 1) for k in range(DEPTHS)]

    def start(tile, _):
        fetch(tile).start()
        return 0

    @pl.when(n == 0)
    def _():
        lax.fori_loop(0, xw_ref.shape[1] // TILE, start, 0)
        prelude()
        weight = lambda at: first_ref[at]
        for k in range(DEPTHS - 1):
            product(k, weight)
            for piece in pieces[share[k] : share[k + 1]]:
                bc_piece(*piece)
        product(DEPTHS - 1, weight)
        for d in range(2):
            at = slice(d * rows, (d + 1) * rows)
            bt_ref[d] = jnp.transpose(bc_ref[at, :STATE].astype(f32)).astype(bf16)
        row = iota((8, LANES), 0)
        for d in range(2):
            dec = jnp.broadcast_to(dec_ref[d : d + 1], (8, LANES))
            hi = dec.astype(bf16).astype(f32)
            tail = jnp.where(row == 0, hi, jnp.where(row == 1, dec - hi, 0.0)).astype(bf16)
            for slot in range(pay_ref.shape[0]):
                if slot % 4 // 2 == d:
                    pay_ref[slot, 80:88] = tail

    @pl.when((n > 0) & (n < steps))
    def _():
        fetch(n - 1).wait()
        column = pl.multiple_of((n - 1) * TILE, TILE)
        weight = lambda at: xw_ref[at, pl.ds(column, TILE)]
        reach()
        for k in range(DEPTHS - 1):
            product(k, weight)
            for i in range(share[k], share[k + 1]):
                x_piece(*pieces[i])
                if (i + 1) % (len(pieces) // 2) == 0:
                    states(pieces[i][0])
        product(DEPTHS - 1, weight)

    @pl.when(n == steps)
    def _():
        reach()
        for piece in pieces:
            x_piece(*piece)
        for d in range(2):
            states(d)


def entry(x, prev_rows, next_rows, gain, first, bcw, xk, bck, wend, dec, xw, slots):
    width = x.shape[1]
    rows = x.shape[0] // 2
    inner = xw.shape[1]
    steps = inner // TILE
    behind = lambda n: jnp.maximum(n - 1, 0)
    whole = lambda *shape: pl.BlockSpec(shape, lambda n: (0,) * len(shape))
    once = lambda *shape: pl.BlockSpec(
        shape, lambda n: (0,) * len(shape), pipeline_mode=pl.Buffered(1)
    )
    vmem = pl.BlockSpec(memory_space=pltpu.VMEM)
    return pl.pallas_call(
        entry_kernel,
        grid=(steps + 1,),
        in_specs=[
            vmem, vmem, vmem, once(width // LANES, LANES),
            vmem, vmem,
            pl.BlockSpec((4, TILE), lambda n: (0, behind(n))),
            once(4, 2 * STATE), vmem, vmem, pl.BlockSpec(memory_space=pltpu.HBM),
        ],
        out_specs=[
            pl.BlockSpec((2 * rows, TILE), lambda n: (0, behind(n))),
            whole(2 * rows, 2 * STATE), whole(slots, 88, LANES),
        ],
        out_shape=[
            pltpu.HBM((2 * rows, inner), bf16),
            pltpu.HBM((2 * rows, 2 * STATE), bf16),
            pltpu.HBM((slots, 88, LANES), bf16),
        ],
        scratch_shapes=[
            pltpu.VMEM((2 * rows + 2 * EXTRA, width), bf16),
            pltpu.VMEM((2 * rows + 2 * EXTRA, TILE), f32),
            pltpu.VMEM((2 * rows + 2 * EXTRA, TILE), f32),
            pltpu.VMEM((2, STATE, rows), bf16),
            pltpu.VMEM((2, EXTRA + HALO, width), bf16),
            pltpu.VMEM((2 * rows, TILE), bf16),
            pltpu.VMEM((2 * rows + 2 * EXTRA, TILE), f32),
            pltpu.VMEM((2 * rows, TILE), f32),
            pltpu.VMEM((width, inner - TILE), bf16),
            pltpu.SemaphoreType.DMA((inner // TILE - 1,)),
        ],
        compiler_params=pltpu.CompilerParams(
            dimension_semantics=("arbitrary",), vmem_limit_bytes=26 << 20
        ),
        cost_estimate=pl.CostEstimate(
            flops=2 * 544 * width * (inner + 256), bytes_accessed=12 << 20, transcendentals=0
        ),
        name="entry",
    )(x, prev_rows, next_rows, off_chip(gain), first, bcw, off_chip(xk), off_chip(bck), wend, dec, off_chip(xw))


def open_gate_kernel(x_ref, zw_ref, z_ref):
    z = mm(x_ref[...], zw_ref[...]).astype(bf16).astype(f32)
    z_ref[...] = silu(z).astype(bf16)


def open_gate(x, zw):
    height, width = x.shape
    inner = zw.shape[1]
    return pl.pallas_call(
        open_gate_kernel,
        grid=(inner // TILE,),
        in_specs=[fixed(height, width), pl.BlockSpec((width, TILE), lambda n: (0, n))],
        out_specs=pl.BlockSpec((height, TILE), lambda n: (0, n)),
        out_shape=jax.ShapeDtypeStruct((height, inner), bf16),
        compiler_params=pltpu.CompilerParams(
            dimension_semantics=("arbitrary",), vmem_limit_bytes=16 << 20
        ),
        cost_estimate=pl.CostEstimate(
            flops=2 * height * width * inner, bytes_accessed=16 << 20, transcendentals=0
        ),
        name="open_gate",
    )(off_chip(x), off_chip(zw))


def within_kernel(x_ref, bc_ref, cum_ref, cumt_ref, delta_ref, y_ref, reach_ref, gram_ref, decay_ref, size_ref):
    d, n = pl.program_id(0), pl.program_id(1)
    rows = x_ref.shape[0]
    heads = TILE // HEAD_DIM

    @pl.when(n == 0)
    def _():
        gram = lax.dot_general(
            bc_ref[:, STATE:], bc_ref[:, :STATE], (((1,), (1,)), ((), ())), preferred_element_type=f32
        )
        t, s = time_of(iota((rows, rows), 0), rows), time_of(iota((rows, rows), 1), rows)
        seen = jnp.where(d == 0, t - s, s - t) >= 0
        gram_ref[...] = jnp.where(seen, gram, 0.0)
        decay_ref[...] = hi_lo(jnp.exp(cum_ref[...]))
        size_ref[...] = hi_lo(delta_ref[...])

    place = spread(n * heads, TILE)
    reach_ref[...] = mm(decay_ref[...], place).astype(bf16)
    weighted = x_ref[...].astype(f32) * mm(size_ref[...], place)
    cum = pltpu.roll(cum_ref[...], (LANES - n * heads) % LANES, 1)
    owner = iota((rows, TILE), 1) // HEAD_DIM
    total = jnp.zeros((rows, TILE), f32)
    for k in range(heads):
        behind = cumt_ref[0, pl.ds(n * heads + k, 1), :]
        decay = jnp.exp(jnp.minimum(cum[:, k : k + 1] - behind, 0.0)) * gram_ref[...]
        total = total + mm(decay.astype(bf16), jnp.where(owner == k, weighted, 0.0).astype(bf16))
    y_ref[...] = total.astype(bf16)


def within(xconv, bc, cum, cumt, delta):
    rows = xconv.shape[0] // 2
    inner = xconv.shape[1]
    return pl.pallas_call(
        within_kernel,
        grid=(2, inner // TILE),
        in_specs=[
            pl.BlockSpec((rows, TILE), lambda d, n: (d, n)),
            pl.BlockSpec((rows, 2 * STATE), lambda d, n: (d, 0)),
            pl.BlockSpec((rows, LANES), lambda d, n: (d, 0)),
            pl.BlockSpec((1, 24, rows), lambda d, n: (d, 0, 0)),
            pl.BlockSpec((rows, LANES), lambda d, n: (d, 0)),
        ],
        out_specs=[pl.BlockSpec((rows, TILE), lambda d, n: (d, n))] * 2,
        out_shape=[pltpu.HBM((2 * rows, inner), bf16)] * 2,
        scratch_shapes=[
            pltpu.VMEM((rows, rows), f32),
            pltpu.VMEM((rows, 2 * LANES), bf16),
            pltpu.VMEM((rows, 2 * LANES), bf16),
        ],
        compiler_params=pltpu.CompilerParams(
            dimension_semantics=("arbitrary", "arbitrary"), vmem_limit_bytes=12 << 20
        ),
        cost_estimate=pl.CostEstimate(flops=3 << 30, bytes_accessed=5 << 20, transcendentals=3 << 20),
        name="within",
    )(off_chip(xconv), off_chip(bc), cum, cumt, delta)


def scan_kernel(q_ref, pay_ref, out_ref, carry_ref, dec_ref):
    q = q_ref[0]
    half, turned = q % 2, q // 2
    depth = out_ref.shape[0]
    step = pl.program_id(0)
    base = depth * jnp.where(turned == 1, pl.num_programs(0) - 1 - step, step)

    @pl.when(pl.program_id(0) == 0)
    def _():
        carry_ref[...] = jnp.zeros_like(carry_ref)

    first = half * (5 * LANES // HEAD_DIM)
    place = iota((LANES, 5 * LANES), 0) == first + iota((LANES, 5 * LANES), 1) // HEAD_DIM
    place = place.astype(bf16)
    tails = pay_ref[pl.ds(base, depth), 80:88].astype(f32).reshape(8 * depth, LANES).astype(bf16)
    dec_ref[...] = mm(tails, place)
    carry = [carry_ref[16 * j : 16 * j + 16] for j in range(5)]
    for i in range(depth):
        at = jnp.where(turned == 1, depth - 1 - i, i)
        decays = dec_ref[pl.ds(pl.multiple_of(8 * at, 8), 8)]
        decay = decays[0:1] + decays[1:2]
        for j in range(5):
            rows = slice(16 * j, 16 * j + 16)
            out_ref[at, rows] = carry[j].astype(bf16)
            carry[j] = carry[j] * decay[:, j * LANES : (j + 1) * LANES] + pay_ref[base + at, rows].astype(f32)
    for j in range(5):
        carry_ref[16 * j : 16 * j + 16] = carry[j]


def scan(q, pay):
    slots = pay.shape[0]
    depth = 8
    steps = slots // depth
    chunk = lambda i, q: (jnp.where(q[0] // 2 == 1, steps - 1 - i, i), 0, 0)
    return pl.pallas_call(
        scan_kernel,
        grid_spec=pltpu.PrefetchScalarGridSpec(
            num_scalar_prefetch=1,
            grid=(steps,),
            in_specs=[pl.BlockSpec(memory_space=pltpu.VMEM)],
            out_specs=pl.BlockSpec((depth, 80, LANES), chunk),
            scratch_shapes=[pltpu.VMEM((80, LANES), f32), pltpu.VMEM((8 * depth, 5 * LANES), f32)],
        ),
        out_shape=jax.ShapeDtypeStruct((slots, 80, LANES), bf16),
        compiler_params=pltpu.CompilerParams(
            dimension_semantics=("arbitrary",), vmem_limit_bytes=6 << 20
        ),
        name="scan",
    )(q, pay)


def weight_fetches(q, w_ref, near_ref, far_ref, sems):
    lanes = near_ref.shape[1]
    near = pl.ds(pl.multiple_of(q * lanes, LANES), lanes)
    far = pl.ds(pl.multiple_of((3 - q) * lanes, LANES), lanes)
    near_copies, far_copies = [], []
    for k in range(near_ref.shape[0] // TILE):
        rows = slice(k * TILE, (k + 1) * TILE)
        near_copies.append(pltpu.make_async_copy(w_ref.at[rows, near], near_ref.at[rows], sems.at[0, k]))
        far_copies.append(pltpu.make_async_copy(w_ref.at[rows, far], far_ref.at[rows], sems.at[1, k]))
    return near_copies, far_copies


def project_into(out_ref, g_ref, copies, near_ref, far_ref, adds):
    inner, lanes = near_ref.shape
    for copy in copies[1]:
        copy.wait()
    behind = mm(g_ref[:, inner:], far_ref[...]).astype(bf16)
    for copy in copies[0]:
        copy.wait()
    ahead = mm(g_ref[:, :inner], near_ref[...])
    flip = flip_matrix(LANES)
    blocks = lanes // LANES
    for b in range(blocks):
        at = slice(b * LANES, (b + 1) * LANES)
        source = slice((blocks - 1 - b) * LANES, (blocks - b) * LANES)
        total = ahead[:, at] + mm(behind[:, source], flip)
        for add in adds:
            total = total + add[:, at].astype(f32)
        out_ref[:, at] = total.astype(out_ref.dtype)


def weight_scratch(inner, lanes):
    return [
        pltpu.VMEM((inner, lanes), bf16),
        pltpu.VMEM((inner, lanes), bf16),
        pltpu.SemaphoreType.DMA((2, inner // TILE)),
    ]


def gate_kernel(
    target_ref, y_ref, z_ref, bc_ref, reach_ref, st_ref, gain_ref, w_ref,
    g_ref, out_ref,
    kept_ref, acc_ref, held_ref, sems,
):
    n = pl.program_id(0)
    rows, lanes = y_ref.shape
    columns = out_ref.shape[1]
    groups = lanes // LANES
    target = target_ref[0]

    def fetch(p):
        quarter = jnp.where(p < 2, target, 3 - target)
        source = pl.ds(pl.multiple_of((p % 2) * lanes, LANES), lanes)
        cols = pl.ds(pl.multiple_of(quarter * columns, LANES), columns)
        to = pl.ds(pl.multiple_of(p * lanes, LANES), lanes)
        return pltpu.make_async_copy(w_ref.at[source, cols], kept_ref.at[to], sems.at[p])

    def start(p, _):
        fetch(p).start()
        return 0

    @pl.when(n == 0)
    def _():
        lax.fori_loop(0, 4, start, 0)

    order = (iota((rows, rows), 0) == time_of(iota((rows, rows), 1), rows)).astype(bf16)
    same = (iota((LANES, LANES), 0) // HEAD_DIM == iota((LANES, LANES), 1) // HEAD_DIM).astype(bf16)

    def gate_group(q, b, carried):
        at = slice(b * LANES, (b + 1) * LANES)
        y = y_ref[:, at].astype(f32) + carried[:, at] * reach_ref[:, at].astype(f32)
        part = y * z_ref[:, at].astype(f32)
        mean_sq = mm((part * part).astype(bf16), same) * (1.0 / HEAD_DIM)
        row = (q % 2) * groups + b
        scaled_part = part * lax.rsqrt(mean_sq + epsilon) * gain_ref[row : row + 1]
        held_ref[:, at] = scaled_part.astype(bf16)

    def settle(q):
        g_ref[:, q * lanes : (q + 1) * lanes] = mm(order, held_ref[...]).astype(bf16)

    def partial(p, first, last):
        at = slice(p * lanes, (p + 1) * lanes)
        part = mm(g_ref[:, at], kept_ref[at, first:last])
        if p % 2:
            acc_ref[p // 2, :, first:last] += part
        else:
            acc_ref[p // 2, :, first:last] = part

    pieces = {0: (0, TILE), 2: (TILE, 2 * TILE), 3: (2 * TILE, columns)}

    def step(k):
        if k > 0:
            fetch(k - 1).wait()
        if k < 4:
            state = [st_ref[:, 0, j].reshape(STATE, LANES) for j in range(groups)]
            carried = mm(bc_ref[:, STATE:], jnp.concatenate(state, axis=1))
        for b in range(groups):
            if k < 4:
                gate_group(k, b, carried)
            if k > 0 and b in pieces:
                partial(k - 1, *pieces[b])
        if k < 4:
            settle(k)
            return
        flip = flip_matrix(LANES)
        blocks = columns // LANES
        for b in range(blocks):
            at = slice(b * LANES, (b + 1) * LANES)
            source = slice((blocks - 1 - b) * LANES, (blocks - b) * LANES)
            turned = mm(acc_ref[1, :, source].astype(bf16), flip)
            out_ref[:, at] = (acc_ref[0, :, at] + turned).astype(bf16)

    for k in range(5):
        pl.when(n == k)(functools.partial(step, k))


def gate(target, y, z, bc, reach, state, gain, weight):
    rows = y.shape[0] // 2
    inner = y.shape[1]
    lanes = inner // 2
    groups = lanes // LANES
    columns = weight.shape[1] // 4
    part = lambda n: jnp.minimum(n, 3)
    return pl.pallas_call(
        gate_kernel,
        grid_spec=pltpu.PrefetchScalarGridSpec(
            num_scalar_prefetch=1,
            grid=(5,),
            in_specs=[
                pl.BlockSpec((rows, lanes), lambda n, t: (part(n) // 2, part(n) % 2)),
                pl.BlockSpec((rows, lanes), lambda n, t: (part(n) // 2, part(n) % 2)),
                pl.BlockSpec((rows, 2 * STATE), lambda n, t: (part(n) // 2, 0)),
                pl.BlockSpec((rows, lanes), lambda n, t: (part(n) // 2, part(n) % 2)),
                pl.BlockSpec((8, 1, groups, 16, LANES), lambda n, t: (0, part(n), 0, 0, 0)),
                fixed(2 * groups, LANES),
                pl.BlockSpec(memory_space=pltpu.HBM),
            ],
            out_specs=[fixed(rows, 2 * inner), fixed(rows, columns)],
            scratch_shapes=[
                pltpu.VMEM((2 * inner, columns), bf16),
                pltpu.VMEM((2, rows, columns), f32),
                pltpu.VMEM((rows, lanes), bf16),
                pltpu.SemaphoreType.DMA((4,)),
            ],
        ),
        out_shape=[
            jax.ShapeDtypeStruct((rows, 2 * inner), bf16),
            jax.ShapeDtypeStruct((rows, columns), bf16),
        ],
        compiler_params=pltpu.CompilerParams(
            dimension_semantics=("arbitrary",), vmem_limit_bytes=20 << 20
        ),
        name="gate",
    )(target, off_chip(y), z, off_chip(bc), off_chip(reach), state.reshape(8, 4, groups, 16, LANES), off_chip(gain), off_chip(weight))


def project_kernel(has_add, q_ref, g_ref, w_ref, *rest):
    adds, (out_ref, near_ref, far_ref, sems) = rest[:has_add], rest[has_add:]
    copies = weight_fetches(q_ref[0], w_ref, near_ref, far_ref, sems)
    for copy in copies[1] + copies[0]:
        copy.start()
    project_into(out_ref, g_ref, copies, near_ref, far_ref, adds)


def project(q, gated, weight, dtype, *adds):
    rows = gated.shape[0]
    inner, width = weight.shape
    lanes = width // 4
    vmem = pl.BlockSpec(memory_space=pltpu.VMEM)
    return pl.pallas_call(
        functools.partial(project_kernel, len(adds)),
        in_specs=[pl.BlockSpec(memory_space=pltpu.SMEM), vmem, pl.BlockSpec(memory_space=pltpu.HBM)]
        + [vmem for _ in adds],
        out_specs=vmem,
        out_shape=jax.ShapeDtypeStruct((rows, lanes), dtype),
        scratch_shapes=weight_scratch(inner, lanes),
        compiler_params=pltpu.CompilerParams(vmem_limit_bytes=16 << 20),
        cost_estimate=pl.CostEstimate(
            flops=4 * rows * inner * lanes, bytes_accessed=5 << 20, transcendentals=0
        ),
        name="project",
    )(q, gated, off_chip(weight), *adds)


def per_device(
    hidden, norm_gain, x_weight, z_weight, bc_weight, dt_weight, x_kernel, bc_kernel,
    dt_bias, log_rate, out_gain, out_weight,
):
    blocks = lax.axis_size("ctx")
    place = lax.axis_index("ctx")
    head = lax.axis_index("head")
    prev_rows = lax.ppermute(hidden[-HALO:], "ctx", [(i, i + 1) for i in range(blocks - 1)])
    next_rows = lax.ppermute(hidden[:HALO], "ctx", [(i + 1, i) for i in range(blocks - 1)])
    gain = norm_gain.reshape(-1, LANES)
    normed, delta, cum, cumt, wend, dec, x_kept, bc_kept = norm(
        hidden, gain, dt_weight.T, dt_bias[None], log_rate[None], x_weight, bc_weight
    )
    xconv, bc, pay = entry(
        normed, prev_rows, next_rows, gain, x_kept, bc_kept, x_kernel, bc_kernel, wend, dec,
        x_weight, blocks,
    )
    pay = lax.all_to_all(pay, "ctx", 0, 0, tiled=True)
    y, reach = within(xconv, bc, cum, cumt, delta)
    pay, y = lax.optimization_barrier((pay, y))
    state = scan((place % 4)[None], pay)
    state = lax.all_to_all(state, "ctx", 0, 0, tiled=True)
    open_z = open_gate(normed, z_weight)
    core, far = head % 2, head // 2
    quarter = lambda f, c: (2 * f + c)[None]
    core_swap = [(0, 1), (1, 0), (2, 3), (3, 2)]
    far_swap = [(0, 2), (2, 0), (1, 3), (3, 1)]
    gated, first = gate(
        quarter(1 - far, 1 - core), y, open_z, bc, reach, state, out_gain.reshape(-1, LANES), out_weight
    )
    first = lax.ppermute(first, "head", core_swap)
    second = project(quarter(1 - far, core), gated, out_weight, f32)
    second = (second + first.astype(f32)).astype(bf16)
    second, gated = lax.optimization_barrier((second, gated))
    second = lax.ppermute(second, "head", far_swap)
    third = project(quarter(far, 1 - core), gated, out_weight, bf16)
    third = lax.ppermute(third, "head", core_swap)
    lanes = hidden.shape[1] // 4
    residual = lax.dynamic_slice_in_dim(hidden, head * lanes, lanes, 1)
    own = project(quarter(far, core), gated, out_weight, f32, third, residual)
    return (own + second.astype(f32)).astype(bf16)


def solution(mesh):
    return jax.shard_map(
        per_device,
        mesh=mesh,
        in_specs=(
            P("ctx", None), P(), P(None, "head"), P(None, "head"), P(), P(None, "head"),
            P(None, "head"), P(), P("head"), P("head"), P("head"), P("head", None),
        ),
        out_specs=P("ctx", "head"),
        check_vma=False,
    )
```

```python
import functools

import jax
import jax.numpy as jnp
from jax import lax
from jax.experimental import pallas as pl
from jax.experimental.pallas import tpu as pltpu
from jax.sharding import PartitionSpec as P

HEAD_DIM = 64
STATE = 128
HALO = 16
EXTRA = 32
CHUNK = 64
DEPTHS = 5
FETCHES = 5
TILE = 256
LANES = 128
epsilon = 1e-05
f32 = jnp.float32
bf16 = jnp.bfloat16


def mm(a, b, precision=None):
    return jnp.dot(a, b, preferred_element_type=f32, precision=precision)


def iota(shape, dim):
    return lax.broadcasted_iota(jnp.int32, shape, dim)


def silu(v):
    return v * jax.nn.sigmoid(v)


def flip_matrix(n):
    return (iota((n, n), 0) + iota((n, n), 1) == n - 1).astype(bf16)


def hi_lo(v):
    hi = v.astype(bf16)
    return jnp.concatenate([hi, (v - hi.astype(f32)).astype(bf16)], axis=1)


def spread(first, width):
    rows = iota((2 * LANES, width), 0) % LANES
    return (rows == first + iota((2 * LANES, width), 1) // HEAD_DIM).astype(bf16)


def time_of(index, rows):
    return (index % 8) * (rows // 8) + index // 8


def conv_rows(ext_ref, taps, direction, rows, first, count):
    base = (EXTRA - 24 if direction == 0 else EXTRA + rows) + first
    total = None
    for k in range(4):
        at = base + 8 * (k if direction == 0 else 3 - k)
        term = taps[k : k + 1] * ext_ref[at : at + count]
        total = term if total is None else total + term
    return silu(total).astype(bf16)


def cumulate(matrix, v, lanes):
    v = jnp.where(iota(v.shape, 1) < lanes, v, 0.0)
    hi = v.astype(bf16).astype(f32)
    mid = (v - hi).astype(bf16).astype(f32)
    low = v - hi - mid
    packed = hi + pltpu.roll(mid, 32, 1) + pltpu.roll(low, 64, 1)
    out = mm(matrix, packed.astype(bf16))
    return out + pltpu.roll(out, LANES - 32, 1) + pltpu.roll(out, LANES - 64, 1)


def off_chip(x):
    return pltpu.with_memory_space_constraint(x, pltpu.HBM)


def fixed(*shape):
    return pl.BlockSpec(shape, lambda *_: (0,) * len(shape), pipeline_mode=pl.Buffered(1))


def scale_of(v):
    return lax.rsqrt(jnp.mean(v * v, axis=-1, keepdims=True) + epsilon)


def scaled(v, scale, gain_ref, first):
    parts = [
        (v[:, g * LANES : (g + 1) * LANES] * scale) * gain_ref[first + g : first + g + 1]
        for g in range(v.shape[1] // LANES)
    ]
    return jnp.concatenate(parts, axis=1).astype(bf16)


def norm_kernel(
    h_ref, gain_ref, dtw_ref, dtb_ref, lr_ref, xw_ref, bcw_ref,
    x_ref, delta_ref, cum_ref, cumt_ref, wend_ref, dec_ref, xw_kept, bcw_kept,
    raw_ref, dtp_ref, sems,
):
    rows, width = h_ref.shape
    heads = dtb_ref.shape[1]

    def fetch(k):
        part = pl.ds(pl.multiple_of(k * (width // FETCHES), TILE), width // FETCHES)
        return (
            pltpu.make_async_copy(bcw_ref.at[part], bcw_kept.at[part], sems.at[0, k]),
            pltpu.make_async_copy(xw_ref.at[part, :TILE], xw_kept.at[part], sems.at[1, k]),
        )

    def start(k, _):
        for copy in fetch(k):
            copy.start()
        return 0

    lax.fori_loop(0, FETCHES, start, 0)

    order = (iota((rows, rows), 1) == time_of(iota((rows, rows), 0), rows)).astype(bf16)
    flip = flip_matrix(TILE)
    blocks = width // TILE
    squares = jnp.zeros((rows, LANES), f32)
    for b in range(blocks):
        cols = slice(b * TILE, (b + 1) * TILE)
        v = mm(order, h_ref[:, cols])
        raw_ref[:, cols] = v.astype(bf16)
        squares = squares + v[:, :LANES] * v[:, :LANES] + v[:, LANES:] * v[:, LANES:]
    mean_sq = jnp.sum(squares, axis=-1, keepdims=True) * (1.0 / width)
    scale = jnp.broadcast_to(lax.rsqrt(mean_sq + epsilon), (rows, LANES))
    for b in range(blocks):
        cols = slice(b * TILE, (b + 1) * TILE)
        mirror = blocks - 1 - b
        x_ref[:rows, cols] = scaled(raw_ref[:, cols].astype(f32), scale, gain_ref, b * 2)
        turned = mm(raw_ref[:, mirror * TILE : (mirror + 1) * TILE], flip)
        x_ref[rows:, cols] = scaled(turned, scale, gain_ref, b * 2)
    dtp_ref[...] = jnp.zeros_like(dtp_ref)
    dtp_ref[0:heads] = dtw_ref[...]
    bias = jnp.concatenate([dtb_ref[...], jnp.zeros((1, LANES - heads), f32)], axis=1)
    rate = jnp.concatenate([lr_ref[...], jnp.zeros((1, LANES - heads), f32)], axis=1)
    dt = lax.dot_general(
        x_ref[...], dtp_ref[...], (((1,), (1,)), ((), ())), preferred_element_type=f32
    )
    dt = dt + bias
    delta = jnp.maximum(dt, 0.0) + jnp.log1p(jnp.exp(-jnp.abs(dt)))
    delta_ref[...] = delta
    log_decay = -delta * jnp.exp(rate)
    later, sooner = time_of(iota((rows, rows), 0), rows), time_of(iota((rows, rows), 1), rows)
    lower = (later >= sooner).astype(bf16)
    upper = (later <= sooner).astype(bf16)
    for d in range(2):
        at = slice(d * rows, (d + 1) * rows)
        cum = cumulate(upper if d else lower, log_decay[at], heads)
        cum_ref[at] = cum
        cumt_ref[d] = jnp.transpose(cum)[: cumt_ref.shape[1]]
        last = cum[0:1] if d else cum[rows - 1 : rows]
        wend_ref[at] = hi_lo(jnp.exp(jnp.minimum(last - cum, 0.0)) * delta[at])
        dec = jnp.where(iota((1, LANES), 1) < heads, jnp.exp(last), 0.0)
        dec_ref[d : d + 1] = dec
    for k in range(FETCHES):
        for copy in fetch(k):
            copy.wait()


def norm(hidden, gain, dtw, dtb, lr, xw, bcw):
    rows, width = hidden.shape
    heads = dtb.shape[1]
    return pl.pallas_call(
        norm_kernel,
        grid=(1,),
        in_specs=[
            fixed(rows, width), fixed(width // LANES, LANES), fixed(heads, width),
            fixed(1, heads), fixed(1, heads),
            pl.BlockSpec(memory_space=pltpu.HBM), pl.BlockSpec(memory_space=pltpu.HBM),
        ],
        out_specs=[
            fixed(2 * rows, width), fixed(2 * rows, LANES), fixed(2 * rows, LANES),
            fixed(2, 24, rows), fixed(2 * rows, 2 * LANES), fixed(8, LANES),
            pl.BlockSpec(memory_space=pltpu.VMEM), pl.BlockSpec(memory_space=pltpu.VMEM),
        ],
        out_shape=[
            jax.ShapeDtypeStruct((2 * rows, width), bf16),
            jax.ShapeDtypeStruct((2 * rows, LANES), f32),
            jax.ShapeDtypeStruct((2 * rows, LANES), f32),
            jax.ShapeDtypeStruct((2, 24, rows), f32),
            jax.ShapeDtypeStruct((2 * rows, 2 * LANES), bf16),
            jax.ShapeDtypeStruct((8, LANES), f32),
            jax.ShapeDtypeStruct((width, TILE), bf16),
            jax.ShapeDtypeStruct(bcw.shape, bf16),
        ],
        scratch_shapes=[
            pltpu.VMEM((rows, width), bf16),
            pltpu.VMEM((LANES, width), bf16),
            pltpu.SemaphoreType.DMA((2, FETCHES)),
        ],
        compiler_params=pltpu.CompilerParams(vmem_limit_bytes=20 << 20),
        cost_estimate=pl.CostEstimate(flops=4 << 30, bytes_accessed=5 << 20, transcendentals=0),
        name="norm",
    )(
        off_chip(hidden), off_chip(gain), off_chip(dtw), off_chip(dtb), off_chip(lr), off_chip(xw), off_chip(bcw)
    )


def entry_kernel(
    x_ref, prev_ref, next_ref, gain_ref, first_ref, bcw_ref, xk_ref, bck_ref, wend_ref, dec_ref, xw_hbm,
    xconv_ref, bc_ref, pay_ref,
    ext_ref, xin_ref, bcin_ref, bt_ref, rim_ref, weighted_ref, acc_ref, reach_ref, xw_ref, sems,
):
    width = x_ref.shape[1]
    rows = x_ref.shape[0] // 2
    n = pl.program_id(0)
    steps = pl.num_programs(0) - 1

    def prelude():
        ext_ref[EXTRA : EXTRA + 2 * rows] = x_ref[...]
        prev = prev_ref[...].astype(f32)
        rim_ref[0, :EXTRA] = x_ref[rows - EXTRA : rows]
        rim_ref[0, EXTRA:] = scaled(prev, scale_of(prev), gain_ref, 0)
        flip = flip_matrix(TILE)
        blocks = width // TILE
        after = next_ref[...]
        after_scale = scale_of(after.astype(f32))
        stacked = jnp.concatenate([after[:, b * TILE : (b + 1) * TILE] for b in range(blocks)], axis=0)
        stacked = mm(stacked, flip)
        rim_ref[1, :EXTRA] = x_ref[rows : rows + EXTRA]
        for b in range(blocks):
            mirror = blocks - 1 - b
            rim_ref[1, EXTRA:, b * TILE : (b + 1) * TILE] = scaled(
                stacked[mirror * HALO : (mirror + 1) * HALO], after_scale, gain_ref, b * 2
            )
        shape = (EXTRA, EXTRA + HALO)
        r, c = iota(shape, 0), iota(shape, 1)
        s = r % 8
        v = r // 8 - 4
        ahead = jnp.where(s == 0, EXTRA + HALO + v, EXTRA + 8 * v + s - 1)
        ahead = ((c == ahead) & (r >= 8)).astype(bf16)
        j = r // 8
        behind = jnp.where(s == 7, EXTRA + j, 8 * j + s + 1)
        behind = ((c == behind) & (r < 24)).astype(bf16)
        ext_ref[:EXTRA] = mm(ahead, rim_ref[0]).astype(bf16)
        ext_ref[EXTRA + 2 * rows :] = mm(behind, rim_ref[1]).astype(bf16)
        bcin_ref[...] = mm(ext_ref[...], bcw_ref[...]).astype(bf16).astype(f32)

    def bc_piece(d, first):
        at = slice(d * rows + first, d * rows + first + CHUNK)
        bc_ref[at] = conv_rows(bcin_ref, bck_ref[...], d, rows, first, CHUNK)

    def x_piece(d, first):
        at = slice(d * rows + first, d * rows + first + CHUNK)
        conv = conv_rows(xin_ref, xk_ref[...], d, rows, first, CHUNK)
        xconv_ref[at] = conv
        weighted_ref[at] = (conv.astype(f32) * reach_ref[at]).astype(bf16)

    def states(d):
        part = mm(bt_ref[d], weighted_ref[d * rows : (d + 1) * rows]).astype(bf16)
        for g in range(TILE // LANES):
            group = d * steps * (TILE // LANES) + (n - 1) * (TILE // LANES) + g
            q, j = group // 5, group % 5
            at = pl.ds(pl.multiple_of(16 * j, 16), 16)
            for i in range(STATE // 16):
                pay_ref[4 * i + q, at] = part[16 * i : 16 * i + 16, g * LANES : (g + 1) * LANES]

    def product(k, weight):
        depth = width // DEPTHS
        at = slice(k * depth, (k + 1) * depth)
        part = mm(ext_ref[:, at], weight(at))
        if k == 0:
            acc_ref[...] = part
        elif k < DEPTHS - 1:
            acc_ref[...] += part
        else:
            xin_ref[...] = (acc_ref[...] + part).astype(bf16).astype(f32)

    def reach():
        reach_ref[...] = mm(wend_ref[...], spread((n - 1) * (TILE // HEAD_DIM), TILE))

    def fetch(tile):
        at = pl.multiple_of(tile * TILE, TILE)
        return pltpu.make_async_copy(
            xw_hbm.at[:, pl.ds(at + TILE, TILE)], xw_ref.at[:, pl.ds(at, TILE)], sems.at[tile]
        )

    pieces = [(d, first) for d in range(2) for first in range(0, rows, CHUNK)]
    share = [k * len(pieces) // (DEPTHS - 1) for k in range(DEPTHS)]

    def start(tile, _):
        fetch(tile).start()
        return 0

    @pl.when(n == 0)
    def _():
        lax.fori_loop(0, xw_ref.shape[1] // TILE, start, 0)
        prelude()
        weight = lambda at: first_ref[at]
        for k in range(DEPTHS - 1):
            product(k, weight)
            for piece in pieces[share[k] : share[k + 1]]:
                bc_piece(*piece)
        product(DEPTHS - 1, weight)
        for d in range(2):
            at = slice(d * rows, (d + 1) * rows)
            bt_ref[d] = jnp.transpose(bc_ref[at, :STATE].astype(f32)).astype(bf16)
        row = iota((8, LANES), 0)
        for d in range(2):
            dec = jnp.broadcast_to(dec_ref[d : d + 1], (8, LANES))
            hi = dec.astype(bf16).astype(f32)
            tail = jnp.where(row == 0, hi, jnp.where(row == 1, dec - hi, 0.0)).astype(bf16)
            for slot in range(pay_ref.shape[0]):
                if slot % 4 // 2 == d:
                    pay_ref[slot, 80:88] = tail

    @pl.when((n > 0) & (n < steps))
    def _():
        fetch(n - 1).wait()
        column = pl.multiple_of((n - 1) * TILE, TILE)
        weight = lambda at: xw_ref[at, pl.ds(column, TILE)]
        reach()
        for k in range(DEPTHS - 1):
            product(k, weight)
            for i in range(share[k], share[k + 1]):
                x_piece(*pieces[i])
                if (i + 1) % (len(pieces) // 2) == 0:
                    states(pieces[i][0])
        product(DEPTHS - 1, weight)

    @pl.when(n == steps)
    def _():
        reach()
        for piece in pieces:
            x_piece(*piece)
        for d in range(2):
            states(d)


def entry(x, prev_rows, next_rows, gain, first, bcw, xk, bck, wend, dec, xw, slots):
    width = x.shape[1]
    rows = x.shape[0] // 2
    inner = xw.shape[1]
    steps = inner // TILE
    behind = lambda n: jnp.maximum(n - 1, 0)
    whole = lambda *shape: pl.BlockSpec(shape, lambda n: (0,) * len(shape))
    once = lambda *shape: pl.BlockSpec(
        shape, lambda n: (0,) * len(shape), pipeline_mode=pl.Buffered(1)
    )
    vmem = pl.BlockSpec(memory_space=pltpu.VMEM)
    return pl.pallas_call(
        entry_kernel,
        grid=(steps + 1,),
        in_specs=[
            vmem, vmem, vmem, once(width // LANES, LANES),
            vmem, vmem,
            pl.BlockSpec((4, TILE), lambda n: (0, behind(n))),
            once(4, 2 * STATE), vmem, vmem, pl.BlockSpec(memory_space=pltpu.HBM),
        ],
        out_specs=[
            pl.BlockSpec((2 * rows, TILE), lambda n: (0, behind(n))),
            whole(2 * rows, 2 * STATE), whole(slots, 88, LANES),
        ],
        out_shape=[
            pltpu.HBM((2 * rows, inner), bf16),
            pltpu.HBM((2 * rows, 2 * STATE), bf16),
            pltpu.HBM((slots, 88, LANES), bf16),
        ],
        scratch_shapes=[
            pltpu.VMEM((2 * rows + 2 * EXTRA, width), bf16),
            pltpu.VMEM((2 * rows + 2 * EXTRA, TILE), f32),
            pltpu.VMEM((2 * rows + 2 * EXTRA, TILE), f32),
            pltpu.VMEM((2, STATE, rows), bf16),
            pltpu.VMEM((2, EXTRA + HALO, width), bf16),
            pltpu.VMEM((2 * rows, TILE), bf16),
            pltpu.VMEM((2 * rows + 2 * EXTRA, TILE), f32),
            pltpu.VMEM((2 * rows, TILE), f32),
            pltpu.VMEM((width, inner - TILE), bf16),
            pltpu.SemaphoreType.DMA((inner // TILE - 1,)),
        ],
        compiler_params=pltpu.CompilerParams(
            dimension_semantics=("arbitrary",), vmem_limit_bytes=26 << 20
        ),
        cost_estimate=pl.CostEstimate(
            flops=2 * 544 * width * (inner + 256), bytes_accessed=12 << 20, transcendentals=0
        ),
        name="entry",
    )(x, prev_rows, next_rows, off_chip(gain), first, bcw, off_chip(xk), off_chip(bck), wend, dec, off_chip(xw))


def open_gate_kernel(x_ref, zw_ref, z_ref):
    z = mm(x_ref[...], zw_ref[...]).astype(bf16).astype(f32)
    z_ref[...] = silu(z).astype(bf16)


def open_gate(x, zw):
    height, width = x.shape
    inner = zw.shape[1]
    return pl.pallas_call(
        open_gate_kernel,
        grid=(inner // TILE,),
        in_specs=[fixed(height, width), pl.BlockSpec((width, TILE), lambda n: (0, n))],
        out_specs=pl.BlockSpec((height, TILE), lambda n: (0, n)),
        out_shape=jax.ShapeDtypeStruct((height, inner), bf16),
        compiler_params=pltpu.CompilerParams(
            dimension_semantics=("arbitrary",), vmem_limit_bytes=16 << 20
        ),
        cost_estimate=pl.CostEstimate(
            flops=2 * height * width * inner, bytes_accessed=16 << 20, transcendentals=0
        ),
        name="open_gate",
    )(off_chip(x), off_chip(zw))


def within_kernel(x_ref, bc_ref, cum_ref, cumt_ref, delta_ref, y_ref, gram_ref, size_ref):
    d, n = pl.program_id(0), pl.program_id(1)
    rows = x_ref.shape[0]
    heads = TILE // HEAD_DIM

    @pl.when(n == 0)
    def _():
        gram = lax.dot_general(
            bc_ref[:, STATE:], bc_ref[:, :STATE], (((1,), (1,)), ((), ())), preferred_element_type=f32
        )
        t, s = time_of(iota((rows, rows), 0), rows), time_of(iota((rows, rows), 1), rows)
        seen = jnp.where(d == 0, t - s, s - t) >= 0
        gram_ref[...] = jnp.where(seen, gram, 0.0)
        size_ref[...] = hi_lo(delta_ref[...])

    weighted = x_ref[...].astype(f32) * mm(size_ref[...], spread(n * heads, TILE))
    cum = pltpu.roll(cum_ref[...], (LANES - n * heads) % LANES, 1)
    owner = iota((rows, TILE), 1) // HEAD_DIM
    total = jnp.zeros((rows, TILE), f32)
    for k in range(heads):
        behind = cumt_ref[0, pl.ds(n * heads + k, 1), :]
        decay = jnp.exp(jnp.minimum(cum[:, k : k + 1] - behind, 0.0)) * gram_ref[...]
        total = total + mm(decay.astype(bf16), jnp.where(owner == k, weighted, 0.0).astype(bf16))
    y_ref[...] = total.astype(bf16)


def within(xconv, bc, cum, cumt, delta):
    rows = xconv.shape[0] // 2
    inner = xconv.shape[1]
    return pl.pallas_call(
        within_kernel,
        grid=(2, inner // TILE),
        in_specs=[
            pl.BlockSpec((rows, TILE), lambda d, n: (d, n)),
            pl.BlockSpec((rows, 2 * STATE), lambda d, n: (d, 0)),
            pl.BlockSpec((rows, LANES), lambda d, n: (d, 0)),
            pl.BlockSpec((1, 24, rows), lambda d, n: (d, 0, 0)),
            pl.BlockSpec((rows, LANES), lambda d, n: (d, 0)),
        ],
        out_specs=pl.BlockSpec((rows, TILE), lambda d, n: (d, n)),
        out_shape=pltpu.HBM((2 * rows, inner), bf16),
        scratch_shapes=[pltpu.VMEM((rows, rows), f32), pltpu.VMEM((rows, 2 * LANES), bf16)],
        compiler_params=pltpu.CompilerParams(
            dimension_semantics=("arbitrary", "arbitrary"), vmem_limit_bytes=12 << 20
        ),
        cost_estimate=pl.CostEstimate(flops=3 << 30, bytes_accessed=5 << 20, transcendentals=3 << 20),
        name="within",
    )(off_chip(xconv), off_chip(bc), cum, cumt, delta)


def scan_kernel(q_ref, pay_ref, out_ref, carry_ref, dec_ref):
    q = q_ref[0]
    half, turned = q % 2, q // 2
    depth = out_ref.shape[0]
    step = pl.program_id(0)
    base = depth * jnp.where(turned == 1, pl.num_programs(0) - 1 - step, step)

    @pl.when(pl.program_id(0) == 0)
    def _():
        carry_ref[...] = jnp.zeros_like(carry_ref)

    first = half * (5 * LANES // HEAD_DIM)
    place = iota((LANES, 5 * LANES), 0) == first + iota((LANES, 5 * LANES), 1) // HEAD_DIM
    place = place.astype(bf16)
    tails = pay_ref[pl.ds(base, depth), 80:88].astype(f32).reshape(8 * depth, LANES).astype(bf16)
    dec_ref[...] = mm(tails, place)
    carry = [carry_ref[16 * j : 16 * j + 16] for j in range(5)]
    for i in range(depth):
        at = jnp.where(turned == 1, depth - 1 - i, i)
        decays = dec_ref[pl.ds(pl.multiple_of(8 * at, 8), 8)]
        decay = decays[0:1] + decays[1:2]
        for j in range(5):
            rows = slice(16 * j, 16 * j + 16)
            out_ref[at, rows] = carry[j].astype(bf16)
            carry[j] = carry[j] * decay[:, j * LANES : (j + 1) * LANES] + pay_ref[base + at, rows].astype(f32)
    for j in range(5):
        carry_ref[16 * j : 16 * j + 16] = carry[j]


def scan(q, pay):
    slots = pay.shape[0]
    depth = 8
    steps = slots // depth
    chunk = lambda i, q: (jnp.where(q[0] // 2 == 1, steps - 1 - i, i), 0, 0)
    return pl.pallas_call(
        scan_kernel,
        grid_spec=pltpu.PrefetchScalarGridSpec(
            num_scalar_prefetch=1,
            grid=(steps,),
            in_specs=[pl.BlockSpec(memory_space=pltpu.VMEM)],
            out_specs=pl.BlockSpec((depth, 80, LANES), chunk),
            scratch_shapes=[pltpu.VMEM((80, LANES), f32), pltpu.VMEM((8 * depth, 5 * LANES), f32)],
        ),
        out_shape=jax.ShapeDtypeStruct((slots, 80, LANES), bf16),
        compiler_params=pltpu.CompilerParams(
            dimension_semantics=("arbitrary",), vmem_limit_bytes=6 << 20
        ),
        name="scan",
    )(q, pay)


def weight_fetches(q, w_ref, near_ref, far_ref, sems):
    lanes = near_ref.shape[1]
    near = pl.ds(pl.multiple_of(q * lanes, LANES), lanes)
    far = pl.ds(pl.multiple_of((3 - q) * lanes, LANES), lanes)
    near_copies, far_copies = [], []
    for k in range(near_ref.shape[0] // TILE):
        rows = slice(k * TILE, (k + 1) * TILE)
        near_copies.append(pltpu.make_async_copy(w_ref.at[rows, near], near_ref.at[rows], sems.at[0, k]))
        far_copies.append(pltpu.make_async_copy(w_ref.at[rows, far], far_ref.at[rows], sems.at[1, k]))
    return near_copies, far_copies


def project_into(out_ref, g_ref, copies, near_ref, far_ref, adds):
    inner, lanes = near_ref.shape
    for copy in copies[1]:
        copy.wait()
    behind = mm(g_ref[:, inner:], far_ref[...]).astype(bf16)
    for copy in copies[0]:
        copy.wait()
    ahead = mm(g_ref[:, :inner], near_ref[...])
    flip = flip_matrix(LANES)
    blocks = lanes // LANES
    for b in range(blocks):
        at = slice(b * LANES, (b + 1) * LANES)
        source = slice((blocks - 1 - b) * LANES, (blocks - b) * LANES)
        total = ahead[:, at] + mm(behind[:, source], flip)
        for add in adds:
            total = total + add[:, at].astype(f32)
        out_ref[:, at] = total.astype(out_ref.dtype)


def weight_scratch(inner, lanes):
    return [
        pltpu.VMEM((inner, lanes), bf16),
        pltpu.VMEM((inner, lanes), bf16),
        pltpu.SemaphoreType.DMA((2, inner // TILE)),
    ]


def gate_kernel(
    target_ref, y_ref, z_ref, bc_ref, cum_ref, st_ref, gain_ref, w_ref,
    g_ref, out_ref,
    kept_ref, acc_ref, held_ref, reach_ref, sems,
):
    n = pl.program_id(0)
    rows, lanes = y_ref.shape
    columns = out_ref.shape[1]
    groups = lanes // LANES
    target = target_ref[0]

    def fetch(p):
        quarter = jnp.where(p < 2, target, 3 - target)
        source = pl.ds(pl.multiple_of((p % 2) * lanes, LANES), lanes)
        cols = pl.ds(pl.multiple_of(quarter * columns, LANES), columns)
        to = pl.ds(pl.multiple_of(p * lanes, LANES), lanes)
        return pltpu.make_async_copy(w_ref.at[source, cols], kept_ref.at[to], sems.at[p])

    def start(p, _):
        fetch(p).start()
        return 0

    @pl.when(n == 0)
    def _():
        lax.fori_loop(0, 4, start, 0)

    order = (iota((rows, rows), 0) == time_of(iota((rows, rows), 1), rows)).astype(bf16)
    same = (iota((LANES, LANES), 0) // HEAD_DIM == iota((LANES, LANES), 1) // HEAD_DIM).astype(bf16)

    def gate_group(q, b, carried, reach):
        at = slice(b * LANES, (b + 1) * LANES)
        y = y_ref[:, at].astype(f32) + carried[:, at] * reach[:, at]
        part = y * z_ref[:, at].astype(f32)
        mean_sq = mm((part * part).astype(bf16), same) * (1.0 / HEAD_DIM)
        row = (q % 2) * groups + b
        scaled_part = part * lax.rsqrt(mean_sq + epsilon) * gain_ref[row : row + 1]
        held_ref[:, at] = scaled_part.astype(bf16)

    def settle(q):
        g_ref[:, q * lanes : (q + 1) * lanes] = mm(order, held_ref[...]).astype(bf16)

    def partial(p, first, last):
        at = slice(p * lanes, (p + 1) * lanes)
        part = mm(g_ref[:, at], kept_ref[at, first:last])
        if p % 2:
            acc_ref[p // 2, :, first:last] += part
        else:
            acc_ref[p // 2, :, first:last] = part

    pieces = {0: (0, TILE), 2: (TILE, 2 * TILE), 3: (2 * TILE, columns)}

    def step(k):
        if k < 4 and k % 2 == 0:
            reach_ref[...] = hi_lo(jnp.exp(cum_ref[...]))
        if k > 0:
            fetch(k - 1).wait()
        if k < 4:
            state = [st_ref[:, 0, j].reshape(STATE, LANES) for j in range(groups)]
            carried = mm(bc_ref[:, STATE:], jnp.concatenate(state, axis=1))
            reach = mm(reach_ref[...], spread((k % 2) * (lanes // HEAD_DIM), lanes))
        for b in range(groups):
            if k < 4:
                gate_group(k, b, carried, reach)
            if k > 0 and b in pieces:
                partial(k - 1, *pieces[b])
        if k < 4:
            settle(k)
            return
        flip = flip_matrix(LANES)
        blocks = columns // LANES
        for b in range(blocks):
            at = slice(b * LANES, (b + 1) * LANES)
            source = slice((blocks - 1 - b) * LANES, (blocks - b) * LANES)
            turned = mm(acc_ref[1, :, source].astype(bf16), flip)
            out_ref[:, at] = (acc_ref[0, :, at] + turned).astype(bf16)

    for k in range(5):
        pl.when(n == k)(functools.partial(step, k))


def gate(target, y, z, bc, cum, state, gain, weight):
    rows = y.shape[0] // 2
    inner = y.shape[1]
    lanes = inner // 2
    groups = lanes // LANES
    columns = weight.shape[1] // 4
    part = lambda n: jnp.minimum(n, 3)
    return pl.pallas_call(
        gate_kernel,
        grid_spec=pltpu.PrefetchScalarGridSpec(
            num_scalar_prefetch=1,
            grid=(5,),
            in_specs=[
                pl.BlockSpec((rows, lanes), lambda n, t: (part(n) // 2, part(n) % 2)),
                pl.BlockSpec((rows, lanes), lambda n, t: (part(n) // 2, part(n) % 2)),
                pl.BlockSpec((rows, 2 * STATE), lambda n, t: (part(n) // 2, 0)),
                pl.BlockSpec((rows, LANES), lambda n, t: (part(n) // 2, 0)),
                pl.BlockSpec((8, 1, groups, 16, LANES), lambda n, t: (0, part(n), 0, 0, 0)),
                fixed(2 * groups, LANES),
                pl.BlockSpec(memory_space=pltpu.HBM),
            ],
            out_specs=[fixed(rows, 2 * inner), fixed(rows, columns)],
            scratch_shapes=[
                pltpu.VMEM((2 * inner, columns), bf16),
                pltpu.VMEM((2, rows, columns), f32),
                pltpu.VMEM((rows, lanes), bf16),
                pltpu.VMEM((rows, 2 * LANES), bf16),
                pltpu.SemaphoreType.DMA((4,)),
            ],
        ),
        out_shape=[
            jax.ShapeDtypeStruct((rows, 2 * inner), bf16),
            jax.ShapeDtypeStruct((rows, columns), bf16),
        ],
        compiler_params=pltpu.CompilerParams(
            dimension_semantics=("arbitrary",), vmem_limit_bytes=20 << 20
        ),
        name="gate",
    )(target, off_chip(y), z, off_chip(bc), cum, state.reshape(8, 4, groups, 16, LANES), off_chip(gain), off_chip(weight))


def project_kernel(has_add, q_ref, g_ref, w_ref, *rest):
    adds, (out_ref, near_ref, far_ref, sems) = rest[:has_add], rest[has_add:]
    copies = weight_fetches(q_ref[0], w_ref, near_ref, far_ref, sems)
    for copy in copies[1] + copies[0]:
        copy.start()
    project_into(out_ref, g_ref, copies, near_ref, far_ref, adds)


def project(q, gated, weight, dtype, *adds):
    rows = gated.shape[0]
    inner, width = weight.shape
    lanes = width // 4
    vmem = pl.BlockSpec(memory_space=pltpu.VMEM)
    return pl.pallas_call(
        functools.partial(project_kernel, len(adds)),
        in_specs=[pl.BlockSpec(memory_space=pltpu.SMEM), vmem, pl.BlockSpec(memory_space=pltpu.HBM)]
        + [vmem for _ in adds],
        out_specs=vmem,
        out_shape=jax.ShapeDtypeStruct((rows, lanes), dtype),
        scratch_shapes=weight_scratch(inner, lanes),
        compiler_params=pltpu.CompilerParams(vmem_limit_bytes=16 << 20),
        cost_estimate=pl.CostEstimate(
            flops=4 * rows * inner * lanes, bytes_accessed=5 << 20, transcendentals=0
        ),
        name="project",
    )(q, gated, off_chip(weight), *adds)


def per_device(
    hidden, norm_gain, x_weight, z_weight, bc_weight, dt_weight, x_kernel, bc_kernel,
    dt_bias, log_rate, out_gain, out_weight,
):
    blocks = lax.axis_size("ctx")
    place = lax.axis_index("ctx")
    head = lax.axis_index("head")
    prev_rows = lax.ppermute(hidden[-HALO:], "ctx", [(i, i + 1) for i in range(blocks - 1)])
    next_rows = lax.ppermute(hidden[:HALO], "ctx", [(i + 1, i) for i in range(blocks - 1)])
    gain = norm_gain.reshape(-1, LANES)
    normed, delta, cum, cumt, wend, dec, x_kept, bc_kept = norm(
        hidden, gain, dt_weight.T, dt_bias[None], log_rate[None], x_weight, bc_weight
    )
    xconv, bc, pay = entry(
        normed, prev_rows, next_rows, gain, x_kept, bc_kept, x_kernel, bc_kernel, wend, dec,
        x_weight, blocks,
    )
    pay = lax.all_to_all(pay, "ctx", 0, 0, tiled=True)
    open_z = open_gate(normed, z_weight)
    pay, open_z = lax.optimization_barrier((pay, open_z))
    state = scan((place % 4)[None], pay)
    state, xconv = lax.optimization_barrier((state, xconv))
    state = lax.all_to_all(state, "ctx", 0, 0, tiled=True)
    y = within(xconv, bc, cum, cumt, delta)
    core, far = head % 2, head // 2
    quarter = lambda f, c: (2 * f + c)[None]
    core_swap = [(0, 1), (1, 0), (2, 3), (3, 2)]
    far_swap = [(0, 2), (2, 0), (1, 3), (3, 1)]
    gated, first = gate(
        quarter(1 - far, 1 - core), y, open_z, bc, cum, state, out_gain.reshape(-1, LANES), out_weight
    )
    first = lax.ppermute(first, "head", core_swap)
    second = project(quarter(1 - far, core), gated, out_weight, f32)
    second = (second + first.astype(f32)).astype(bf16)
    second, gated = lax.optimization_barrier((second, gated))
    second = lax.ppermute(second, "head", far_swap)
    third = project(quarter(far, 1 - core), gated, out_weight, bf16)
    third = lax.ppermute(third, "head", core_swap)
    lanes = hidden.shape[1] // 4
    residual = lax.dynamic_slice_in_dim(hidden, head * lanes, lanes, 1)
    own = project(quarter(far, core), gated, out_weight, f32, third, residual)
    return (own + second.astype(f32)).astype(bf16)


def solution(mesh):
    return jax.shard_map(
        per_device,
        mesh=mesh,
        in_specs=(
            P("ctx", None), P(), P(None, "head"), P(None, "head"), P(), P(None, "head"),
            P(None, "head"), P(), P("head"), P("head"), P("head"), P("head", None),
        ),
        out_specs=P("ctx", "head"),
        check_vma=False,
    )
```
